256 devices in a mesh: ctx: 8 (over z_hi, y), tp: 32 (over x, z_lo, core).
Axes of the slice: x: 4, y: 4, z: 8 (z_hi: 2, z_lo: 4; z = z_hi * 4 + z_lo), core: 2. Of those that a mesh axis runs over, the one named last changes fastest.
Arguments:
- tokens: bfloat16 [4096, 4096], P(('ctx', 'tp')), may hold values from -6 to 6
- gate_weight: bfloat16 [4096, 16384], P(None, 'tp'), may hold values from -0.09375 to 0.09375
- input_weight: bfloat16 [4096, 16384], P(None, 'tp'), may hold values from -0.09375 to 0.09375
- state_weight: bfloat16 [4096, 2048], P(None, 'tp'), may hold values from -0.09375 to 0.09375
- step_weight: bfloat16 [4096, 256], P(None, 'tp'), may hold values from -0.09375 to 0.09375
- input_conv: float32 [5, 16384], P(None, 'tp'), may hold values from -0.5 to 0.5
- state_conv: float32 [5, 2048], P(None, 'tp'), may hold values from -0.5 to 0.5
- log_rate: float32 [256], P('tp'), may hold values from -12 to 2.1
- step_bias: float32 [256], P('tp'), may hold values from -6 to -2
- skip_gain: float32 [256], P('tp'), may hold values from 0.5 to 2
- norm_gain: float32 [16384], P('tp'), may hold values from 0.25 to 1.75
- out_weight: bfloat16 [16384, 4096], P('tp'), may hold values from -0.046875 to 0.046875
Outputs:
- mixed_out: bfloat16 [4096, 4096], P(('ctx', 'tp'))
The draws below stay inside these ranges and needn't reach their ends.
All inputs are finite; a program needn't handle non-finite values.
Results may differ from the reference program's by a relative error of at most 0.0035.
The reference program's roundings to bfloat16 on the way (of `gate_rows`, `input_rows`, `state_rows`, `conv_inputs`, `conv_states` and `normed`) count: a program that leaves them out, or rounds other values in their place, can miss the bound.
Values may be sent and summed in bfloat16 or wider, within the bound.
No kernel may reach another device: no remote copies, remote signals or barrier semaphores. Data moves between devices by JAX's collectives and lax.ppermute only.
A program may use at most 128 MiB of HBM per device.

```python
import math
import jax
import jax.numpy as jnp
from jax import lax

D = 4096
HEADS = 256
PDIM = 64
NSTATE = 256
GROUPS = 4
CONV = 4
SPAN = 64
TOKENS = 4096
DINNER = 16384
BCW = 2048


def draw_log_rate(key, part):
    first_key, second_key, third_key = jax.random.split(key, 3)
    fast_share = 0.5
    is_fast = jax.random.uniform(first_key, (HEADS,), jnp.float32) < fast_share
    fast_rate = jnp.exp(jax.random.uniform(second_key, (HEADS,), jnp.float32, math.log(2.0), math.log(8.0)))
    slow_rate = jnp.exp(jax.random.uniform(third_key, (HEADS,), jnp.float32, math.log(0.3), math.log(1.5))) / (0.2 * TOKENS)
    return jnp.log(jnp.where(is_fast, fast_rate, slow_rate)).astype(jnp.float32)


def shard_levels(stream_key, shape, cuts, smallest, high):
    factor_of, own = 1.0, jax.random.fold_in(stream_key, 6)
    for dim, blocks in cuts:
        steps = jnp.exp(jax.random.uniform(jax.random.fold_in(own, dim), (blocks,), jnp.float32, smallest / len(cuts), high / len(cuts)))
        factor_of = factor_of * jnp.repeat(steps, shape[dim] // blocks).reshape([-1 if axis == dim else 1 for axis in range(len(shape))])
    return factor_of


def normal_values(key, dims, width, reach, cuts=(), held_as=jnp.bfloat16):
    entries = jax.random.normal(key, dims, jnp.float32) * width
    if len(cuts) > 0:
        entries = shard_levels(key, dims, cuts, -0.22, 0.18) * entries
    return jnp.clip(entries, min=-reach, max=reach).astype(held_as)


def setup_inputs(seed: int = 0) -> dict:
    splits = jax.random.split(jax.random.key(seed), 13)
    tokens = normal_values(splits[0], (TOKENS, D), 1.0, 6.0, ((0, 256),))
    gate_weight = normal_values(splits[1], (D, DINNER), D ** -0.5, 0.09375, ((1, 32),))
    input_weight = normal_values(splits[2], (D, DINNER), D ** -0.5, 0.09375, ((1, 32),))
    state_weight = normal_values(splits[3], (D, BCW), D ** -0.5, 0.09375, ((1, 32),))
    step_weight = normal_values(splits[4], (D, HEADS), D ** -0.5, 0.09375, ((1, 32),))
    input_conv = jnp.clip(jax.random.uniform(splits[5], (CONV + 1, DINNER), jnp.float32, -0.5, 0.5) * shard_levels(splits[5], (CONV + 1, DINNER), ((1, 32),), -0.4, 0.0), -0.5, 0.5)
    state_conv = jnp.clip(jax.random.uniform(splits[6], (CONV + 1, BCW), jnp.float32, -0.5, 0.5) * shard_levels(splits[6], (CONV + 1, BCW), ((1, 32),), -0.4, 0.0), -0.5, 0.5)
    log_rate = draw_log_rate(jax.random.fold_in(splits[12], 71), 0)
    step_bias = jnp.clip(-6.0 + 4.0 * jax.random.uniform(splits[8], (HEADS,), jnp.float32) ** shard_levels(splits[8], (HEADS,), ((0, 32),), -0.2, 0.2), -6.0, -2.0)
    skip_gain = jnp.clip(0.5 + 1.5 * jax.random.uniform(splits[9], (HEADS,), jnp.float32) ** shard_levels(splits[9], (HEADS,), ((0, 32),), -0.2, 0.2), 0.5, 2.0)
    norm_gain = jnp.clip(1.0 + 0.15 * jax.random.normal(splits[10], (DINNER,), jnp.float32), 0.25, 1.75)
    out_weight = normal_values(splits[11], (DINNER, D), DINNER ** -0.5, 0.046875, ((0, 32),))
    return {"tokens": tokens, "gate_weight": gate_weight, "input_weight": input_weight, "state_weight": state_weight, "step_weight": step_weight, "input_conv": input_conv, "state_conv": state_conv, "log_rate": log_rate, "step_bias": step_bias, "skip_gain": skip_gain, "norm_gain": norm_gain, "out_weight": out_weight}


def conv_silu(sequence, conv_taps):
    row_count = sequence.shape[0]
    padded = jnp.concatenate([jnp.zeros((CONV - 1, sequence.shape[1]), sequence.dtype), sequence], axis=0).astype(jnp.float32)
    running = conv_taps[CONV] + conv_taps[0] * padded[0:row_count]
    for offset in range(1, CONV):
        running = running + conv_taps[offset] * padded[offset:offset + row_count]
    return jax.nn.silu(running).astype(jnp.bfloat16)

def span_terms(inputs, step_size, log_damp, write_vec, read_vec):
    highest = lax.Precision.HIGHEST
    cumulative = jnp.cumsum(log_damp, axis=1)
    length = log_damp.shape[1]
    causal = (jnp.arange(length)[:, None] >= jnp.arange(length)[None, :])[None, :, :, None]
    scores = jnp.einsum('kin,kjn->kij', read_vec, write_vec, precision=highest)
    spread = cumulative[:, :, None, :] - cumulative[:, None, :, :]
    damping = jnp.exp(jnp.where(causal, spread, -jnp.inf))
    mixing = scores[:, :, :, None] * damping * step_size[:, None, :, :]
    within = jnp.einsum('kijh,kjhp->kihp', mixing, inputs, precision=highest)
    to_end = jnp.exp(cumulative[:, -1:, :] - cumulative) * step_size
    states = jnp.einsum('kjh,kjhp,kjn->khpn', to_end, inputs, write_vec, precision=highest)
    return (cumulative, within, states)

def span_pass(cumulative, states, read_vec, zero_state):

    def advance(carried, payload):
        factor, increment = payload
        return (factor[:, None, None] * carried + increment, carried)
    last_state, entering = lax.scan(advance, zero_state, (jnp.exp(cumulative[:, -1, :]), states))
    across = jnp.einsum('kih,kin,khpn->kihp', jnp.exp(cumulative), read_vec, entering, precision=lax.Precision.HIGHEST)
    return (last_state, across)

def reference(tokens, gate_weight, input_weight, state_weight, step_weight, input_conv, state_conv, log_rate, step_bias, skip_gain, norm_gain, out_weight):
    gate_rows = jnp.dot(tokens, gate_weight, preferred_element_type=jnp.float32).astype(jnp.bfloat16)
    input_rows = jnp.dot(tokens, input_weight, preferred_element_type=jnp.float32).astype(jnp.bfloat16)
    state_rows = jnp.dot(tokens, state_weight, preferred_element_type=jnp.float32).astype(jnp.bfloat16)
    step_raw = jnp.dot(tokens, step_weight, preferred_element_type=jnp.float32)
    conv_inputs = conv_silu(input_rows, input_conv)
    conv_states = conv_silu(state_rows, state_conv)
    step_size = jax.nn.softplus(step_raw + step_bias)
    log_damp = -step_size * jnp.exp(log_rate)
    per_group = HEADS // GROUPS
    blocks = TOKENS // SPAN
    inputs = conv_inputs.astype(jnp.float32).reshape(blocks, SPAN, GROUPS, per_group, PDIM).transpose(2, 0, 1, 3, 4)
    group_steps = step_size.reshape(blocks, SPAN, GROUPS, per_group).transpose(2, 0, 1, 3)
    group_damp = log_damp.reshape(blocks, SPAN, GROUPS, per_group).transpose(2, 0, 1, 3)
    vectors = conv_states.astype(jnp.float32).reshape(blocks, SPAN, GROUPS, 2, NSTATE).transpose(2, 3, 0, 1, 4)

    def one_group(payload):
        group_inputs, steps_here, damp_here, vectors_here = payload
        cumulative, within, states = span_terms(group_inputs, steps_here, damp_here, vectors_here[0], vectors_here[1])
        zero_state = jnp.zeros((per_group, PDIM, NSTATE), jnp.float32)
        last_state, across = span_pass(cumulative, states, vectors_here[1], zero_state)
        return within + across
    outputs = lax.map(one_group, (inputs, group_steps, group_damp, vectors))
    outputs = outputs.transpose(1, 2, 0, 3, 4).reshape(TOKENS, HEADS, PDIM)
    outputs = outputs + skip_gain[None, :, None] * conv_inputs.astype(jnp.float32).reshape(TOKENS, HEADS, PDIM)
    gate_out = outputs.reshape(TOKENS, DINNER) * jax.nn.silu(gate_rows.astype(jnp.float32))
    grouped = gate_out.reshape(TOKENS, GROUPS, DINNER // GROUPS)
    mean_square = lax.optimization_barrier(jnp.sum(grouped * grouped, axis=2)) / (DINNER // GROUPS)
    scaled = (grouped * lax.rsqrt(mean_square + 1e-05)[:, :, None]).reshape(TOKENS, DINNER)
    normed = (scaled * norm_gain).astype(jnp.bfloat16)
    return jnp.dot(normed, out_weight, preferred_element_type=jnp.float32).astype(jnp.bfloat16)
```

```python
import jax
import jax.numpy as jnp
from jax import lax
from jax.experimental import pallas as pl
from jax.experimental.pallas import tpu as pltpu
from jax.sharding import PartitionSpec as P


GROUPS = 4
CONV = 4
DINNER = 16384
F32 = jnp.float32
BF16 = jnp.bfloat16
F16 = jnp.float16
MIB = 1024 * 1024


VM = pl.BlockSpec(memory_space=pltpu.VMEM)
SM = pl.BlockSpec(memory_space=pltpu.SMEM)


def sds(shape, dtype):
    return jax.ShapeDtypeStruct(shape, dtype)


def cost(flops, nbytes):
    return pl.CostEstimate(flops=int(flops), bytes_accessed=int(nbytes), transcendentals=0)


def send(array, axis, to):
    size = lax.axis_size(axis)
    pairs = [(i, to(i)) for i in range(size) if to(i) is not None]
    return lax.ppermute(array, axis, pairs)


def flip(array, axis, mask):
    return send(array, axis, lambda i: i ^ mask)


def along_x(array, by):
    return send(array, "tp", lambda i: (i + 8 * by) % 32)


def dot(a, b):
    return lax.dot_general(a, b, (((1,), (0,)), ((), ())), preferred_element_type=F32)


def dot_nt(a, b):
    return lax.dot_general(a, b, (((1,), (1,)), ((), ())), preferred_element_type=F32)


def dot_tn(a, b):
    return lax.dot_general(a, b, (((0,), (0,)), ((), ())), preferred_element_type=F32)


def silu(v):
    return v * jax.nn.sigmoid(v)


def pair_scale(cols, pair):
    rows = cols.shape[0]
    lane = lax.broadcasted_iota(jnp.int32, (rows, 128), 1)
    low = jnp.broadcast_to(cols[:, 2 * pair : 2 * pair + 1], (rows, 128))
    high = jnp.broadcast_to(cols[:, 2 * pair + 1 : 2 * pair + 2], (rows, 128))
    return jnp.where(lane < 64, low, high)


def split(value):
    high = value.astype(BF16)
    return high, (value - high.astype(F32)).astype(BF16)


def project(parts, slots, idx, gate_w, input_w, small_w, bufs):
    depth = parts[0].shape[1]
    steps = 4
    kb = depth // steps
    count = len(slots)
    rows = 128 * count
    weights, wspecs, outs, accs = [], [], [], []
    if gate_w is not None:
        weights.append(gate_w)
        wspecs.append(pl.BlockSpec((kb, 512), lambda k, i: (k, 0)))
        outs.append(sds((512, 512), BF16))
        accs.append(pltpu.VMEM((rows, 512), F32))
    if input_w is not None:
        weights += [input_w, small_w]
        wspecs += [
            pl.BlockSpec((kb, 512), lambda k, i: (k, 0)),
            pl.BlockSpec((256, kb), lambda k, i: (0, k)),
        ]
        outs += [sds((512, 512), BF16), sds((512, 128), BF16), sds((8, 512), F32)]
        accs += [pltpu.VMEM((rows, 512), F32), pltpu.VMEM((rows, 256), F32)]
    nw, no, na = len(weights), len(outs), len(accs)
    aliased = [] if bufs is None else list(bufs)
    ready = [pltpu.VMEM((rows, 512), BF16)] if gate_w is not None else []
    if input_w is not None:
        ready += [pltpu.VMEM((rows, 512), BF16), pltpu.VMEM((rows, 128), BF16), pltpu.VMEM((8, rows), F32)]
        ready += [pltpu.VMEM((rows, 128), F32)]
    nl = len(parts)

    def kernel(i, *refs):
        lrefs, refs = refs[:nl], refs[nl:]
        wrefs, refs = refs[:nw], refs[nw + len(aliased) :]
        orefs, refs = refs[:no], refs[no:]
        arefs, refs = refs[:na], refs[na:]
        rrefs, sem = refs[:-1], refs[-1]
        k = pl.program_id(0)
        lhs = jnp.concatenate([r[...] for r in lrefs], axis=0)
        for n, w in enumerate(wrefs):
            nt = input_w is not None and n == nw - 1
            part = dot_nt(lhs, w[...]) if nt else dot(lhs, w[...])

            @pl.when(k == 0)
            def _():
                arefs[n][...] = part

            @pl.when(k > 0)
            def _():
                arefs[n][...] += part

        @pl.when(k == steps - 1)
        def _():
            copies = []
            for s in range(count):
                for t in range(8):
                    at = slice(s * 128 + t * 16, s * 128 + t * 16 + 16)
                    dst = pl.ds(pl.multiple_of(i[4 + t] * 16, 16) + s * 128, 16)
                    n = 0
                    if gate_w is not None:
                        rrefs[n][dst, :] = arefs[n][at, :].astype(BF16)
                        n += 1
                    if input_w is not None:
                        rrefs[n][dst, :] = arefs[n][at, :].astype(BF16)
                        rrefs[n + 1][dst, :] = arefs[n + 1][at, 0:128].astype(BF16)
                        rrefs[n + 3][dst, :] = arefs[n + 1][at, 128:256]
                here = slice(s * 128, s * 128 + 128)
                if input_w is not None:
                    rrefs[n + 2][:, here] = jnp.transpose(rrefs[n + 3][here, :])[0:8, :]
                there = pl.ds(pl.multiple_of(i[slots[s]] * 128, 128), 128)
                for n in range(no):
                    if n == no - 1 and input_w is not None:
                        source, target = rrefs[n].at[:, here], orefs[n].at[:, there]
                    else:
                        source, target = rrefs[n].at[here, :], orefs[n].at[there, :]
                    copies.append(pltpu.make_async_copy(source, target, sem.at[len(copies)]))
            for copy in copies:
                copy.start()
            for copy in copies:
                copy.wait()

    cols = (512 if gate_w is not None else 0) + (768 if input_w is not None else 0)
    first = 1 + nl + nw
    lspecs = [pl.BlockSpec((p.shape[0], kb), lambda k, i: (0, k)) for p in parts]
    out = pl.pallas_call(
        kernel,
        out_shape=outs,
        grid_spec=pltpu.PrefetchScalarGridSpec(
            num_scalar_prefetch=1,
            grid=(steps,),
            in_specs=lspecs + wspecs + [pl.BlockSpec(memory_space=pl.ANY)] * len(aliased),
            out_specs=[pl.BlockSpec(memory_space=pl.ANY)] * no,
            scratch_shapes=accs + ready + [pltpu.SemaphoreType.DMA((no * count,))],
        ),
        input_output_aliases={first + n: n for n in range(len(aliased))},
        compiler_params=pltpu.CompilerParams(vmem_limit_bytes=14 * MIB),
        cost_estimate=cost(2 * rows * depth * cols, 2 * depth * cols),
    )(idx, *parts, *weights, *aliased)
    return list(out)


def conv_rows(window, taps, rows):
    running = taps[CONV : CONV + 1, :] + taps[0:1, :] * window[13 : 13 + rows, :]
    for k in range(1, CONV):
        running = running + taps[k : k + 1, :] * window[13 + k : 13 + k + rows, :]
    return silu(running)


def conv_states_kernel(idx, rows_ref, halo_ref, taps_ref, out_ref, full):
    taps = taps_ref[...]
    for k in range(4):
        if k == 0:
            window = jnp.concatenate([halo_ref[:, 512:640], rows_ref[0:128, :]], axis=0).astype(F32)
        else:
            window = rows_ref[128 * k - 16 : 128 * k + 128, :].astype(F32)
        full[128 * k : 128 * k + 128, :] = conv_rows(window, taps, 128).astype(BF16)
    half = idx[13]
    out_ref[...] = full[pl.ds(pl.multiple_of(half * 256, 256), 256), :]


def conv_states(idx, rows, halo, taps):
    return pl.pallas_call(
        conv_states_kernel,
        out_shape=sds((256, 128), BF16),
        in_specs=[SM, VM, VM, VM],
        out_specs=VM,
        scratch_shapes=[pltpu.VMEM((512, 128), BF16)],
        compiler_params=pltpu.CompilerParams(vmem_limit_bytes=14 * MIB),
        cost_estimate=cost(2e6, 4e5),
        name="conv_states",
    )(idx, rows, halo, taps)


def columns_of(rows8):
    return jnp.transpose(rows8)


def column(par, start):
    row = lax.broadcasted_iota(jnp.int32, (8, 128), 0)
    out = jnp.zeros((8, 128), F32)
    for h in range(8):
        out = jnp.where(row == h, par[start + h], out)
    return out


def inputs_kernel(par_ref, rows_ref, halo_ref, taps_ref, step_ref, x_ref, hi_ref, lo_ref, dt_ref, cum_ref):
    taps = taps_ref[...]
    rate = jnp.exp(column(par_ref, 0))
    bias = column(par_ref, 8)
    lane = lax.broadcasted_iota(jnp.int32, (8, 128), 1)
    dts, cums = [], []
    for k in range(4):
        raw = step_ref[:, 128 * k : 128 * k + 128] + bias
        dt = jnp.maximum(raw, 0.0) + jnp.log1p(jnp.exp(-jnp.abs(raw)))
        cum = -dt * rate
        for b in range(7):
            moved = pltpu.roll(cum, 1 << b, 1)
            cum = cum + jnp.where(lane >= (1 << b), moved, 0.0)
        dts.append(dt)
        cums.append(cum)
        dt_ref[:, 128 * k : 128 * k + 128] = dt
        cum_ref[:, 128 * k : 128 * k + 128] = cum
    after = jnp.zeros((8, 1), F32)
    for k in reversed(range(4)):
        total = cums[k][:, 127:128]
        weight = jnp.exp(total - cums[k] + after) * dts[k]
        after = after + total
        cols = columns_of(weight)
        if k == 0:
            window = jnp.concatenate([halo_ref[:, 0:512], rows_ref[0:128, :]], axis=0)
        else:
            window = rows_ref[128 * k - 16 : 128 * k + 128, :]
        for p in range(4):
            ch = slice(128 * p, 128 * p + 128)
            x = conv_rows(window[:, ch].astype(F32), taps[:, ch], 128).astype(BF16)
            here = slice(128 * k, 128 * k + 128)
            x_ref[here, ch] = x
            hi, lo = split(x.astype(F32) * pair_scale(cols, p))
            hi_ref[here, ch] = hi
            lo_ref[here, ch] = lo


def inputs_stage(rows, halo, taps, step, par):
    return pl.pallas_call(
        inputs_kernel,
        out_shape=[sds((512, 512), BF16)] * 3 + [sds((8, 512), F32)] * 2,
        in_specs=[SM] + [VM] * 4,
        out_specs=[VM] * 5,
        compiler_params=pltpu.CompilerParams(vmem_limit_bytes=14 * MIB),
        cost_estimate=cost(1e7, 2e6),
        name="inputs_stage",
    )(par, rows, halo, taps, step)


def gathered_block(idx, own_ref, oth_ref, block, rows):
    place = lax.bitwise_xor(jnp.int32(block), idx[12])
    return jnp.where(idx[13] == rows, own_ref[place], oth_ref[place])


LOG2 = 0.6931471805599453


def scaled(value):
    most = jnp.max(jnp.abs(value), axis=0, keepdims=True)
    power = jnp.ceil(jnp.log(most) * (1.0 / LOG2))
    power = jnp.minimum(jnp.maximum(power, -100.0), 120.0)
    return value * jnp.exp(power * -LOG2), power


def unscaled(ref_value):
    return ref_value[0:256, :] * jnp.exp(ref_value[256:257, :] * LOG2)


def state_kernel(idx, own_ref, oth_ref, hi_ref, lo_ref, cum_ref, out_ref):
    halves = []
    for n in range(2):
        write = jnp.concatenate(
            [gathered_block(idx, own_ref, oth_ref, n, 0), gathered_block(idx, own_ref, oth_ref, n, 1)], axis=0
        )
        halves.append(write)
    write = jnp.concatenate(halves, axis=1)
    state = dot_tn(write, hi_ref[...]) + dot_tn(write, lo_ref[...])
    total = (
        cum_ref[:, 127:128] + cum_ref[:, 255:256] + cum_ref[:, 383:384] + cum_ref[:, 511:512]
    )
    damp = jnp.maximum(total, -110.0) * 256.0
    lane = lax.broadcasted_iota(jnp.int32, (16, 128), 1)
    row = lax.broadcasted_iota(jnp.int32, (16, 128), 0)
    for q in range(4):
        place = lax.bitwise_xor(jnp.int32(q), idx[14])
        mant, power = scaled(state[:, 128 * q : 128 * q + 128])
        out_ref[place, 0:256, :] = mant
        low = jnp.broadcast_to(damp[2 * q : 2 * q + 1, :], (16, 128))
        high = jnp.broadcast_to(damp[2 * q + 1 : 2 * q + 2, :], (16, 128))
        value = jnp.where(lane < 64, low, high)
        one = value.astype(BF16).astype(F32)
        two = (value - one).astype(BF16).astype(F32)
        three = value - one - two
        packed = jnp.where(row == 1, one, jnp.where(row == 2, two, jnp.where(row == 3, three, 0.0)))
        out_ref[place, 256:272, :] = jnp.where(row == 0, power, packed)


def state_stage(idx, own, oth, hi, lo, cum):
    return pl.pallas_call(
        state_kernel,
        out_shape=sds((4, 272, 128), F32),
        in_specs=[SM] + [VM] * 5,
        out_specs=VM,
        compiler_params=pltpu.CompilerParams(vmem_limit_bytes=14 * MIB),
        cost_estimate=cost(2.7e8, 2e6),
        name="state_stage",
    )(idx, own, oth, hi, lo, cum)


def prefix_kernel(idx, s0, s1, s2, s3, inc_ref, pre_ref, tot_ref):
    place = idx[14]
    odd = lax.bitwise_and(place, 1) == 1
    far = lax.bitwise_and(place, 2) == 2
    slots = [s0[...], s1[...], s2[...], s3[...]]
    a, b = jnp.where(odd, slots[1], slots[0]), jnp.where(odd, slots[0], slots[1])
    c, d = jnp.where(odd, slots[3], slots[2]), jnp.where(odd, slots[2], slots[3])
    ordered = [jnp.where(far, c, a), jnp.where(far, d, b), jnp.where(far, a, c), jnp.where(far, b, d)]
    running = jnp.zeros((256, 128), F32)
    carried = jnp.ones((1, 128), F32)
    for k in range(4):
        inc_ref[k] = running
        pre_ref[k] = jnp.broadcast_to(carried, (8, 128))
        tail = ordered[k][256:272, :]
        damp = jnp.exp((tail[1:2, :] + tail[2:3, :] + tail[3:4, :]) * (1.0 / 256.0))
        running = damp * running + unscaled(ordered[k])
        carried = carried * damp
    mant, power = scaled(running)
    tot_ref[0:256, :] = mant
    tot_ref[256:272, :] = jnp.broadcast_to(power, (16, 128))


def prefix_stage(idx, s0, s1, s2, s3):
    return pl.pallas_call(
        prefix_kernel,
        out_shape=[sds((4, 256, 128), F32), sds((4, 8, 128), F32), sds((272, 128), F32)],
        in_specs=[SM] + [VM] * 4,
        out_specs=[VM] * 3,
        compiler_params=pltpu.CompilerParams(vmem_limit_bytes=14 * MIB),
        cost_estimate=cost(1e6, 1e6),
        name="prefix_stage",
    )(idx, s0, s1, s2, s3)


def spread_kernel(idx, inc_ref, pre_ref, far_ref, out_ref):
    far = unscaled(far_ref[...])
    for k in range(4):
        place = lax.bitwise_xor(jnp.int32(k), idx[14])
        mant, power = scaled(inc_ref[k] + pre_ref[k][0:1, :] * far)
        out_ref[place, 0:256, :] = mant
        out_ref[place, 256:272, :] = jnp.broadcast_to(power, (16, 128))


def spread_stage(idx, inc, pre, far):
    return pl.pallas_call(
        spread_kernel,
        out_shape=sds((4, 272, 128), F32),
        in_specs=[SM] + [VM] * 3,
        out_specs=VM,
        compiler_params=pltpu.CompilerParams(vmem_limit_bytes=14 * MIB),
        cost_estimate=cost(1e6, 1e6),
        name="spread_stage",
    )(idx, inc, pre, far)


def scan_kernel(idx, par_ref, own_ref, oth_ref, x_ref, dt_ref, cum_ref, y_ref, read_ref, state):
    row = lax.broadcasted_iota(jnp.int32, (128, 128), 0)
    col = lax.broadcasted_iota(jnp.int32, (128, 128), 1)
    causal = row >= col
    left = col < 64
    zero = jnp.zeros((128, 128), BF16)
    for k in range(4):
        here = slice(128 * k, 128 * k + 128)
        half, sub = k // 2, slice(128 * (k % 2), 128 * (k % 2) + 128)

        def part(block):
            place = lax.bitwise_xor(jnp.int32(block), idx[12])
            return jnp.where(idx[13] == half, own_ref[place, sub, :], oth_ref[place, sub, :])

        write = jnp.concatenate([part(0), part(1)], axis=1)
        read = jnp.concatenate([part(2), part(3)], axis=1)
        read_ref[here, :] = read
        scores = dot_nt(read, write)
        cum = cum_ref[:, here]
        dt = dt_ref[:, here]
        cols = columns_of(cum)
        exp_cols = columns_of(jnp.exp(cum))
        total = cum[:, 127:128]
        end_cols = columns_of(jnp.exp(total - cum) * dt)
        damp = jnp.exp(total)
        for p in range(4):
            ch = slice(128 * p, 128 * p + 128)
            x = x_ref[here, ch]
            xf = x.astype(F32)
            mixes = []
            for h in (2 * p, 2 * p + 1):
                gap = jnp.broadcast_to(cols[:, h : h + 1], (128, 128)) - cum[h : h + 1, :]
                damping = jnp.exp(jnp.where(causal, gap, -jnp.inf))
                mixes.append(scores * damping * dt[h : h + 1, :])
            mix = jnp.concatenate(mixes, axis=1)
            both = jnp.concatenate([jnp.where(left, x, zero), jnp.where(left, zero, x)], axis=0)
            mix_hi, mix_lo = split(mix)
            y = dot(mix_hi, both) + dot(mix_lo, both)
            skip = jnp.where(left[0:1, :], par_ref[16 + 2 * p], par_ref[17 + 2 * p])
            y = y + skip * xf
            if k > 0:
                s_hi, s_lo = split(state[:, ch])
                y = y + pair_scale(exp_cols, p) * (dot(read, s_hi) + dot(read, s_lo))
            y_ref[here, ch] = y
            if k < 3:
                in_hi, in_lo = split(xf * pair_scale(end_cols, p))
                fresh = dot_tn(write, in_hi) + dot_tn(write, in_lo)
                if k == 0:
                    state[:, ch] = fresh
                else:
                    keep = jnp.where(
                        left[0:1, :],
                        jnp.broadcast_to(damp[2 * p : 2 * p + 1, :], (1, 128)),
                        jnp.broadcast_to(damp[2 * p + 1 : 2 * p + 2, :], (1, 128)),
                    )
                    state[:, ch] = keep * state[:, ch] + fresh


def scan_stage(idx, own, oth, x, dt, cum, par):
    return pl.pallas_call(
        scan_kernel,
        out_shape=[sds((512, 512), F32), sds((512, 256), BF16)],
        in_specs=[SM] * 2 + [VM] * 5,
        out_specs=[VM] * 2,
        scratch_shapes=[pltpu.VMEM((256, 512), F32)],
        compiler_params=pltpu.CompilerParams(vmem_limit_bytes=14 * MIB),
        cost_estimate=cost(6e9, 3e6),
        name="scan_stage",
    )(idx, par, own, oth, x, dt, cum)


def gate_kernel(idx, y_ref, read_ref, q0, q1, q2, q3, cum_ref, gate_ref, u_ref, ss_ref):
    place = idx[14]
    odd = lax.bitwise_and(place, 1) == 1
    far = lax.bitwise_and(place, 2) == 2
    slots = [q0[...], q1[...], q2[...], q3[...]]
    a, b = jnp.where(odd, slots[1], slots[0]), jnp.where(odd, slots[0], slots[1])
    c, d = jnp.where(odd, slots[3], slots[2]), jnp.where(odd, slots[2], slots[3])
    ordered = [jnp.where(far, c, a), jnp.where(far, d, b), jnp.where(far, a, c), jnp.where(far, b, d)]
    halves = [split(unscaled(v)) for v in ordered]
    before = jnp.zeros((8, 1), F32)
    for k in range(4):
        here = slice(128 * k, 128 * k + 128)
        cum = cum_ref[:, here]
        cols = columns_of(jnp.exp(cum + before))
        before = before + cum[:, 127:128]
        read = read_ref[here, :]
        squares = jnp.zeros((128, 128), F32)
        for p in range(4):
            ch = slice(128 * p, 128 * p + 128)
            y = y_ref[here, ch] + pair_scale(cols, p) * (dot(read, halves[p][0]) + dot(read, halves[p][1]))
            u = y * silu(gate_ref[here, ch].astype(F32))
            u_ref[here, ch] = u
            squares = squares + u * u
        ss_ref[k : k + 1, :] = jnp.sum(jnp.transpose(squares), axis=0, keepdims=True)


def gate_stage(idx, y, read, quarters, cum, gate):
    return pl.pallas_call(
        gate_kernel,
        out_shape=[sds((512, 512), F32), sds((4, 128), F32)],
        in_specs=[SM] + [VM] * 8,
        out_specs=[VM] * 2,
        compiler_params=pltpu.CompilerParams(vmem_limit_bytes=14 * MIB),
        cost_estimate=cost(2e8, 3e6),
        name="gate_stage",
    )(idx, y, read, *quarters, cum, gate)


def out_block(idx, slot, u, ss, gain, out_w):
    def kernel(i, u_ref, ss_ref, gain_ref, w_ref, own_ref, oth_ref, lhs):
        n = pl.program_id(0)

        @pl.when(n == 0)
        def _():
            mean = ss_ref[pl.ds(i[slot], 1), :] / (DINNER // GROUPS)
            rows = jnp.broadcast_to(lax.rsqrt(mean + 1e-05), (128, 128))
            scale = jnp.transpose(rows)
            for p in range(4):
                ch = slice(128 * p, 128 * p + 128)
                normed = (u_ref[:, ch] * scale * gain_ref[:, ch]).astype(BF16)
                for t in range(8):
                    core, tile = t % 2, t // 2
                    at = lax.bitwise_xor(jnp.int32(core), i[13]) * 64 + tile * 16
                    lhs[pl.ds(pl.multiple_of(at, 16), 16), ch] = normed[t * 16 : t * 16 + 16, :]

        part = dot(lhs[...], w_ref[...])
        own_ref[...] = part[0:64, :]
        oth_ref[...] = part[64:128, :]

    return pl.pallas_call(
        kernel,
        out_shape=[sds((64, 4096), F32)] * 2,
        grid_spec=pltpu.PrefetchScalarGridSpec(
            num_scalar_prefetch=1,
            grid=(4,),
            in_specs=[
                pl.BlockSpec((128, 512), lambda n, i: (i[slot], 0)),
                pl.BlockSpec((4, 128), lambda n, i: (0, 0)),
                pl.BlockSpec((1, 512), lambda n, i: (0, 0)),
                pl.BlockSpec((512, 1024), lambda n, i: (0, n)),
            ],
            out_specs=[
                pl.BlockSpec((64, 1024), lambda n, i: (0, n)),
                pl.BlockSpec((64, 1024), lambda n, i: (0, n)),
            ],
            scratch_shapes=[pltpu.VMEM((128, 512), BF16)],
        ),
        compiler_params=pltpu.CompilerParams(vmem_limit_bytes=14 * MIB),
        cost_estimate=cost(2 * 128 * 512 * 4096, 6e6),
        name="out_block",
    )(idx, u, ss, gain, out_w)


def body(
    tokens,
    gate_weight,
    input_weight,
    state_weight,
    step_weight,
    input_conv,
    state_conv,
    log_rate,
    step_bias,
    skip_gain,
    norm_gain,
    out_weight,
):
    me = lax.axis_index("tp")
    x, zl, core = me // 8, (me // 2) % 4, me % 2
    y = lax.axis_index("ctx") % 4
    n = jnp.arange(16, dtype=jnp.int32)
    turn = jnp.where(n == 1, 3, jnp.where(n == 2, 1, jnp.where(n == 3, 2, 0)))
    tile = n - 4
    where = jnp.bitwise_xor(tile % 4, zl) * 2 + jnp.bitwise_xor(tile // 4, core)
    idx = jnp.where(n < 4, (x + turn) % 4, where)
    idx = jnp.where(n == 12, zl, jnp.where(n == 13, core, jnp.where(n == 14, y, idx)))
    idx = idx.astype(jnp.int32)

    state_rows_w = state_weight.T
    state_pair = flip(state_rows_w, "tp", 1)
    taps_pair = flip(state_conv, "tp", 1)
    low = core == 0
    first = jnp.where(low, state_rows_w, state_pair)
    second = jnp.where(low, state_pair, state_rows_w)
    small_w = jnp.concatenate([first, second, step_weight.T, jnp.zeros((120, tokens.shape[1]), BF16)], axis=0)
    state_taps = jnp.concatenate(
        [jnp.where(low, state_conv, taps_pair), jnp.where(low, taps_pair, state_conv)], axis=1
    )
    par = jnp.concatenate([log_rate, step_bias, skip_gain])

    tiles = [tokens] + [flip(tokens, "tp", 2 * s) for s in (1, 2, 3)]
    mine = jnp.concatenate(tiles, axis=0)
    right = along_x(mine, 1)
    left = along_x(mine, -1)
    mine_other = flip(mine, "tp", 1)
    bufs = project([mine, mine_other], [0], idx, None, input_weight, small_w, None)
    far_a = along_x(right[:32], 1)
    far_b = along_x(left[32:], -1)
    right_other = flip(right, "tp", 1)
    left_other = flip(left, "tp", 1)
    bufs = project(
        [right, right_other, left, left_other], [1, 2], idx, None, input_weight, small_w, bufs
    )
    far_a_other = flip(far_a, "tp", 1)
    far_b_other = flip(far_b, "tp", 1)
    fars = [far_a, far_b, far_a_other, far_b_other]
    input_rows, state_rows, step_raw = project(fars, [3], idx, None, input_weight, small_w, bufs)

    halo = jnp.concatenate([input_rows[496:], state_rows[496:]], axis=1)
    halo = send(halo, "ctx", lambda i: i + 1 if i < 7 else None)

    piece = conv_states(idx, state_rows, halo, state_taps)
    pieces = jnp.stack([piece] + [flip(piece, "tp", 2 * s) for s in (1, 2, 3)])
    pieces_other = flip(pieces, "tp", 1)

    xs, x_hi, x_lo, dt, cum = inputs_stage(input_rows, halo, input_conv, step_raw, par)
    payload = state_stage(idx, pieces, pieces_other, x_hi, x_lo, cum)
    ends = [payload[0]] + [half_flip(payload[s], s) for s in (1, 2, 3)]
    y_local, read_vec = scan_stage(idx, pieces, pieces_other, xs, dt, cum, par)
    inc, pre, total = prefix_stage(idx, *ends)
    before = send(total.astype(F16), "ctx", lambda i: i + 4 if i < 4 else None).astype(F32)
    everything = [mine, mine_other, right, right_other, left, left_other] + fars
    (gate_rows,) = project(everything, [0, 1, 2, 3], idx, gate_weight, None, None, None)
    spread = spread_stage(idx, inc, pre, before)
    quarters = [spread[0]] + [half_flip(spread[s], s) for s in (1, 2, 3)]
    u, squares = gate_stage(idx, y_local, read_vec, quarters, cum, gate_rows)

    squares = squares + flip(squares, "tp", 1)
    squares = squares + flip(squares, "tp", 2)
    squares = squares + flip(squares, "tp", 4)

    gain = norm_gain.reshape(1, 512)
    far_own, far_oth = out_block(idx, 3, u, squares, gain, out_weight)
    ahead_own, ahead_oth = out_block(idx, 2, u, squares, gain, out_weight)
    behind_own, behind_oth = out_block(idx, 1, u, squares, gain, out_weight)
    mine_own, mine_oth = out_block(idx, 0, u, squares, gain, out_weight)
    far_sum = swap_add(far_own, far_oth)
    ahead_sum = swap_add(ahead_own, ahead_oth)
    behind_sum = swap_add(behind_own, behind_oth)
    mine_sum = swap_add(mine_own, mine_oth)
    got_a = along_x(narrow(far_sum[:32]), 1)
    got_b = along_x(narrow(far_sum[32:]), -1)
    ahead_b = along_x(narrow(ahead_sum[32:]), 1)
    behind_a = along_x(narrow(behind_sum[:32]), -1)
    ahead_a = along_x(narrow(ahead_sum[:32] + widen(got_a)), 1)
    behind_b = along_x(narrow(behind_sum[32:] + widen(got_b)), -1)
    top = mine_sum[:32] + widen(ahead_a) + widen(behind_a)
    bottom = mine_sum[32:] + widen(ahead_b) + widen(behind_b)
    block = jnp.concatenate([top, bottom], axis=0).reshape(4, 16, 4096)
    out = lax.dynamic_index_in_dim(block, zl, 0, False)
    for s in (1, 2, 3):
        part = narrow(lax.dynamic_index_in_dim(block, jnp.bitwise_xor(zl, s), 0, False))
        part = flip(part, "tp", 2 * s)
        out = out + widen(part)
    return out.astype(BF16)


def half_flip(value, mask):
    return flip(value.astype(F16), "ctx", mask).astype(F32)


def narrow(value):
    return (value * 32.0).astype(F16)


def widen(value):
    return value.astype(F32) * 0.03125


def swap_add(own, other):
    return own + widen(flip(narrow(other), "tp", 1))


def solution(mesh):
    placed = (
        P(("ctx", "tp"), None),
        P(None, "tp"),
        P(None, "tp"),
        P(None, "tp"),
        P(None, "tp"),
        P(None, "tp"),
        P(None, "tp"),
        P("tp"),
        P("tp"),
        P("tp"),
        P("tp"),
        P("tp", None),
    )

    return jax.shard_map(
        body, mesh=mesh, in_specs=placed, out_specs=P(("ctx", "tp"), None), check_vma=False
    )
```

```python
import jax
import jax.numpy as jnp
from jax import lax
from jax.experimental import pallas as pl
from jax.experimental.pallas import tpu as pltpu
from jax.sharding import PartitionSpec as P


GROUPS = 4
CONV = 4
DINNER = 16384
F32 = jnp.float32
BF16 = jnp.bfloat16
F16 = jnp.float16
MIB = 1024 * 1024


VM = pl.BlockSpec(memory_space=pltpu.VMEM)
SM = pl.BlockSpec(memory_space=pltpu.SMEM)


def sds(shape, dtype):
    return jax.ShapeDtypeStruct(shape, dtype)


def cost(flops, nbytes):
    return pl.CostEstimate(flops=int(flops), bytes_accessed=int(nbytes), transcendentals=0)


def send(array, axis, to):
    size = lax.axis_size(axis)
    pairs = [(i, to(i)) for i in range(size) if to(i) is not None]
    return lax.ppermute(array, axis, pairs)


def hop(array, to):
    pairs = [(c * 32 + t, to(c, t)) for c in range(8) for t in range(32)]
    pairs = [(i, d[0] * 32 + d[1]) for i, d in pairs if d is not None]
    return lax.ppermute(array, ("ctx", "tp"), pairs)


def flip(array, axis, mask):
    return send(array, axis, lambda i: i ^ mask)


def along_x(array, by):
    return send(array, "tp", lambda i: (i + 8 * by) % 32)


def dot(a, b):
    return lax.dot_general(a, b, (((1,), (0,)), ((), ())), preferred_element_type=F32)


def dot_nt(a, b):
    return lax.dot_general(a, b, (((1,), (1,)), ((), ())), preferred_element_type=F32)


def dot_tn(a, b):
    return lax.dot_general(a, b, (((0,), (0,)), ((), ())), preferred_element_type=F32)


def silu(v):
    return v * jax.nn.sigmoid(v)


def pair_scale(cols, pair):
    rows = cols.shape[0]
    lane = lax.broadcasted_iota(jnp.int32, (rows, 128), 1)
    low = jnp.broadcast_to(cols[:, 2 * pair : 2 * pair + 1], (rows, 128))
    high = jnp.broadcast_to(cols[:, 2 * pair + 1 : 2 * pair + 2], (rows, 128))
    return jnp.where(lane < 64, low, high)


def split(value):
    high = value.astype(BF16)
    return high, (value - high.astype(F32)).astype(BF16)


def project(parts, slots, idx, gate_w, input_w, small_w, bufs):
    depth = parts[0].shape[1]
    steps = 4
    kb = depth // steps
    count = len(slots)
    rows = 128 * count
    weights, wspecs, outs, accs = [], [], [], []
    if gate_w is not None:
        weights.append(gate_w)
        wspecs.append(pl.BlockSpec((kb, 512), lambda k, i: (k, 0)))
        outs.append(sds((512, 512), BF16))
        accs.append(pltpu.VMEM((rows, 512), F32))
    if input_w is not None:
        weights += [input_w, small_w]
        wspecs += [
            pl.BlockSpec((kb, 512), lambda k, i: (k, 0)),
            pl.BlockSpec((256, kb), lambda k, i: (0, k)),
        ]
        outs += [sds((512, 512), BF16), sds((512, 128), BF16), sds((8, 512), F32)]
        accs += [pltpu.VMEM((rows, 512), F32), pltpu.VMEM((rows, 256), F32)]
    nw, no, na = len(weights), len(outs), len(accs)
    aliased = [] if bufs is None else list(bufs)
    ready = [pltpu.VMEM((rows, 512), BF16)] if gate_w is not None else []
    if input_w is not None:
        ready += [pltpu.VMEM((rows, 512), BF16), pltpu.VMEM((rows, 128), BF16), pltpu.VMEM((8, rows), F32)]
        ready += [pltpu.VMEM((rows, 128), F32)]
    nl = len(parts)

    def kernel(i, *refs):
        lrefs, refs = refs[:nl], refs[nl:]
        wrefs, refs = refs[:nw], refs[nw + len(aliased) :]
        orefs, refs = refs[:no], refs[no:]
        arefs, refs = refs[:na], refs[na:]
        rrefs, sem = refs[:-1], refs[-1]
        k = pl.program_id(0)
        lhs = jnp.concatenate([r[...] for r in lrefs], axis=0)
        for n, w in enumerate(wrefs):
            nt = input_w is not None and n == nw - 1
            part = dot_nt(lhs, w[...]) if nt else dot(lhs, w[...])

            @pl.when(k == 0)
            def _():
                arefs[n][...] = part

            @pl.when(k > 0)
            def _():
                arefs[n][...] += part

        @pl.when(k == steps - 1)
        def _():
            copies = []
            for s in range(count):
                for t in range(8):
                    at = slice(s * 128 + t * 16, s * 128 + t * 16 + 16)
                    dst = pl.ds(pl.multiple_of(i[4 + t] * 16, 16) + s * 128, 16)
                    n = 0
                    if gate_w is not None:
                        rrefs[n][dst, :] = arefs[n][at, :].astype(BF16)
                        n += 1
                    if input_w is not None:
                        rrefs[n][dst, :] = arefs[n][at, :].astype(BF16)
                        rrefs[n + 1][dst, :] = arefs[n + 1][at, 0:128].astype(BF16)
                        rrefs[n + 3][dst, :] = arefs[n + 1][at, 128:256]
                here = slice(s * 128, s * 128 + 128)
                if input_w is not None:
                    rrefs[n + 2][:, here] = jnp.transpose(rrefs[n + 3][here, :])[0:8, :]
                there = pl.ds(pl.multiple_of(i[slots[s]] * 128, 128), 128)
                for n in range(no):
                    if n == no - 1 and input_w is not None:
                        source, target = rrefs[n].at[:, here], orefs[n].at[:, there]
                    else:
                        source, target = rrefs[n].at[here, :], orefs[n].at[there, :]
                    copies.append(pltpu.make_async_copy(source, target, sem.at[len(copies)]))
            for copy in copies:
                copy.start()
            for copy in copies:
                copy.wait()

    cols = (512 if gate_w is not None else 0) + (768 if input_w is not None else 0)
    first = 1 + nl + nw
    lspecs = [pl.BlockSpec((p.shape[0], kb), lambda k, i: (0, k)) for p in parts]
    out = pl.pallas_call(
        kernel,
        out_shape=outs,
        grid_spec=pltpu.PrefetchScalarGridSpec(
            num_scalar_prefetch=1,
            grid=(steps,),
            in_specs=lspecs + wspecs + [pl.BlockSpec(memory_space=pl.ANY)] * len(aliased),
            out_specs=[pl.BlockSpec(memory_space=pl.ANY)] * no,
            scratch_shapes=accs + ready + [pltpu.SemaphoreType.DMA((no * count,))],
        ),
        input_output_aliases={first + n: n for n in range(len(aliased))},
        compiler_params=pltpu.CompilerParams(vmem_limit_bytes=14 * MIB),
        cost_estimate=cost(2 * rows * depth * cols, 2 * depth * cols),
    )(idx, *parts, *weights, *aliased)
    return list(out)


def project_resident(parts, halo, slots, idx, input_w, small_w, bufs):
    depth = parts[0].shape[1]
    kb = 1024
    count = len(slots)
    rows = 128 * count
    extra = 0 if halo is None else 16
    lefts = list(parts) + ([] if halo is None else [halo])
    nl = len(lefts)
    outs = [sds((512, 512), BF16), sds((512, 128), BF16), sds((8, 512), F32)]
    ospecs = [pl.BlockSpec(memory_space=pl.ANY)] * 3
    if extra:
        outs.append(sds((16, 640), BF16))
        ospecs.append(VM)
    no = len(outs)
    aliased = [] if bufs is None else list(bufs)

    def kernel(i, *refs):
        lrefs, refs = refs[:nl], refs[nl:]
        w_ref, s_ref = refs[:2]
        refs = refs[2 + len(aliased) :]
        orefs, refs = refs[:no], refs[no:]
        acc, acc_s, main, small, turned, steps, sem = refs

        acc[...] = jnp.zeros_like(acc)
        acc_s[...] = jnp.zeros_like(acc_s)

        def one(k, carry):
            here = pl.ds(pl.multiple_of(k * kb, kb), kb)
            lhs = jnp.concatenate([r[:, here] for r in lrefs], axis=0)
            acc[...] += dot(lhs, w_ref[here, :])
            acc_s[...] += dot_nt(lhs, s_ref[:, here])
            return carry

        lax.fori_loop(0, depth // kb, one, 0)
        copies = []
        for s in range(count):
            for t in range(8):
                at = slice(s * 128 + t * 16, s * 128 + t * 16 + 16)
                dst = pl.ds(pl.multiple_of(i[4 + t] * 16, 16) + s * 128, 16)
                main[dst, :] = acc[at, :].astype(BF16)
                small[dst, :] = acc_s[at, 0:128].astype(BF16)
                turned[dst, :] = acc_s[at, 128:256]
            here = slice(s * 128, s * 128 + 128)
            steps[:, here] = jnp.transpose(turned[here, :])[0:8, :]
            there = pl.ds(pl.multiple_of(i[slots[s]] * 128, 128), 128)
            for source, target in (
                (main.at[here, :], orefs[0].at[there, :]),
                (small.at[here, :], orefs[1].at[there, :]),
                (steps.at[:, here], orefs[2].at[:, there]),
            ):
                copies.append(pltpu.make_async_copy(source, target, sem.at[len(copies)]))
        for copy in copies:
            copy.start()
        if extra:
            orefs[3][:, 0:512] = acc[rows : rows + 16, :].astype(BF16)
            orefs[3][:, 512:640] = acc_s[rows : rows + 16, 0:128].astype(BF16)
        for copy in copies:
            copy.wait()

    first = 1 + nl + 2
    out = pl.pallas_call(
        kernel,
        out_shape=outs,
        in_specs=[SM] + [VM] * (nl + 2) + [pl.BlockSpec(memory_space=pl.ANY)] * len(aliased),
        out_specs=ospecs,
        scratch_shapes=[
            pltpu.VMEM((rows + extra, 512), F32),
            pltpu.VMEM((rows + extra, 256), F32),
            pltpu.VMEM((rows, 512), BF16),
            pltpu.VMEM((rows, 128), BF16),
            pltpu.VMEM((rows, 128), F32),
            pltpu.VMEM((8, rows), F32),
            pltpu.SemaphoreType.DMA((3 * count,)),
        ],
        input_output_aliases={first + n: n for n in range(len(aliased))},
        compiler_params=pltpu.CompilerParams(vmem_limit_bytes=14 * MIB),
        cost_estimate=cost(2 * rows * depth * 768, 2 * depth * 768),
    )(idx, *lefts, input_w, small_w, *aliased)
    return list(out)


def conv_rows(window, taps, rows):
    running = taps[CONV : CONV + 1, :] + taps[0:1, :] * window[13 : 13 + rows, :]
    for k in range(1, CONV):
        running = running + taps[k : k + 1, :] * window[13 + k : 13 + k + rows, :]
    return silu(running)


def conv_states_kernel(idx, rows_ref, halo_ref, taps_ref, out_ref, full):
    taps = taps_ref[...]
    for k in range(4):
        if k == 0:
            window = jnp.concatenate([halo_ref[:, 512:640], rows_ref[0:128, :]], axis=0).astype(F32)
        else:
            window = rows_ref[128 * k - 16 : 128 * k + 128, :].astype(F32)
        full[128 * k : 128 * k + 128, :] = conv_rows(window, taps, 128).astype(BF16)
    half = idx[13]
    out_ref[...] = full[pl.ds(pl.multiple_of(half * 256, 256), 256), :]


def conv_states(idx, rows, halo, taps):
    return pl.pallas_call(
        conv_states_kernel,
        out_shape=sds((256, 128), BF16),
        in_specs=[SM, VM, VM, VM],
        out_specs=VM,
        scratch_shapes=[pltpu.VMEM((512, 128), BF16)],
        compiler_params=pltpu.CompilerParams(vmem_limit_bytes=14 * MIB),
        cost_estimate=cost(2e6, 4e5),
        name="conv_states",
    )(idx, rows, halo, taps)


def columns_of(rows8):
    return jnp.transpose(rows8)


def column(par, start):
    row = lax.broadcasted_iota(jnp.int32, (8, 128), 0)
    out = jnp.zeros((8, 128), F32)
    for h in range(8):
        out = jnp.where(row == h, par[start + h], out)
    return out


def inputs_kernel(par_ref, rows_ref, halo_ref, taps_ref, step_ref, x_ref, hi_ref, lo_ref, dt_ref, cum_ref, weight_ref, longer):
    taps = taps_ref[...]
    rate = jnp.exp(column(par_ref, 0))
    bias = column(par_ref, 8)
    lane = lax.broadcasted_iota(jnp.int32, (8, 128), 1)
    dts, cums = [], []
    for k in range(4):
        raw = step_ref[:, 128 * k : 128 * k + 128] + bias
        dt = jnp.maximum(raw, 0.0) + jnp.log1p(jnp.exp(-jnp.abs(raw)))
        cum = -dt * rate
        for b in range(7):
            moved = pltpu.roll(cum, 1 << b, 1)
            cum = cum + jnp.where(lane >= (1 << b), moved, 0.0)
        dts.append(dt)
        cums.append(cum)
        dt_ref[:, 128 * k : 128 * k + 128] = dt
        cum_ref[:, 128 * k : 128 * k + 128] = cum
    after = jnp.zeros((8, 1), F32)
    for k in reversed(range(4)):
        total = cums[k][:, 127:128]
        weight_ref[:, 128 * k : 128 * k + 128] = jnp.exp(total - cums[k] + after) * dts[k]
        after = after + total
    longer[0:16, :] = halo_ref[:, 0:512]
    longer[16:528, :] = rows_ref[...]

    def one(k, carry):
        start = pl.multiple_of(k * 128, 128)
        here = pl.ds(start, 128)
        cols = columns_of(weight_ref[:, here])
        window = longer[pl.ds(start, 144), :]
        for p in range(4):
            ch = slice(128 * p, 128 * p + 128)
            x = conv_rows(window[:, ch].astype(F32), taps[:, ch], 128).astype(BF16)
            x_ref[here, ch] = x
            hi, lo = split(x.astype(F32) * pair_scale(cols, p))
            hi_ref[here, ch] = hi
            lo_ref[here, ch] = lo
        return carry

    lax.fori_loop(0, 4, one, 0)


def inputs_stage(rows, halo, taps, step, par):
    return pl.pallas_call(
        inputs_kernel,
        out_shape=[sds((512, 512), BF16)] * 3 + [sds((8, 512), F32)] * 2,
        in_specs=[SM] + [VM] * 4,
        out_specs=[VM] * 5,
        scratch_shapes=[pltpu.VMEM((8, 512), F32), pltpu.VMEM((528, 512), BF16)],
        compiler_params=pltpu.CompilerParams(vmem_limit_bytes=14 * MIB),
        cost_estimate=cost(1e7, 2e6),
        name="inputs_stage",
    )(par, rows, halo, taps, step)


def gathered_block(idx, own_ref, oth_ref, block, rows):
    place = lax.bitwise_xor(jnp.int32(block), idx[12])
    return jnp.where(idx[13] == rows, own_ref[place], oth_ref[place])


LOG2 = 0.6931471805599453


def scaled(value):
    most = jnp.max(jnp.abs(value), axis=0, keepdims=True)
    power = jnp.ceil(jnp.log(most) * (1.0 / LOG2))
    power = jnp.minimum(jnp.maximum(power, -100.0), 120.0)
    return value * jnp.exp(power * -LOG2), power


def unscaled(ref_value):
    return ref_value[0:256, :] * jnp.exp(ref_value[256:257, :] * LOG2)


def state_kernel(idx, own_ref, oth_ref, hi_ref, lo_ref, cum_ref, out_ref):
    halves = []
    for n in range(2):
        write = jnp.concatenate(
            [gathered_block(idx, own_ref, oth_ref, n, 0), gathered_block(idx, own_ref, oth_ref, n, 1)], axis=0
        )
        halves.append(write)
    write = jnp.concatenate(halves, axis=1)
    state = dot_tn(write, hi_ref[...]) + dot_tn(write, lo_ref[...])
    total = (
        cum_ref[:, 127:128] + cum_ref[:, 255:256] + cum_ref[:, 383:384] + cum_ref[:, 511:512]
    )
    damp = jnp.maximum(total, -110.0) * 256.0
    lane = lax.broadcasted_iota(jnp.int32, (16, 128), 1)
    row = lax.broadcasted_iota(jnp.int32, (16, 128), 0)
    for q in range(4):
        place = lax.bitwise_xor(jnp.int32(q), idx[14])
        mant, power = scaled(state[:, 128 * q : 128 * q + 128])
        out_ref[place, 0:256, :] = mant
        low = jnp.broadcast_to(damp[2 * q : 2 * q + 1, :], (16, 128))
        high = jnp.broadcast_to(damp[2 * q + 1 : 2 * q + 2, :], (16, 128))
        value = jnp.where(lane < 64, low, high)
        one = value.astype(BF16).astype(F32)
        two = (value - one).astype(BF16).astype(F32)
        three = value - one - two
        packed = jnp.where(row == 1, one, jnp.where(row == 2, two, jnp.where(row == 3, three, 0.0)))
        out_ref[place, 256:272, :] = jnp.where(row == 0, power, packed)


def state_stage(idx, own, oth, hi, lo, cum):
    return pl.pallas_call(
        state_kernel,
        out_shape=sds((4, 272, 128), F32),
        in_specs=[SM] + [VM] * 5,
        out_specs=VM,
        compiler_params=pltpu.CompilerParams(vmem_limit_bytes=14 * MIB),
        cost_estimate=cost(2.7e8, 2e6),
        name="state_stage",
    )(idx, own, oth, hi, lo, cum)


def prefix_kernel(idx, s0, s1, s2, s3, inc_ref, pre_ref, tot_ref):
    place = idx[14]
    odd = lax.bitwise_and(place, 1) == 1
    far = lax.bitwise_and(place, 2) == 2
    slots = [s0[...], s1[...], s2[...], s3[...]]
    a, b = jnp.where(odd, slots[1], slots[0]), jnp.where(odd, slots[0], slots[1])
    c, d = jnp.where(odd, slots[3], slots[2]), jnp.where(odd, slots[2], slots[3])
    ordered = [jnp.where(far, c, a), jnp.where(far, d, b), jnp.where(far, a, c), jnp.where(far, b, d)]
    running = jnp.zeros((256, 128), F32)
    carried = jnp.ones((1, 128), F32)
    for k in range(4):
        inc_ref[k] = running
        pre_ref[k] = jnp.broadcast_to(carried, (8, 128))
        tail = ordered[k][256:272, :]
        damp = jnp.exp((tail[1:2, :] + tail[2:3, :] + tail[3:4, :]) * (1.0 / 256.0))
        running = damp * running + unscaled(ordered[k])
        carried = carried * damp
    mant, power = scaled(running)
    tot_ref[0:256, :] = mant
    tot_ref[256:272, :] = jnp.broadcast_to(power, (16, 128))


def prefix_stage(idx, s0, s1, s2, s3):
    return pl.pallas_call(
        prefix_kernel,
        out_shape=[sds((4, 256, 128), F32), sds((4, 8, 128), F32), sds((272, 128), F32)],
        in_specs=[SM] + [VM] * 4,
        out_specs=[VM] * 3,
        compiler_params=pltpu.CompilerParams(vmem_limit_bytes=14 * MIB),
        cost_estimate=cost(1e6, 1e6),
        name="prefix_stage",
    )(idx, s0, s1, s2, s3)


def spread_kernel(idx, inc_ref, pre_ref, far_ref, out_ref):
    far = jnp.where(idx[15] > 0, unscaled(far_ref[...]), 0.0)
    for k in range(4):
        place = lax.bitwise_xor(jnp.int32(k), idx[14])
        mant, power = scaled(inc_ref[k] + pre_ref[k][0:1, :] * far)
        out_ref[place, 0:256, :] = mant
        out_ref[place, 256:272, :] = jnp.broadcast_to(power, (16, 128))


def spread_stage(idx, inc, pre, far):
    return pl.pallas_call(
        spread_kernel,
        out_shape=sds((4, 272, 128), F32),
        in_specs=[SM] + [VM] * 3,
        out_specs=VM,
        compiler_params=pltpu.CompilerParams(vmem_limit_bytes=14 * MIB),
        cost_estimate=cost(1e6, 1e6),
        name="spread_stage",
    )(idx, inc, pre, far)


def scan_kernel(idx, par_ref, own_ref, oth_ref, x_ref, dt_ref, cum_ref, y_ref, read_ref, state):
    row = lax.broadcasted_iota(jnp.int32, (128, 128), 0)
    col = lax.broadcasted_iota(jnp.int32, (128, 128), 1)
    causal = row >= col
    left = col < 64
    zero = jnp.zeros((128, 128), BF16)
    state[...] = jnp.zeros_like(state)

    def one(k, carry):
        here = pl.ds(pl.multiple_of(k * 128, 128), 128)
        half = lax.div(k, 2)
        sub = pl.ds(pl.multiple_of(lax.rem(k, 2) * 128, 128), 128)

        def part(block):
            place = lax.bitwise_xor(jnp.int32(block), idx[12])
            return jnp.where(idx[13] == half, own_ref[place, sub, :], oth_ref[place, sub, :])

        write = jnp.concatenate([part(0), part(1)], axis=1)
        read = jnp.concatenate([part(2), part(3)], axis=1)
        read_ref[here, :] = read
        scores = dot_nt(read, write)
        cum = cum_ref[:, here]
        dt = dt_ref[:, here]
        cols = columns_of(cum)
        exp_cols = columns_of(jnp.exp(cum))
        total = cum[:, 127:128]
        end_cols = columns_of(jnp.exp(total - cum) * dt)
        damp = jnp.exp(total)
        for p in range(4):
            ch = slice(128 * p, 128 * p + 128)
            x = x_ref[here, ch]
            xf = x.astype(F32)
            mixes = []
            for h in (2 * p, 2 * p + 1):
                gap = jnp.broadcast_to(cols[:, h : h + 1], (128, 128)) - cum[h : h + 1, :]
                damping = jnp.exp(jnp.where(causal, gap, -jnp.inf))
                mixes.append(scores * damping * dt[h : h + 1, :])
            mix = jnp.concatenate(mixes, axis=1)
            both = jnp.concatenate([jnp.where(left, x, zero), jnp.where(left, zero, x)], axis=0)
            mix_hi, mix_lo = split(mix)
            y = dot(mix_hi, both) + dot(mix_lo, both)
            y = y + jnp.where(left[0:1, :], par_ref[16 + 2 * p], par_ref[17 + 2 * p]) * xf
            before = state[:, ch]
            s_hi, s_lo = split(before)
            y_ref[here, ch] = y + pair_scale(exp_cols, p) * (dot(read, s_hi) + dot(read, s_lo))
            in_hi, in_lo = split(xf * pair_scale(end_cols, p))
            keep = jnp.where(
                left[0:1, :],
                jnp.broadcast_to(damp[2 * p : 2 * p + 1, :], (1, 128)),
                jnp.broadcast_to(damp[2 * p + 1 : 2 * p + 2, :], (1, 128)),
            )
            state[:, ch] = keep * before + dot_tn(write, in_hi) + dot_tn(write, in_lo)
        return carry

    lax.fori_loop(0, 4, one, 0)


def scan_stage(idx, own, oth, x, dt, cum, par):
    return pl.pallas_call(
        scan_kernel,
        out_shape=[sds((512, 512), F32), sds((512, 256), BF16)],
        in_specs=[SM] * 2 + [VM] * 5,
        out_specs=[VM] * 2,
        scratch_shapes=[pltpu.VMEM((256, 512), F32)],
        compiler_params=pltpu.CompilerParams(vmem_limit_bytes=14 * MIB),
        cost_estimate=cost(6e9, 3e6),
        name="scan_stage",
    )(idx, par, own, oth, x, dt, cum)


def gate_kernel(idx, y_ref, read_ref, q0, q1, q2, q3, cum_ref, gate_ref, u_ref, ss_ref):
    place = idx[14]
    odd = lax.bitwise_and(place, 1) == 1
    far = lax.bitwise_and(place, 2) == 2
    slots = [q0[...], q1[...], q2[...], q3[...]]
    a, b = jnp.where(odd, slots[1], slots[0]), jnp.where(odd, slots[0], slots[1])
    c, d = jnp.where(odd, slots[3], slots[2]), jnp.where(odd, slots[2], slots[3])
    ordered = [jnp.where(far, c, a), jnp.where(far, d, b), jnp.where(far, a, c), jnp.where(far, b, d)]
    halves = [split(unscaled(v)) for v in ordered]

    def one(k, before):
        here = pl.ds(pl.multiple_of(k * 128, 128), 128)
        cum = cum_ref[:, here]
        cols = columns_of(jnp.exp(cum + before))
        read = read_ref[here, :]
        squares = jnp.zeros((128, 128), F32)
        for p in range(4):
            ch = slice(128 * p, 128 * p + 128)
            carried = dot(read, halves[p][0]) + dot(read, halves[p][1])
            y = y_ref[here, ch] + pair_scale(cols, p) * carried
            u = y * silu(gate_ref[here, ch].astype(F32))
            u_ref[here, ch] = u
            squares = squares + u * u
        ss_ref[pl.ds(k, 1), :] = jnp.sum(jnp.transpose(squares), axis=0, keepdims=True)
        return before + cum[:, 127:128]

    lax.fori_loop(0, 4, one, jnp.zeros((8, 1), F32))


def gate_stage(idx, y, read, quarters, cum, gate):
    return pl.pallas_call(
        gate_kernel,
        out_shape=[sds((512, 512), F32), sds((4, 128), F32)],
        in_specs=[SM] + [VM] * 8,
        out_specs=[VM] * 2,
        compiler_params=pltpu.CompilerParams(vmem_limit_bytes=14 * MIB),
        cost_estimate=cost(2e8, 3e6),
        name="gate_stage",
    )(idx, y, read, *quarters, cum, gate)


def load_kernel(src_ref, dst_ref, sem):
    copy = pltpu.make_async_copy(src_ref, dst_ref, sem)
    copy.start()
    copy.wait()


def load(array):
    return pl.pallas_call(
        load_kernel,
        out_shape=sds(array.shape, array.dtype),
        in_specs=[pl.BlockSpec(memory_space=pltpu.HBM)],
        out_specs=VM,
        scratch_shapes=[pltpu.SemaphoreType.DMA],
        compiler_params=pltpu.CompilerParams(vmem_limit_bytes=8 * MIB),
        cost_estimate=cost(1, 8 * MIB),
        name="load",
    )(array)


def out_block(idx, slots, u, ss, gain, out_w):
    count = len(slots)
    rows = 64 * count

    def kernel(i, u_ref, ss_ref, gain_ref, w_ref, own_ref, oth_ref, lhs):
        for s in range(count):
            place = i[slots[s]]
            mean = ss_ref[pl.ds(place, 1), :] / (DINNER // GROUPS)
            scale = jnp.transpose(jnp.broadcast_to(lax.rsqrt(mean + 1e-05), (128, 128)))
            here = pl.ds(pl.multiple_of(place * 128, 128), 128)
            for p in range(4):
                ch = slice(128 * p, 128 * p + 128)
                normed = (u_ref[here, ch] * scale * gain_ref[:, ch]).astype(BF16)
                for t in range(8):
                    core, tile = t % 2, t // 2
                    at = lax.bitwise_xor(jnp.int32(core), i[13]) * rows + 64 * s + tile * 16
                    lhs[pl.ds(pl.multiple_of(at, 16), 16), ch] = normed[t * 16 : t * 16 + 16, :]

        def one(n, carry):
            here = pl.ds(pl.multiple_of(n * 1024, 1024), 1024)
            part = dot(lhs[...], w_ref[:, here])
            own_ref[:, here] = part[0:rows, :]
            oth_ref[:, here] = part[rows : 2 * rows, :]
            return carry

        lax.fori_loop(0, 4, one, 0)

    return pl.pallas_call(
        kernel,
        out_shape=[sds((rows, 4096), F32)] * 2,
        in_specs=[SM] + [VM] * 4,
        out_specs=[VM] * 2,
        scratch_shapes=[pltpu.VMEM((2 * rows, 512), BF16)],
        compiler_params=pltpu.CompilerParams(vmem_limit_bytes=20 * MIB),
        cost_estimate=cost(4 * rows * 512 * 4096, 6e6),
        name="out_block",
    )(idx, u, ss, gain, out_w)


def body(
    tokens,
    gate_weight,
    input_weight,
    state_weight,
    step_weight,
    input_conv,
    state_conv,
    log_rate,
    step_bias,
    skip_gain,
    norm_gain,
    out_weight,
):
    me = lax.axis_index("tp")
    x, zl, core = me // 8, (me // 2) % 4, me % 2
    y, later = lax.axis_index("ctx") % 4, lax.axis_index("ctx") // 4
    n = jnp.arange(16, dtype=jnp.int32)
    turn = jnp.where(n == 1, 3, jnp.where(n == 2, 1, jnp.where(n == 3, 2, 0)))
    tile = n - 4
    where = jnp.bitwise_xor(tile % 4, zl) * 2 + jnp.bitwise_xor(tile // 4, core)
    idx = jnp.where(n < 4, (x + turn) % 4, where)
    idx = jnp.where(n == 12, zl, jnp.where(n == 13, core, jnp.where(n == 14, y, jnp.where(n == 15, later, idx))))
    idx = idx.astype(jnp.int32)

    state_rows_w = state_weight.T
    state_pair = flip(state_rows_w, "tp", 1)
    taps_pair = flip(state_conv, "tp", 1)
    low = core == 0
    first = jnp.where(low, state_rows_w, state_pair)
    second = jnp.where(low, state_pair, state_rows_w)
    small_w = jnp.concatenate([first, second, step_weight.T, jnp.zeros((120, tokens.shape[1]), BF16)], axis=0)
    state_taps = jnp.concatenate(
        [jnp.where(low, state_conv, taps_pair), jnp.where(low, taps_pair, state_conv)], axis=1
    )
    par = jnp.concatenate([log_rate, step_bias, skip_gain])

    tiles = [tokens] + [flip(tokens, "tp", 2 * s) for s in (1, 2, 3)]
    mine = jnp.concatenate(tiles, axis=0)
    right = along_x(mine, 1)
    left = along_x(mine, -1)
    mine_other = flip(mine, "tp", 1)
    last = lax.dynamic_index_in_dim(mine.reshape(4, 16, mine.shape[1]), 3 - zl, 0, False)[8:]
    before_all = {"h0": lambda c, t: (c + 1, t) if c < 7 and t >= 24 and t % 2 else None}
    before_all["h1"] = lambda c, t: (c, t - 24) if t >= 24 and t % 2 else None
    before_all["h2"] = lambda c, t: (c, t - 8) if t >= 24 and t % 2 else ((c, t + 8) if t < 8 and t % 2 else None)
    before_all["h3"] = lambda c, t: (c, t - 1) if t % 2 else None
    rim = hop(last, before_all["h0"])
    bufs = project_resident([mine, mine_other], None, [0], idx, input_weight, small_w, None)
    rim = rim + hop(rim, before_all["h1"])
    far_a = along_x(right[:32], 1)
    far_b = along_x(left[32:], -1)
    right_other = flip(right, "tp", 1)
    left_other = flip(left, "tp", 1)
    rim = rim + hop(rim, before_all["h2"])
    bufs = project_resident(
        [right, right_other, left, left_other], None, [1, 2], idx, input_weight, small_w, bufs
    )
    rim = rim + hop(rim, before_all["h3"])
    rim = jnp.concatenate([jnp.zeros_like(rim), rim], axis=0)
    far_a_other = flip(far_a, "tp", 1)
    far_b_other = flip(far_b, "tp", 1)
    fars = [far_a, far_b, far_a_other, far_b_other]
    input_rows, state_rows, step_raw, halo = project_resident(
        fars, rim, [3], idx, input_weight, small_w, bufs
    )

    piece = conv_states(idx, state_rows, halo, state_taps)
    pieces = jnp.stack([piece] + [flip(piece, "tp", 2 * s) for s in (1, 2, 3)])
    pieces_other = flip(pieces, "tp", 1)

    xs, x_hi, x_lo, dt, cum = inputs_stage(input_rows, halo, input_conv, step_raw, par)
    payload = state_stage(idx, pieces, pieces_other, x_hi, x_lo, cum)
    ends = [payload[0]] + [half_flip(payload[s], s) for s in (1, 2, 3)]
    y_local, read_vec = scan_stage(idx, pieces, pieces_other, xs, dt, cum, par)
    inc, pre, total = prefix_stage(idx, *ends)
    before = half_flip(total, 4)
    everything = [mine, mine_other, right, right_other, left, left_other] + fars
    (gate_rows,) = project(everything, [0, 1, 2, 3], idx, gate_weight, None, None, None)
    spread = spread_stage(idx, inc, pre, before)
    quarters = [spread[0]] + [half_flip(spread[s], s) for s in (1, 2, 3)]
    u, squares = gate_stage(idx, y_local, read_vec, quarters, cum, gate_rows)

    squares = squares + flip(squares, "tp", 1)
    squares = squares + flip(squares, "tp", 2)
    squares = squares + flip(squares, "tp", 4)

    gain = norm_gain.reshape(1, 512)
    out_w = load(out_weight)
    far_own, far_oth = out_block(idx, [3], u, squares, gain, out_w)
    far_sum = swap_add(far_own, far_oth)
    got_a = along_x(narrow(far_sum[:32]), 1)
    got_b = along_x(narrow(far_sum[32:]), -1)
    rest_own, rest_oth = out_block(idx, [2, 1, 0], u, squares, gain, out_w)
    rest = swap_add(rest_own, rest_oth)
    ahead_sum, behind_sum, mine_sum = rest[:64], rest[64:128], rest[128:]
    to_right = narrow(jnp.concatenate([ahead_sum[:32] + widen(got_a), ahead_sum[32:]], axis=0))
    to_left = narrow(jnp.concatenate([behind_sum[:32], behind_sum[32:] + widen(got_b)], axis=0))
    from_left = along_x(to_right, 1)
    from_right = along_x(to_left, -1)
    both_sums = mine_sum + widen(from_left) + widen(from_right)
    block = both_sums.reshape(4, 16, 4096)
    out = lax.dynamic_index_in_dim(block, zl, 0, False)
    for s in (1, 2, 3):
        part = narrow(lax.dynamic_index_in_dim(block, jnp.bitwise_xor(zl, s), 0, False))
        part = flip(part, "tp", 2 * s)
        out = out + widen(part)
    return out.astype(BF16)


def half_flip(value, mask):
    return flip(value.astype(F16), "ctx", mask).astype(F32)


def narrow(value):
    return (value * 32.0).astype(F16)


def widen(value):
    return value.astype(F32) * 0.03125


def swap_add(own, other):
    return own + widen(flip(narrow(other), "tp", 1))


def solution(mesh):
    placed = (
        P(("ctx", "tp"), None),
        P(None, "tp"),
        P(None, "tp"),
        P(None, "tp"),
        P(None, "tp"),
        P(None, "tp"),
        P(None, "tp"),
        P("tp"),
        P("tp"),
        P("tp"),
        P("tp"),
        P("tp", None),
    )

    return jax.shard_map(
        body, mesh=mesh, in_specs=placed, out_specs=P(("ctx", "tp"), None), check_vma=False
    )
```

```python
import jax
import jax.numpy as jnp
from jax import lax
from jax.experimental import pallas as pl
from jax.experimental.pallas import tpu as pltpu
from jax.sharding import PartitionSpec as P


GROUPS = 4
CONV = 4
DINNER = 16384
F32 = jnp.float32
BF16 = jnp.bfloat16
F16 = jnp.float16
MIB = 1024 * 1024


VM = pl.BlockSpec(memory_space=pltpu.VMEM)
SM = pl.BlockSpec(memory_space=pltpu.SMEM)


def sds(shape, dtype):
    return jax.ShapeDtypeStruct(shape, dtype)


def cost(flops, nbytes):
    return pl.CostEstimate(flops=int(flops), bytes_accessed=int(nbytes), transcendentals=0)


def send(array, axis, to):
    size = lax.axis_size(axis)
    pairs = [(i, to(i)) for i in range(size) if to(i) is not None]
    return lax.ppermute(array, axis, pairs)


def hop(array, to):
    pairs = [(c * 32 + t, to(c, t)) for c in range(8) for t in range(32)]
    pairs = [(i, d[0] * 32 + d[1]) for i, d in pairs if d is not None]
    return lax.ppermute(array, ("ctx", "tp"), pairs)


def flip(array, axis, mask):
    return send(array, axis, lambda i: i ^ mask)


def along_x(array, by):
    return send(array, "tp", lambda i: (i + 8 * by) % 32)


def dot(a, b):
    return lax.dot_general(a, b, (((1,), (0,)), ((), ())), preferred_element_type=F32)


def dot_nt(a, b):
    return lax.dot_general(a, b, (((1,), (1,)), ((), ())), preferred_element_type=F32)


def dot_tn(a, b):
    return lax.dot_general(a, b, (((0,), (0,)), ((), ())), preferred_element_type=F32)


def silu(v):
    return v * jax.nn.sigmoid(v)


def pair_scale(cols, pair):
    rows = cols.shape[0]
    lane = lax.broadcasted_iota(jnp.int32, (rows, 128), 1)
    low = jnp.broadcast_to(cols[:, 2 * pair : 2 * pair + 1], (rows, 128))
    high = jnp.broadcast_to(cols[:, 2 * pair + 1 : 2 * pair + 2], (rows, 128))
    return jnp.where(lane < 64, low, high)


def split(value):
    high = value.astype(BF16)
    return high, (value - high.astype(F32)).astype(BF16)


def project(parts, slots, idx, gate_w, input_w, small_w, bufs):
    depth = parts[0].shape[1]
    steps = 4
    kb = depth // steps
    count = len(slots)
    rows = 128 * count
    weights, wspecs, outs, accs = [], [], [], []
    if gate_w is not None:
        weights.append(gate_w)
        wspecs.append(pl.BlockSpec((kb, 512), lambda k, i: (k, 0)))
        outs.append(sds((512, 512), BF16))
        accs.append(pltpu.VMEM((rows, 512), F32))
    if input_w is not None:
        weights += [input_w, small_w]
        wspecs += [
            pl.BlockSpec((kb, 512), lambda k, i: (k, 0)),
            pl.BlockSpec((256, kb), lambda k, i: (0, k)),
        ]
        outs += [sds((512, 512), BF16), sds((512, 128), BF16), sds((8, 512), F32)]
        accs += [pltpu.VMEM((rows, 512), F32), pltpu.VMEM((rows, 256), F32)]
    nw, no, na = len(weights), len(outs), len(accs)
    aliased = [] if bufs is None else list(bufs)
    ready = [pltpu.VMEM((rows, 512), BF16)] if gate_w is not None else []
    if input_w is not None:
        ready += [pltpu.VMEM((rows, 512), BF16), pltpu.VMEM((rows, 128), BF16), pltpu.VMEM((8, rows), F32)]
        ready += [pltpu.VMEM((rows, 128), F32)]
    nl = len(parts)

    def kernel(i, *refs):
        lrefs, refs = refs[:nl], refs[nl:]
        wrefs, refs = refs[:nw], refs[nw + len(aliased) :]
        orefs, refs = refs[:no], refs[no:]
        arefs, refs = refs[:na], refs[na:]
        rrefs, sem = refs[:-1], refs[-1]
        k = pl.program_id(0)
        lhs = jnp.concatenate([r[...] for r in lrefs], axis=0)
        for n, w in enumerate(wrefs):
            nt = input_w is not None and n == nw - 1
            part = dot_nt(lhs, w[...]) if nt else dot(lhs, w[...])

            @pl.when(k == 0)
            def _():
                arefs[n][...] = part

            @pl.when(k > 0)
            def _():
                arefs[n][...] += part

        @pl.when(k == steps - 1)
        def _():
            copies = []
            for s in range(count):
                for t in range(8):
                    at = slice(s * 128 + t * 16, s * 128 + t * 16 + 16)
                    dst = pl.ds(pl.multiple_of(i[4 + t] * 16, 16) + s * 128, 16)
                    n = 0
                    if gate_w is not None:
                        rrefs[n][dst, :] = arefs[n][at, :].astype(BF16)
                        n += 1
                    if input_w is not None:
                        rrefs[n][dst, :] = arefs[n][at, :].astype(BF16)
                        rrefs[n + 1][dst, :] = arefs[n + 1][at, 0:128].astype(BF16)
                        rrefs[n + 3][dst, :] = arefs[n + 1][at, 128:256]
                here = slice(s * 128, s * 128 + 128)
                if input_w is not None:
                    rrefs[n + 2][:, here] = jnp.transpose(rrefs[n + 3][here, :])[0:8, :]
                there = pl.ds(pl.multiple_of(i[slots[s]] * 128, 128), 128)
                for n in range(no):
                    if n == no - 1 and input_w is not None:
                        source, target = rrefs[n].at[:, here], orefs[n].at[:, there]
                    else:
                        source, target = rrefs[n].at[here, :], orefs[n].at[there, :]
                    copies.append(pltpu.make_async_copy(source, target, sem.at[len(copies)]))
            for copy in copies:
                copy.start()
            for copy in copies:
                copy.wait()

    cols = (512 if gate_w is not None else 0) + (768 if input_w is not None else 0)
    first = 1 + nl + nw
    lspecs = [pl.BlockSpec((p.shape[0], kb), lambda k, i: (0, k)) for p in parts]
    out = pl.pallas_call(
        kernel,
        out_shape=outs,
        grid_spec=pltpu.PrefetchScalarGridSpec(
            num_scalar_prefetch=1,
            grid=(steps,),
            in_specs=lspecs + wspecs + [pl.BlockSpec(memory_space=pl.ANY)] * len(aliased),
            out_specs=[pl.BlockSpec(memory_space=pl.ANY)] * no,
            scratch_shapes=accs + ready + [pltpu.SemaphoreType.DMA((no * count,))],
        ),
        input_output_aliases={first + n: n for n in range(len(aliased))},
        compiler_params=pltpu.CompilerParams(vmem_limit_bytes=14 * MIB),
        cost_estimate=cost(2 * rows * depth * cols, 2 * depth * cols),
    )(idx, *parts, *weights, *aliased)
    return list(out)


def project_resident(parts, halo, slots, idx, input_w, small_w, bufs):
    depth = parts[0].shape[1]
    kb = 1024
    count = len(slots)
    rows = 128 * count
    extra = 0 if halo is None else 16
    lefts = list(parts) + ([] if halo is None else [halo])
    nl = len(lefts)
    outs = [sds((512, 512), BF16), sds((512, 128), BF16), sds((8, 512), F32)]
    ospecs = [pl.BlockSpec(memory_space=pl.ANY)] * 3
    if extra:
        outs.append(sds((16, 640), BF16))
        ospecs.append(VM)
    no = len(outs)
    aliased = [] if bufs is None else list(bufs)

    def kernel(i, *refs):
        lrefs, refs = refs[:nl], refs[nl:]
        w_ref, s_ref = refs[:2]
        refs = refs[2 + len(aliased) :]
        orefs, refs = refs[:no], refs[no:]
        acc, acc_s, main, small, turned, steps, sem = refs

        acc[...] = jnp.zeros_like(acc)
        acc_s[...] = jnp.zeros_like(acc_s)

        def one(k, carry):
            here = pl.ds(pl.multiple_of(k * kb, kb), kb)
            lhs = jnp.concatenate([r[:, here] for r in lrefs], axis=0)
            acc[...] += dot(lhs, w_ref[here, :])
            acc_s[...] += dot_nt(lhs, s_ref[:, here])
            return carry

        lax.fori_loop(0, depth // kb, one, 0)
        copies = []
        for s in range(count):
            for t in range(8):
                at = slice(s * 128 + t * 16, s * 128 + t * 16 + 16)
                dst = pl.ds(pl.multiple_of(i[4 + t] * 16, 16) + s * 128, 16)
                main[dst, :] = acc[at, :].astype(BF16)
                small[dst, :] = acc_s[at, 0:128].astype(BF16)
                turned[dst, :] = acc_s[at, 128:256]
            here = slice(s * 128, s * 128 + 128)
            steps[:, here] = jnp.transpose(turned[here, :])[0:8, :]
            there = pl.ds(pl.multiple_of(i[slots[s]] * 128, 128), 128)
            for source, target in (
                (main.at[here, :], orefs[0].at[there, :]),
                (small.at[here, :], orefs[1].at[there, :]),
                (steps.at[:, here], orefs[2].at[:, there]),
            ):
                copies.append(pltpu.make_async_copy(source, target, sem.at[len(copies)]))
        for copy in copies:
            copy.start()
        if extra:
            orefs[3][:, 0:512] = acc[rows : rows + 16, :].astype(BF16)
            orefs[3][:, 512:640] = acc_s[rows : rows + 16, 0:128].astype(BF16)
        for copy in copies:
            copy.wait()

    first = 1 + nl + 2
    out = pl.pallas_call(
        kernel,
        out_shape=outs,
        in_specs=[SM] + [VM] * (nl + 2) + [pl.BlockSpec(memory_space=pl.ANY)] * len(aliased),
        out_specs=ospecs,
        scratch_shapes=[
            pltpu.VMEM((rows + extra, 512), F32),
            pltpu.VMEM((rows + extra, 256), F32),
            pltpu.VMEM((rows, 512), BF16),
            pltpu.VMEM((rows, 128), BF16),
            pltpu.VMEM((rows, 128), F32),
            pltpu.VMEM((8, rows), F32),
            pltpu.SemaphoreType.DMA((3 * count,)),
        ],
        input_output_aliases={first + n: n for n in range(len(aliased))},
        compiler_params=pltpu.CompilerParams(vmem_limit_bytes=14 * MIB),
        cost_estimate=cost(2 * rows * depth * 768, 2 * depth * 768),
    )(idx, *lefts, input_w, small_w, *aliased)
    return list(out)


def conv_rows(window, taps, rows):
    running = taps[CONV : CONV + 1, :] + taps[0:1, :] * window[13 : 13 + rows, :]
    for k in range(1, CONV):
        running = running + taps[k : k + 1, :] * window[13 + k : 13 + k + rows, :]
    return silu(running)


def conv_states_kernel(idx, rows_ref, halo_ref, taps_ref, out_ref, full):
    taps = taps_ref[...]
    for k in range(4):
        if k == 0:
            window = jnp.concatenate([halo_ref[:, 512:640], rows_ref[0:128, :]], axis=0).astype(F32)
        else:
            window = rows_ref[128 * k - 16 : 128 * k + 128, :].astype(F32)
        full[128 * k : 128 * k + 128, :] = conv_rows(window, taps, 128).astype(BF16)
    half = idx[13]
    out_ref[...] = full[pl.ds(pl.multiple_of(half * 256, 256), 256), :]


def conv_states(idx, rows, halo, taps):
    return pl.pallas_call(
        conv_states_kernel,
        out_shape=sds((256, 128), BF16),
        in_specs=[SM, VM, VM, VM],
        out_specs=VM,
        scratch_shapes=[pltpu.VMEM((512, 128), BF16)],
        compiler_params=pltpu.CompilerParams(vmem_limit_bytes=14 * MIB),
        cost_estimate=cost(2e6, 4e5),
        name="conv_states",
    )(idx, rows, halo, taps)


def columns_of(rows8):
    return jnp.transpose(rows8)


def column(par, start):
    row = lax.broadcasted_iota(jnp.int32, (8, 128), 0)
    out = jnp.zeros((8, 128), F32)
    for h in range(8):
        out = jnp.where(row == h, par[start + h], out)
    return out


def inputs_kernel(par_ref, rows_ref, halo_ref, taps_ref, step_ref, x_ref, hi_ref, lo_ref, dt_ref, cum_ref, weight_ref, longer):
    taps = taps_ref[...]
    rate = jnp.exp(column(par_ref, 0))
    bias = column(par_ref, 8)
    lane = lax.broadcasted_iota(jnp.int32, (8, 128), 1)
    dts, cums = [], []
    for k in range(4):
        raw = step_ref[:, 128 * k : 128 * k + 128] + bias
        dt = jnp.maximum(raw, 0.0) + jnp.log1p(jnp.exp(-jnp.abs(raw)))
        cum = -dt * rate
        for b in range(7):
            moved = pltpu.roll(cum, 1 << b, 1)
            cum = cum + jnp.where(lane >= (1 << b), moved, 0.0)
        dts.append(dt)
        cums.append(cum)
        dt_ref[:, 128 * k : 128 * k + 128] = dt
        cum_ref[:, 128 * k : 128 * k + 128] = cum
    after = jnp.zeros((8, 1), F32)
    for k in reversed(range(4)):
        total = cums[k][:, 127:128]
        weight_ref[:, 128 * k : 128 * k + 128] = jnp.exp(total - cums[k] + after) * dts[k]
        after = after + total
    longer[0:16, :] = halo_ref[:, 0:512]
    longer[16:528, :] = rows_ref[...]

    def one(k, carry):
        start = pl.multiple_of(k * 128, 128)
        here = pl.ds(start, 128)
        cols = columns_of(weight_ref[:, here])
        window = longer[pl.ds(start, 144), :]
        for p in range(4):
            ch = slice(128 * p, 128 * p + 128)
            x = conv_rows(window[:, ch].astype(F32), taps[:, ch], 128).astype(BF16)
            x_ref[here, ch] = x
            hi, lo = split(x.astype(F32) * pair_scale(cols, p))
            hi_ref[here, ch] = hi
            lo_ref[here, ch] = lo
        return carry

    lax.fori_loop(0, 4, one, 0)


def inputs_stage(rows, halo, taps, step, par):
    return pl.pallas_call(
        inputs_kernel,
        out_shape=[sds((512, 512), BF16)] * 3 + [sds((8, 512), F32)] * 2,
        in_specs=[SM] + [VM] * 4,
        out_specs=[VM] * 5,
        scratch_shapes=[pltpu.VMEM((8, 512), F32), pltpu.VMEM((528, 512), BF16)],
        compiler_params=pltpu.CompilerParams(vmem_limit_bytes=14 * MIB),
        cost_estimate=cost(1e7, 2e6),
        name="inputs_stage",
    )(par, rows, halo, taps, step)


def gathered_block(idx, own_ref, oth_ref, block, rows):
    place = lax.bitwise_xor(jnp.int32(block), idx[12])
    return jnp.where(idx[13] == rows, own_ref[place], oth_ref[place])


LOG2 = 0.6931471805599453


def scaled(value):
    most = jnp.max(jnp.abs(value), axis=0, keepdims=True)
    power = jnp.ceil(jnp.log(most) * (1.0 / LOG2))
    power = jnp.minimum(jnp.maximum(power, -100.0), 120.0)
    return value * jnp.exp(power * -LOG2), power


def unscaled(ref_value):
    return ref_value[0:256, :] * jnp.exp(ref_value[256:257, :] * LOG2)


def state_kernel(idx, own_ref, oth_ref, hi_ref, lo_ref, cum_ref, out_ref):
    halves = []
    for n in range(2):
        write = jnp.concatenate(
            [gathered_block(idx, own_ref, oth_ref, n, 0), gathered_block(idx, own_ref, oth_ref, n, 1)], axis=0
        )
        halves.append(write)
    write = jnp.concatenate(halves, axis=1)
    state = dot_tn(write, hi_ref[...]) + dot_tn(write, lo_ref[...])
    total = (
        cum_ref[:, 127:128] + cum_ref[:, 255:256] + cum_ref[:, 383:384] + cum_ref[:, 511:512]
    )
    damp = jnp.maximum(total, -110.0) * 256.0
    lane = lax.broadcasted_iota(jnp.int32, (16, 128), 1)
    row = lax.broadcasted_iota(jnp.int32, (16, 128), 0)
    for q in range(4):
        place = lax.bitwise_xor(jnp.int32(q), idx[14])
        mant, power = scaled(state[:, 128 * q : 128 * q + 128])
        out_ref[place, 0:256, :] = mant
        low = jnp.broadcast_to(damp[2 * q : 2 * q + 1, :], (16, 128))
        high = jnp.broadcast_to(damp[2 * q + 1 : 2 * q + 2, :], (16, 128))
        value = jnp.where(lane < 64, low, high)
        one = value.astype(BF16).astype(F32)
        two = (value - one).astype(BF16).astype(F32)
        three = value - one - two
        packed = jnp.where(row == 1, one, jnp.where(row == 2, two, jnp.where(row == 3, three, 0.0)))
        out_ref[place, 256:272, :] = jnp.where(row == 0, power, packed)


def state_stage(idx, own, oth, hi, lo, cum):
    return pl.pallas_call(
        state_kernel,
        out_shape=sds((4, 272, 128), F32),
        in_specs=[SM] + [VM] * 5,
        out_specs=VM,
        compiler_params=pltpu.CompilerParams(vmem_limit_bytes=14 * MIB),
        cost_estimate=cost(2.7e8, 2e6),
        name="state_stage",
    )(idx, own, oth, hi, lo, cum)


def prefix_kernel(idx, s0, s1, s2, s3, inc_ref, pre_ref, tot_ref):
    place = idx[14]
    odd = lax.bitwise_and(place, 1) == 1
    far = lax.bitwise_and(place, 2) == 2
    slots = [s0[...], s1[...], s2[...], s3[...]]
    a, b = jnp.where(odd, slots[1], slots[0]), jnp.where(odd, slots[0], slots[1])
    c, d = jnp.where(odd, slots[3], slots[2]), jnp.where(odd, slots[2], slots[3])
    ordered = [jnp.where(far, c, a), jnp.where(far, d, b), jnp.where(far, a, c), jnp.where(far, b, d)]
    running = jnp.zeros((256, 128), F32)
    carried = jnp.ones((1, 128), F32)
    for k in range(4):
        inc_ref[k] = running
        pre_ref[k] = jnp.broadcast_to(carried, (8, 128))
        tail = ordered[k][256:272, :]
        damp = jnp.exp((tail[1:2, :] + tail[2:3, :] + tail[3:4, :]) * (1.0 / 256.0))
        running = damp * running + unscaled(ordered[k])
        carried = carried * damp
    mant, power = scaled(running)
    tot_ref[0:256, :] = mant
    tot_ref[256:272, :] = jnp.broadcast_to(power, (16, 128))


def prefix_stage(idx, s0, s1, s2, s3):
    return pl.pallas_call(
        prefix_kernel,
        out_shape=[sds((4, 256, 128), F32), sds((4, 8, 128), F32), sds((272, 128), F32)],
        in_specs=[SM] + [VM] * 4,
        out_specs=[VM] * 3,
        compiler_params=pltpu.CompilerParams(vmem_limit_bytes=14 * MIB),
        cost_estimate=cost(1e6, 1e6),
        name="prefix_stage",
    )(idx, s0, s1, s2, s3)


def spread_kernel(idx, inc_ref, pre_ref, far_ref, out_ref):
    far = jnp.where(idx[15] > 0, unscaled(far_ref[...]), 0.0)
    for k in range(4):
        place = lax.bitwise_xor(jnp.int32(k), idx[14])
        mant, power = scaled(inc_ref[k] + pre_ref[k][0:1, :] * far)
        out_ref[place, 0:256, :] = mant
        out_ref[place, 256:272, :] = jnp.broadcast_to(power, (16, 128))


def spread_stage(idx, inc, pre, far):
    return pl.pallas_call(
        spread_kernel,
        out_shape=sds((4, 272, 128), F32),
        in_specs=[SM] + [VM] * 3,
        out_specs=VM,
        compiler_params=pltpu.CompilerParams(vmem_limit_bytes=14 * MIB),
        cost_estimate=cost(1e6, 1e6),
        name="spread_stage",
    )(idx, inc, pre, far)


def scan_kernel(idx, par_ref, own_ref, oth_ref, x_ref, dt_ref, cum_ref, y_ref, read_ref, state):
    row = lax.broadcasted_iota(jnp.int32, (128, 128), 0)
    col = lax.broadcasted_iota(jnp.int32, (128, 128), 1)
    causal = row >= col
    left = col < 64
    zero = jnp.zeros((128, 128), BF16)
    state[...] = jnp.zeros_like(state)

    def one(k, carry):
        here = pl.ds(pl.multiple_of(k * 128, 128), 128)
        half = lax.div(k, 2)
        sub = pl.ds(pl.multiple_of(lax.rem(k, 2) * 128, 128), 128)

        def part(block):
            place = lax.bitwise_xor(jnp.int32(block), idx[12])
            return jnp.where(idx[13] == half, own_ref[place, sub, :], oth_ref[place, sub, :])

        write = jnp.concatenate([part(0), part(1)], axis=1)
        read = jnp.concatenate([part(2), part(3)], axis=1)
        read_ref[here, :] = read
        scores = dot_nt(read, write)
        cum = cum_ref[:, here]
        dt = dt_ref[:, here]
        cols = columns_of(cum)
        exp_cols = columns_of(jnp.exp(cum))
        total = cum[:, 127:128]
        end_cols = columns_of(jnp.exp(total - cum) * dt)
        damp = jnp.exp(total)
        for p in range(4):
            ch = slice(128 * p, 128 * p + 128)
            x = x_ref[here, ch]
            xf = x.astype(F32)
            mixes = []
            for h in (2 * p, 2 * p + 1):
                gap = jnp.broadcast_to(cols[:, h : h + 1], (128, 128)) - cum[h : h + 1, :]
                damping = jnp.exp(jnp.where(causal, gap, -jnp.inf))
                mixes.append(scores * damping * dt[h : h + 1, :])
            mix = jnp.concatenate(mixes, axis=1)
            both = jnp.concatenate([jnp.where(left, x, zero), jnp.where(left, zero, x)], axis=0)
            mix_hi, mix_lo = split(mix)
            y = dot(mix_hi, both) + dot(mix_lo, both)
            y = y + jnp.where(left[0:1, :], par_ref[16 + 2 * p], par_ref[17 + 2 * p]) * xf
            before = state[:, ch]
            s_hi, s_lo = split(before)
            y_ref[here, ch] = y + pair_scale(exp_cols, p) * (dot(read, s_hi) + dot(read, s_lo))
            in_hi, in_lo = split(xf * pair_scale(end_cols, p))
            keep = jnp.where(
                left[0:1, :],
                jnp.broadcast_to(damp[2 * p : 2 * p + 1, :], (1, 128)),
                jnp.broadcast_to(damp[2 * p + 1 : 2 * p + 2, :], (1, 128)),
            )
            state[:, ch] = keep * before + dot_tn(write, in_hi) + dot_tn(write, in_lo)
        return carry

    lax.fori_loop(0, 4, one, 0)


def scan_stage(idx, own, oth, x, dt, cum, par):
    return pl.pallas_call(
        scan_kernel,
        out_shape=[sds((512, 512), F32), sds((512, 256), BF16)],
        in_specs=[SM] * 2 + [VM] * 5,
        out_specs=[VM] * 2,
        scratch_shapes=[pltpu.VMEM((256, 512), F32)],
        compiler_params=pltpu.CompilerParams(vmem_limit_bytes=14 * MIB),
        cost_estimate=cost(6e9, 3e6),
        name="scan_stage",
    )(idx, par, own, oth, x, dt, cum)


def gate_kernel(idx, y_ref, read_ref, q0, q1, q2, q3, cum_ref, gate_ref, u_ref, ss_ref):
    place = idx[14]
    odd = lax.bitwise_and(place, 1) == 1
    far = lax.bitwise_and(place, 2) == 2
    slots = [q0[...], q1[...], q2[...], q3[...]]
    a, b = jnp.where(odd, slots[1], slots[0]), jnp.where(odd, slots[0], slots[1])
    c, d = jnp.where(odd, slots[3], slots[2]), jnp.where(odd, slots[2], slots[3])
    ordered = [jnp.where(far, c, a), jnp.where(far, d, b), jnp.where(far, a, c), jnp.where(far, b, d)]
    halves = [split(unscaled(v)) for v in ordered]

    def one(k, before):
        here = pl.ds(pl.multiple_of(k * 128, 128), 128)
        cum = cum_ref[:, here]
        cols = columns_of(jnp.exp(cum + before))
        read = read_ref[here, :]
        squares = jnp.zeros((128, 128), F32)
        for p in range(4):
            ch = slice(128 * p, 128 * p + 128)
            carried = dot(read, halves[p][0]) + dot(read, halves[p][1])
            y = y_ref[here, ch] + pair_scale(cols, p) * carried
            u = y * silu(gate_ref[here, ch].astype(F32))
            u_ref[here, ch] = u
            squares = squares + u * u
        ss_ref[pl.ds(k, 1), :] = jnp.sum(jnp.transpose(squares), axis=0, keepdims=True)
        return before + cum[:, 127:128]

    lax.fori_loop(0, 4, one, jnp.zeros((8, 1), F32))


def gate_stage(idx, y, read, quarters, cum, gate):
    return pl.pallas_call(
        gate_kernel,
        out_shape=[sds((512, 512), F32), sds((4, 128), F32)],
        in_specs=[SM] + [VM] * 8,
        out_specs=[VM] * 2,
        compiler_params=pltpu.CompilerParams(vmem_limit_bytes=14 * MIB),
        cost_estimate=cost(2e8, 3e6),
        name="gate_stage",
    )(idx, y, read, *quarters, cum, gate)


def load_kernel(src_ref, dst_ref, sem):
    copy = pltpu.make_async_copy(src_ref, dst_ref, sem)
    copy.start()
    copy.wait()


def load(array):
    return pl.pallas_call(
        load_kernel,
        out_shape=sds(array.shape, array.dtype),
        in_specs=[pl.BlockSpec(memory_space=pltpu.HBM)],
        out_specs=VM,
        scratch_shapes=[pltpu.SemaphoreType.DMA],
        compiler_params=pltpu.CompilerParams(vmem_limit_bytes=8 * MIB),
        cost_estimate=cost(1, 8 * MIB),
        name="load",
    )(array)


def out_block(idx, slots, u, ss, gain, out_w):
    count = len(slots)
    rows = 64 * count

    def kernel(i, u_ref, ss_ref, gain_ref, w_ref, own_ref, oth_ref, lhs):
        for s in range(count):
            place = i[slots[s]]
            mean = ss_ref[pl.ds(place, 1), :] / (DINNER // GROUPS)
            scale = jnp.transpose(jnp.broadcast_to(lax.rsqrt(mean + 1e-05), (128, 128)))
            here = pl.ds(pl.multiple_of(place * 128, 128), 128)
            for p in range(4):
                ch = slice(128 * p, 128 * p + 128)
                normed = (u_ref[here, ch] * scale * gain_ref[:, ch]).astype(BF16)
                for t in range(8):
                    core, tile = t % 2, t // 2
                    at = lax.bitwise_xor(jnp.int32(core), i[13]) * rows + 64 * s + tile * 16
                    lhs[pl.ds(pl.multiple_of(at, 16), 16), ch] = normed[t * 16 : t * 16 + 16, :]

        def one(n, carry):
            here = pl.ds(pl.multiple_of(n * 1024, 1024), 1024)
            part = dot(lhs[...], w_ref[:, here])
            own_ref[:, here] = part[0:rows, :]
            oth_ref[:, here] = part[rows : 2 * rows, :]
            return carry

        lax.fori_loop(0, 4, one, 0)

    return pl.pallas_call(
        kernel,
        out_shape=[sds((rows, 4096), F32)] * 2,
        in_specs=[SM] + [VM] * 4,
        out_specs=[VM] * 2,
        scratch_shapes=[pltpu.VMEM((2 * rows, 512), BF16)],
        compiler_params=pltpu.CompilerParams(vmem_limit_bytes=20 * MIB),
        cost_estimate=cost(4 * rows * 512 * 4096, 6e6),
        name="out_block",
    )(idx, u, ss, gain, out_w)


def body(
    tokens,
    gate_weight,
    input_weight,
    state_weight,
    step_weight,
    input_conv,
    state_conv,
    log_rate,
    step_bias,
    skip_gain,
    norm_gain,
    out_weight,
):
    me = lax.axis_index("tp")
    x, zl, core = me // 8, (me // 2) % 4, me % 2
    y, later = lax.axis_index("ctx") % 4, lax.axis_index("ctx") // 4
    n = jnp.arange(16, dtype=jnp.int32)
    turn = jnp.where(n == 1, 3, jnp.where(n == 2, 1, jnp.where(n == 3, 2, 0)))
    tile = n - 4
    where = jnp.bitwise_xor(tile % 4, zl) * 2 + jnp.bitwise_xor(tile // 4, core)
    idx = jnp.where(n < 4, (x + turn) % 4, where)
    idx = jnp.where(n == 12, zl, jnp.where(n == 13, core, jnp.where(n == 14, y, jnp.where(n == 15, later, idx))))
    idx = idx.astype(jnp.int32)

    state_rows_w = state_weight.T
    state_pair = flip(state_rows_w, "tp", 1)
    taps_pair = flip(state_conv, "tp", 1)
    low = core == 0
    first = jnp.where(low, state_rows_w, state_pair)
    second = jnp.where(low, state_pair, state_rows_w)
    small_w = jnp.concatenate([first, second, step_weight.T, jnp.zeros((120, tokens.shape[1]), BF16)], axis=0)
    state_taps = jnp.concatenate(
        [jnp.where(low, state_conv, taps_pair), jnp.where(low, taps_pair, state_conv)], axis=1
    )
    par = jnp.concatenate([log_rate, step_bias, skip_gain])

    tiles = [tokens] + [flip(tokens, "tp", 2 * s) for s in (1, 2, 3)]
    mine = jnp.concatenate(tiles, axis=0)
    right = along_x(mine, 1)
    left = along_x(mine, -1)
    mine_other = flip(mine, "tp", 1)
    last = lax.dynamic_index_in_dim(mine.reshape(4, 16, mine.shape[1]), 3 - zl, 0, False)[8:]
    before_all = {"h0": lambda c, t: (c + 1, t) if c < 7 and t >= 24 and t % 2 else None}
    before_all["hc"] = lambda c, t: (c, t - 1) if t >= 24 and t % 2 else None
    before_all["h1"] = lambda c, t: (c, t - 24) if t >= 24 else None
    before_all["h2"] = lambda c, t: (c, t - 8) if t >= 24 else ((c, t + 8) if t < 8 else None)
    rim = hop(last, before_all["h0"])
    bufs = project_resident([mine, mine_other], None, [0], idx, input_weight, small_w, None)
    rim = rim + hop(rim, before_all["hc"])
    right, left, rim = lax.optimization_barrier((right, left, rim))
    rim = rim + hop(rim, before_all["h1"])
    far_a = along_x(right[:32], 1)
    far_b = along_x(left[32:], -1)
    right_other = flip(right, "tp", 1)
    left_other = flip(left, "tp", 1)
    rim = rim + hop(rim, before_all["h2"])
    bufs = project_resident(
        [right, right_other, left, left_other], None, [1, 2], idx, input_weight, small_w, bufs
    )
    rim = jnp.concatenate([jnp.zeros_like(rim), rim], axis=0)
    far_a_other = flip(far_a, "tp", 1)
    far_b_other = flip(far_b, "tp", 1)
    fars = [far_a, far_b, far_a_other, far_b_other]
    input_rows, state_rows, step_raw, halo = project_resident(
        fars, rim, [3], idx, input_weight, small_w, bufs
    )

    piece = conv_states(idx, state_rows, halo, state_taps)
    pieces = jnp.stack([piece] + [flip(piece, "tp", 2 * s) for s in (1, 2, 3)])
    pieces_other = flip(pieces, "tp", 1)

    xs, x_hi, x_lo, dt, cum = inputs_stage(input_rows, halo, input_conv, step_raw, par)
    payload = state_stage(idx, pieces, pieces_other, x_hi, x_lo, cum)
    ends = [payload[0]] + [half_flip(payload[s], s) for s in (1, 2, 3)]
    y_local, read_vec = scan_stage(idx, pieces, pieces_other, xs, dt, cum, par)
    inc, pre, total = prefix_stage(idx, *ends)
    before = half_flip(total, 4)
    everything = [mine, mine_other, right, right_other, left, left_other] + fars
    (gate_rows,) = project(everything, [0, 1, 2, 3], idx, gate_weight, None, None, None)
    spread = spread_stage(idx, inc, pre, before)
    quarters = [spread[0]] + [half_flip(spread[s], s) for s in (1, 2, 3)]
    u, squares = gate_stage(idx, y_local, read_vec, quarters, cum, gate_rows)

    squares = squares + flip(squares, "tp", 1)
    squares = squares + flip(squares, "tp", 2)
    squares = squares + flip(squares, "tp", 4)

    gain = norm_gain.reshape(1, 512)
    out_w = load(out_weight)
    far_own, far_oth = out_block(idx, [3], u, squares, gain, out_w)
    far_sum = swap_add(far_own, far_oth)
    got_a = along_x(narrow(far_sum[:32]), 1)
    got_b = along_x(narrow(far_sum[32:]), -1)
    rest_own, rest_oth = out_block(idx, [2, 1, 0], u, squares, gain, out_w)
    rest = swap_add(rest_own, rest_oth)
    ahead_sum, behind_sum, mine_sum = rest[:64], rest[64:128], rest[128:]
    half = out_w.shape[1] // 2
    outs = []
    moved = []
    for n in range(2):
        cols = slice(n * half, n * half + half)
        to_right = narrow(
            jnp.concatenate([ahead_sum[:32, cols] + widen(got_a[:, cols]), ahead_sum[32:, cols]], axis=0)
        )
        to_left = narrow(
            jnp.concatenate([behind_sum[:32, cols], behind_sum[32:, cols] + widen(got_b[:, cols])], axis=0)
        )
        from_left = along_x(to_right, 1)
        from_right = along_x(to_left, -1)
        moved.append((mine_sum[:, cols], from_left, from_right))
    for n in range(2):
        own, from_left, from_right = moved[n]

        def tile_sum(place):
            at = place * 16
            return (
                lax.dynamic_slice_in_dim(own, at, 16, 0)
                + widen(lax.dynamic_slice_in_dim(from_left, at, 16, 0))
                + widen(lax.dynamic_slice_in_dim(from_right, at, 16, 0))
            )

        out = tile_sum(zl)
        for p in (1, 2, 3):
            part = narrow(tile_sum(jnp.bitwise_xor(zl, p)))
            part = flip(part, "tp", 2 * p)
            out = out + widen(part)
        outs.append(out.astype(BF16))
    return jnp.concatenate(outs, axis=1)


def half_flip(value, mask):
    return flip(value.astype(F16), "ctx", mask).astype(F32)


def narrow(value):
    return (value * 32.0).astype(F16)


def widen(value):
    return value.astype(F32) * 0.03125


def swap_add(own, other):
    return own + widen(flip(narrow(other), "tp", 1))


def solution(mesh):
    placed = (
        P(("ctx", "tp"), None),
        P(None, "tp"),
        P(None, "tp"),
        P(None, "tp"),
        P(None, "tp"),
        P(None, "tp"),
        P(None, "tp"),
        P("tp"),
        P("tp"),
        P("tp"),
        P("tp"),
        P("tp", None),
    )

    return jax.shard_map(
        body, mesh=mesh, in_specs=placed, out_specs=P(("ctx", "tp"), None), check_vma=False
    )
```

```python
import jax
import jax.numpy as jnp
from jax import lax
from jax.experimental import pallas as pl
from jax.experimental.pallas import tpu as pltpu
from jax.sharding import PartitionSpec as P


GROUPS = 4
CONV = 4
DINNER = 16384
F32 = jnp.float32
BF16 = jnp.bfloat16
F16 = jnp.float16
MIB = 1024 * 1024


VM = pl.BlockSpec(memory_space=pltpu.VMEM)
SM = pl.BlockSpec(memory_space=pltpu.SMEM)


def sds(shape, dtype):
    return jax.ShapeDtypeStruct(shape, dtype)


def cost(flops, nbytes):
    return pl.CostEstimate(flops=int(flops), bytes_accessed=int(nbytes), transcendentals=0)


def send(array, axis, to):
    size = lax.axis_size(axis)
    pairs = [(i, to(i)) for i in range(size) if to(i) is not None]
    return lax.ppermute(array, axis, pairs)


def hop(array, to):
    pairs = [(c * 32 + t, to(c, t)) for c in range(8) for t in range(32)]
    pairs = [(i, d[0] * 32 + d[1]) for i, d in pairs if d is not None]
    return lax.ppermute(array, ("ctx", "tp"), pairs)


def flip(array, axis, mask):
    return send(array, axis, lambda i: i ^ mask)


def along_x(array, by):
    return send(array, "tp", lambda i: (i + 8 * by) % 32)


def dot(a, b):
    return lax.dot_general(a, b, (((1,), (0,)), ((), ())), preferred_element_type=F32)


def dot_nt(a, b):
    return lax.dot_general(a, b, (((1,), (1,)), ((), ())), preferred_element_type=F32)


def dot_tn(a, b):
    return lax.dot_general(a, b, (((0,), (0,)), ((), ())), preferred_element_type=F32)


def silu(v):
    return v * jax.nn.sigmoid(v)


def pair_scale(cols, pair):
    rows = cols.shape[0]
    lane = lax.broadcasted_iota(jnp.int32, (rows, 128), 1)
    low = jnp.broadcast_to(cols[:, 2 * pair : 2 * pair + 1], (rows, 128))
    high = jnp.broadcast_to(cols[:, 2 * pair + 1 : 2 * pair + 2], (rows, 128))
    return jnp.where(lane < 64, low, high)


def split(value):
    high = value.astype(BF16)
    return high, (value - high.astype(F32)).astype(BF16)


def project(parts, slots, idx, gate_w, input_w, small_w, bufs):
    depth = parts[0][0].shape[1]
    steps = 4
    kb = depth // steps
    count = len(slots)
    rows = 128 * count
    weights, wspecs, outs, accs = [], [], [], []
    if gate_w is not None:
        weights.append(gate_w)
        wspecs.append(pl.BlockSpec((kb, 512), lambda k, i: (k, 0)))
        outs.append(sds((512, 512), BF16))
        accs.append(pltpu.VMEM((rows, 512), F32))
    if input_w is not None:
        weights += [input_w, small_w]
        wspecs += [
            pl.BlockSpec((kb, 512), lambda k, i: (k, 0)),
            pl.BlockSpec((256, kb), lambda k, i: (0, k)),
        ]
        outs += [sds((512, 512), BF16), sds((512, 128), BF16), sds((8, 512), F32)]
        accs += [pltpu.VMEM((rows, 512), F32), pltpu.VMEM((rows, 256), F32)]
    nw, no, na = len(weights), len(outs), len(accs)
    aliased = [] if bufs is None else list(bufs)
    ready = [pltpu.VMEM((rows, 512), BF16)] if gate_w is not None else []
    if input_w is not None:
        ready += [pltpu.VMEM((rows, 512), BF16), pltpu.VMEM((rows, 128), BF16), pltpu.VMEM((8, rows), F32)]
        ready += [pltpu.VMEM((rows, 128), F32)]
    nl = len(parts)

    def kernel(i, *refs):
        lrefs, refs = refs[:nl], refs[nl:]
        wrefs, refs = refs[:nw], refs[nw + len(aliased) :]
        orefs, refs = refs[:no], refs[no:]
        arefs, refs = refs[:na], refs[na:]
        rrefs, sem = refs[:-1], refs[-1]
        k = pl.program_id(0)
        lhs = jnp.concatenate([r[...] for r in lrefs], axis=0)
        for n, w in enumerate(wrefs):
            nt = input_w is not None and n == nw - 1
            part = dot_nt(lhs, w[...]) if nt else dot(lhs, w[...])

            @pl.when(k == 0)
            def _():
                arefs[n][...] = part

            @pl.when(k > 0)
            def _():
                arefs[n][...] += part

        @pl.when(k == steps - 1)
        def _():
            copies = []
            for s in range(count):
                for t in range(8):
                    at = slice(s * 128 + t * 16, s * 128 + t * 16 + 16)
                    dst = pl.ds(pl.multiple_of(i[4 + t] * 16, 16) + s * 128, 16)
                    n = 0
                    if gate_w is not None:
                        rrefs[n][dst, :] = arefs[n][at, :].astype(BF16)
                        n += 1
                    if input_w is not None:
                        rrefs[n][dst, :] = arefs[n][at, :].astype(BF16)
                        rrefs[n + 1][dst, :] = arefs[n + 1][at, 0:128].astype(BF16)
                        rrefs[n + 3][dst, :] = arefs[n + 1][at, 128:256]
                here = slice(s * 128, s * 128 + 128)
                if input_w is not None:
                    rrefs[n + 2][:, here] = jnp.transpose(rrefs[n + 3][here, :])[0:8, :]
                there = pl.ds(pl.multiple_of(i[slots[s]] * 128, 128), 128)
                for n in range(no):
                    if n == no - 1 and input_w is not None:
                        source, target = rrefs[n].at[:, here], orefs[n].at[:, there]
                    else:
                        source, target = rrefs[n].at[here, :], orefs[n].at[there, :]
                    copies.append(pltpu.make_async_copy(source, target, sem.at[len(copies)]))
            for copy in copies:
                copy.start()
            for copy in copies:
                copy.wait()

    cols = (512 if gate_w is not None else 0) + (768 if input_w is not None else 0)
    first = 1 + nl + nw
    lspecs = [pl.BlockSpec((32, kb), lambda k, i, b=b: (b, k)) for _, b in parts]
    out = pl.pallas_call(
        kernel,
        out_shape=outs,
        grid_spec=pltpu.PrefetchScalarGridSpec(
            num_scalar_prefetch=1,
            grid=(steps,),
            in_specs=lspecs + wspecs + [pl.BlockSpec(memory_space=pl.ANY)] * len(aliased),
            out_specs=[pl.BlockSpec(memory_space=pl.ANY)] * no,
            scratch_shapes=accs + ready + [pltpu.SemaphoreType.DMA((no * count,))],
        ),
        input_output_aliases={first + n: n for n in range(len(aliased))},
        compiler_params=pltpu.CompilerParams(vmem_limit_bytes=14 * MIB),
        cost_estimate=cost(2 * rows * depth * cols, 2 * depth * cols),
    )(idx, *[p for p, _ in parts], *weights, *aliased)
    return list(out)


def project_resident(parts, halo, slots, idx, input_w, small_w, bufs):
    depth = parts[0][0].shape[1]
    kb = 512
    count = len(slots)
    rows = 128 * count
    extra = 0 if halo is None else 16
    lefts, pieces = [], []
    for array, block in list(parts):
        known = [n for n, seen in enumerate(lefts) if seen is array]
        if not known:
            lefts.append(array)
        pieces.append((known[0] if known else len(lefts) - 1, slice(block * 32, block * 32 + 32)))
    if halo is not None:
        lefts.append(halo)
        pieces.append((len(lefts) - 1, slice(0, 16)))
    nl = len(lefts)
    outs = [sds((512, 512), BF16), sds((512, 128), BF16), sds((8, 512), F32)]
    ospecs = [pl.BlockSpec(memory_space=pl.ANY)] * 3
    if extra:
        outs.append(sds((16, 640), BF16))
        ospecs.append(VM)
    no = len(outs)
    aliased = [] if bufs is None else list(bufs)

    def kernel(i, *refs):
        lrefs, refs = refs[:nl], refs[nl:]
        w_ref, s_ref = refs[:2]
        refs = refs[2 + len(aliased) :]
        orefs, refs = refs[:no], refs[no:]
        acc, acc_s, main, small, turned, steps, sem = refs

        acc[...] = jnp.zeros_like(acc)
        acc_s[...] = jnp.zeros_like(acc_s)

        def one(k, carry):
            here = pl.ds(pl.multiple_of(k * kb, kb), kb)
            lhs = jnp.concatenate([lrefs[n][rows_of, here] for n, rows_of in pieces], axis=0)
            acc[...] += dot(lhs, w_ref[here, :])
            acc_s[...] += dot_nt(lhs, s_ref[:, here])
            return carry

        lax.fori_loop(0, depth // kb, one, 0)
        copies = []
        for s in range(count):
            for t in range(8):
                at = slice(s * 128 + t * 16, s * 128 + t * 16 + 16)
                dst = pl.ds(pl.multiple_of(i[4 + t] * 16, 16) + s * 128, 16)
                main[dst, :] = acc[at, :].astype(BF16)
                small[dst, :] = acc_s[at, 0:128].astype(BF16)
                turned[dst, :] = acc_s[at, 128:256]
            here = slice(s * 128, s * 128 + 128)
            steps[:, here] = jnp.transpose(turned[here, :])[0:8, :]
            there = pl.ds(pl.multiple_of(i[slots[s]] * 128, 128), 128)
            for source, target in (
                (main.at[here, :], orefs[0].at[there, :]),
                (small.at[here, :], orefs[1].at[there, :]),
                (steps.at[:, here], orefs[2].at[:, there]),
            ):
                copies.append(pltpu.make_async_copy(source, target, sem.at[len(copies)]))
        for copy in copies:
            copy.start()
        if extra:
            orefs[3][:, 0:512] = acc[rows : rows + 16, :].astype(BF16)
            orefs[3][:, 512:640] = acc_s[rows : rows + 16, 0:128].astype(BF16)
        for copy in copies:
            copy.wait()

    first = 1 + nl + 2
    out = pl.pallas_call(
        kernel,
        out_shape=outs,
        in_specs=[SM] + [VM] * (nl + 2) + [pl.BlockSpec(memory_space=pl.ANY)] * len(aliased),
        out_specs=ospecs,
        scratch_shapes=[
            pltpu.VMEM((rows + extra, 512), F32),
            pltpu.VMEM((rows + extra, 256), F32),
            pltpu.VMEM((rows, 512), BF16),
            pltpu.VMEM((rows, 128), BF16),
            pltpu.VMEM((rows, 128), F32),
            pltpu.VMEM((8, rows), F32),
            pltpu.SemaphoreType.DMA((3 * count,)),
        ],
        input_output_aliases={first + n: n for n in range(len(aliased))},
        compiler_params=pltpu.CompilerParams(vmem_limit_bytes=14 * MIB),
        cost_estimate=cost(2 * rows * depth * 768, 2 * depth * 768),
    )(idx, *lefts, input_w, small_w, *aliased)
    return list(out)


def conv_rows(window, taps, rows):
    running = taps[CONV : CONV + 1, :] + taps[0:1, :] * window[13 : 13 + rows, :]
    for k in range(1, CONV):
        running = running + taps[k : k + 1, :] * window[13 + k : 13 + k + rows, :]
    return silu(running)


def conv_states_kernel(idx, rows_ref, halo_ref, taps_ref, out_ref, full):
    taps = taps_ref[...]
    for k in range(4):
        if k == 0:
            window = jnp.concatenate([halo_ref[:, 512:640], rows_ref[0:128, :]], axis=0).astype(F32)
        else:
            window = rows_ref[128 * k - 16 : 128 * k + 128, :].astype(F32)
        full[128 * k : 128 * k + 128, :] = conv_rows(window, taps, 128).astype(BF16)
    half = idx[13]
    out_ref[...] = full[pl.ds(pl.multiple_of(half * 256, 256), 256), :]


def conv_states(idx, rows, halo, taps):
    return pl.pallas_call(
        conv_states_kernel,
        out_shape=sds((256, 128), BF16),
        in_specs=[SM, VM, VM, VM],
        out_specs=VM,
        scratch_shapes=[pltpu.VMEM((512, 128), BF16)],
        compiler_params=pltpu.CompilerParams(vmem_limit_bytes=14 * MIB),
        cost_estimate=cost(2e6, 4e5),
        name="conv_states",
    )(idx, rows, halo, taps)


def columns_of(rows8):
    return jnp.transpose(rows8)


def column(par, start):
    row = lax.broadcasted_iota(jnp.int32, (8, 128), 0)
    out = jnp.zeros((8, 128), F32)
    for h in range(8):
        out = jnp.where(row == h, par[start + h], out)
    return out


def inputs_kernel(par_ref, rows_ref, halo_ref, taps_ref, step_ref, x_ref, hi_ref, lo_ref, dt_ref, cum_ref, weight_ref, longer):
    taps = taps_ref[...]
    rate = jnp.exp(column(par_ref, 0))
    bias = column(par_ref, 8)
    lane = lax.broadcasted_iota(jnp.int32, (8, 128), 1)
    dts, cums = [], []
    for k in range(4):
        raw = step_ref[:, 128 * k : 128 * k + 128] + bias
        dt = jnp.maximum(raw, 0.0) + jnp.log1p(jnp.exp(-jnp.abs(raw)))
        cum = -dt * rate
        for b in range(7):
            moved = pltpu.roll(cum, 1 << b, 1)
            cum = cum + jnp.where(lane >= (1 << b), moved, 0.0)
        dts.append(dt)
        cums.append(cum)
        dt_ref[:, 128 * k : 128 * k + 128] = dt
        cum_ref[:, 128 * k : 128 * k + 128] = cum
    after = jnp.zeros((8, 1), F32)
    for k in reversed(range(4)):
        total = cums[k][:, 127:128]
        weight_ref[:, 128 * k : 128 * k + 128] = jnp.exp(total - cums[k] + after) * dts[k]
        after = after + total
    longer[0:16, :] = halo_ref[:, 0:512]
    longer[16:528, :] = rows_ref[...]

    def one(k, carry):
        start = pl.multiple_of(k * 128, 128)
        here = pl.ds(start, 128)
        cols = columns_of(weight_ref[:, here])
        window = longer[pl.ds(start, 144), :]
        for p in range(4):
            ch = slice(128 * p, 128 * p + 128)
            x = conv_rows(window[:, ch].astype(F32), taps[:, ch], 128).astype(BF16)
            x_ref[here, ch] = x
            hi, lo = split(x.astype(F32) * pair_scale(cols, p))
            hi_ref[here, ch] = hi
            lo_ref[here, ch] = lo
        return carry

    lax.fori_loop(0, 4, one, 0)


def inputs_stage(rows, halo, taps, step, par):
    return pl.pallas_call(
        inputs_kernel,
        out_shape=[sds((512, 512), BF16)] * 3 + [sds((8, 512), F32)] * 2,
        in_specs=[SM] + [VM] * 4,
        out_specs=[VM] * 5,
        scratch_shapes=[pltpu.VMEM((8, 512), F32), pltpu.VMEM((528, 512), BF16)],
        compiler_params=pltpu.CompilerParams(vmem_limit_bytes=14 * MIB),
        cost_estimate=cost(1e7, 2e6),
        name="inputs_stage",
    )(par, rows, halo, taps, step)


def gathered_block(idx, own_ref, oth_ref, block, rows):
    place = lax.bitwise_xor(jnp.int32(block), idx[12])
    return jnp.where(idx[13] == rows, own_ref[place], oth_ref[place])


LOG2 = 0.6931471805599453


def scaled(value):
    most = jnp.max(jnp.abs(value), axis=0, keepdims=True)
    power = jnp.ceil(jnp.log(most) * (1.0 / LOG2))
    power = jnp.minimum(jnp.maximum(power, -100.0), 120.0)
    return value * jnp.exp(power * -LOG2), power


def unscaled(ref_value):
    return ref_value[0:256, :] * jnp.exp(ref_value[256:257, :] * LOG2)


def state_kernel(idx, own_ref, oth_ref, hi_ref, lo_ref, cum_ref, out_ref):
    halves = []
    for n in range(2):
        write = jnp.concatenate(
            [gathered_block(idx, own_ref, oth_ref, n, 0), gathered_block(idx, own_ref, oth_ref, n, 1)], axis=0
        )
        halves.append(write)
    write = jnp.concatenate(halves, axis=1)
    state = dot_tn(write, hi_ref[...]) + dot_tn(write, lo_ref[...])
    total = (
        cum_ref[:, 127:128] + cum_ref[:, 255:256] + cum_ref[:, 383:384] + cum_ref[:, 511:512]
    )
    damp = jnp.maximum(total, -110.0) * 256.0
    lane = lax.broadcasted_iota(jnp.int32, (16, 128), 1)
    row = lax.broadcasted_iota(jnp.int32, (16, 128), 0)
    for q in range(4):
        place = lax.bitwise_xor(jnp.int32(q), idx[14])
        mant, power = scaled(state[:, 128 * q : 128 * q + 128])
        out_ref[place, 0:256, :] = mant
        low = jnp.broadcast_to(damp[2 * q : 2 * q + 1, :], (16, 128))
        high = jnp.broadcast_to(damp[2 * q + 1 : 2 * q + 2, :], (16, 128))
        value = jnp.where(lane < 64, low, high)
        one = value.astype(BF16).astype(F32)
        two = (value - one).astype(BF16).astype(F32)
        three = value - one - two
        packed = jnp.where(row == 1, one, jnp.where(row == 2, two, jnp.where(row == 3, three, 0.0)))
        out_ref[place, 256:272, :] = jnp.where(row == 0, power, packed)


def state_stage(idx, own, oth, hi, lo, cum):
    return pl.pallas_call(
        state_kernel,
        out_shape=sds((4, 272, 128), F32),
        in_specs=[SM] + [VM] * 5,
        out_specs=VM,
        compiler_params=pltpu.CompilerParams(vmem_limit_bytes=14 * MIB),
        cost_estimate=cost(2.7e8, 2e6),
        name="state_stage",
    )(idx, own, oth, hi, lo, cum)


def prefix_kernel(idx, s0, s1, s2, s3, inc_ref, pre_ref, tot_ref):
    place = idx[14]
    odd = lax.bitwise_and(place, 1) == 1
    far = lax.bitwise_and(place, 2) == 2
    slots = [s0[...], s1[...], s2[...], s3[...]]
    a, b = jnp.where(odd, slots[1], slots[0]), jnp.where(odd, slots[0], slots[1])
    c, d = jnp.where(odd, slots[3], slots[2]), jnp.where(odd, slots[2], slots[3])
    ordered = [jnp.where(far, c, a), jnp.where(far, d, b), jnp.where(far, a, c), jnp.where(far, b, d)]
    running = jnp.zeros((256, 128), F32)
    carried = jnp.ones((1, 128), F32)
    for k in range(4):
        inc_ref[k] = running
        pre_ref[k] = jnp.broadcast_to(carried, (8, 128))
        tail = ordered[k][256:272, :]
        damp = jnp.exp((tail[1:2, :] + tail[2:3, :] + tail[3:4, :]) * (1.0 / 256.0))
        running = damp * running + unscaled(ordered[k])
        carried = carried * damp
    mant, power = scaled(running)
    tot_ref[0:256, :] = mant
    tot_ref[256:272, :] = jnp.broadcast_to(power, (16, 128))


def prefix_stage(idx, s0, s1, s2, s3):
    return pl.pallas_call(
        prefix_kernel,
        out_shape=[sds((4, 256, 128), F32), sds((4, 8, 128), F32), sds((272, 128), F32)],
        in_specs=[SM] + [VM] * 4,
        out_specs=[VM] * 3,
        compiler_params=pltpu.CompilerParams(vmem_limit_bytes=14 * MIB),
        cost_estimate=cost(1e6, 1e6),
        name="prefix_stage",
    )(idx, s0, s1, s2, s3)


def spread_kernel(idx, inc_ref, pre_ref, far_ref, out_ref):
    far = jnp.where(idx[15] > 0, unscaled(far_ref[...]), 0.0)
    for k in range(4):
        place = lax.bitwise_xor(jnp.int32(k), idx[14])
        mant, power = scaled(inc_ref[k] + pre_ref[k][0:1, :] * far)
        out_ref[place, 0:256, :] = mant
        out_ref[place, 256:272, :] = jnp.broadcast_to(power, (16, 128))


def spread_stage(idx, inc, pre, far):
    return pl.pallas_call(
        spread_kernel,
        out_shape=sds((4, 272, 128), F32),
        in_specs=[SM] + [VM] * 3,
        out_specs=VM,
        compiler_params=pltpu.CompilerParams(vmem_limit_bytes=14 * MIB),
        cost_estimate=cost(1e6, 1e6),
        name="spread_stage",
    )(idx, inc, pre, far)


def scan_kernel(idx, par_ref, own_ref, oth_ref, x_ref, dt_ref, cum_ref, y_ref, read_ref, state):
    row = lax.broadcasted_iota(jnp.int32, (128, 128), 0)
    col = lax.broadcasted_iota(jnp.int32, (128, 128), 1)
    causal = row >= col
    left = col < 64
    zero = jnp.zeros((128, 128), BF16)
    state[...] = jnp.zeros_like(state)

    def one(k, carry):
        here = pl.ds(pl.multiple_of(k * 128, 128), 128)
        half = lax.div(k, 2)
        sub = pl.ds(pl.multiple_of(lax.rem(k, 2) * 128, 128), 128)

        def part(block):
            place = lax.bitwise_xor(jnp.int32(block), idx[12])
            return jnp.where(idx[13] == half, own_ref[place, sub, :], oth_ref[place, sub, :])

        write = jnp.concatenate([part(0), part(1)], axis=1)
        read = jnp.concatenate([part(2), part(3)], axis=1)
        read_ref[here, :] = read
        scores = dot_nt(read, write)
        cum = cum_ref[:, here]
        dt = dt_ref[:, here]
        cols = columns_of(cum)
        exp_cols = columns_of(jnp.exp(cum))
        total = cum[:, 127:128]
        end_cols = columns_of(jnp.exp(total - cum) * dt)
        damp = jnp.exp(total)
        for p in range(4):
            ch = slice(128 * p, 128 * p + 128)
            x = x_ref[here, ch]
            xf = x.astype(F32)
            mixes = []
            for h in (2 * p, 2 * p + 1):
                gap = jnp.broadcast_to(cols[:, h : h + 1], (128, 128)) - cum[h : h + 1, :]
                damping = jnp.exp(jnp.where(causal, gap, -jnp.inf))
                mixes.append(scores * damping * dt[h : h + 1, :])
            mix = jnp.concatenate(mixes, axis=1)
            both = jnp.concatenate([jnp.where(left, x, zero), jnp.where(left, zero, x)], axis=0)
            mix_hi, mix_lo = split(mix)
            y = dot(mix_hi, both) + dot(mix_lo, both)
            y = y + jnp.where(left[0:1, :], par_ref[16 + 2 * p], par_ref[17 + 2 * p]) * xf
            before = state[:, ch]
            s_hi, s_lo = split(before)
            y_ref[here, ch] = y + pair_scale(exp_cols, p) * (dot(read, s_hi) + dot(read, s_lo))
            in_hi, in_lo = split(xf * pair_scale(end_cols, p))
            keep = jnp.where(
                left[0:1, :],
                jnp.broadcast_to(damp[2 * p : 2 * p + 1, :], (1, 128)),
                jnp.broadcast_to(damp[2 * p + 1 : 2 * p + 2, :], (1, 128)),
            )
            state[:, ch] = keep * before + dot_tn(write, in_hi) + dot_tn(write, in_lo)
        return carry

    lax.fori_loop(0, 4, one, 0)


def scan_stage(idx, own, oth, x, dt, cum, par):
    return pl.pallas_call(
        scan_kernel,
        out_shape=[sds((512, 512), F32), sds((512, 256), BF16)],
        in_specs=[SM] * 2 + [VM] * 5,
        out_specs=[VM] * 2,
        scratch_shapes=[pltpu.VMEM((256, 512), F32)],
        compiler_params=pltpu.CompilerParams(vmem_limit_bytes=14 * MIB),
        cost_estimate=cost(6e9, 3e6),
        name="scan_stage",
    )(idx, par, own, oth, x, dt, cum)


def gate_kernel(idx, y_ref, read_ref, q0, q1, q2, q3, cum_ref, gate_ref, u_ref, ss_ref):
    place = idx[14]
    odd = lax.bitwise_and(place, 1) == 1
    far = lax.bitwise_and(place, 2) == 2
    slots = [q0[...], q1[...], q2[...], q3[...]]
    a, b = jnp.where(odd, slots[1], slots[0]), jnp.where(odd, slots[0], slots[1])
    c, d = jnp.where(odd, slots[3], slots[2]), jnp.where(odd, slots[2], slots[3])
    ordered = [jnp.where(far, c, a), jnp.where(far, d, b), jnp.where(far, a, c), jnp.where(far, b, d)]
    halves = [split(unscaled(v)) for v in ordered]

    def one(k, before):
        here = pl.ds(pl.multiple_of(k * 128, 128), 128)
        cum = cum_ref[:, here]
        cols = columns_of(jnp.exp(cum + before))
        read = read_ref[here, :]
        squares = jnp.zeros((128, 128), F32)
        for p in range(4):
            ch = slice(128 * p, 128 * p + 128)
            carried = dot(read, halves[p][0]) + dot(read, halves[p][1])
            y = y_ref[here, ch] + pair_scale(cols, p) * carried
            u = y * silu(gate_ref[here, ch].astype(F32))
            u_ref[here, ch] = u
            squares = squares + u * u
        ss_ref[pl.ds(k, 1), :] = jnp.sum(jnp.transpose(squares), axis=0, keepdims=True)
        return before + cum[:, 127:128]

    lax.fori_loop(0, 4, one, jnp.zeros((8, 1), F32), unroll=1)


def gate_stage(idx, y, read, quarters, cum, gate):
    return pl.pallas_call(
        gate_kernel,
        out_shape=[sds((512, 512), F32), sds((4, 128), F32)],
        in_specs=[SM] + [VM] * 8,
        out_specs=[VM] * 2,
        compiler_params=pltpu.CompilerParams(vmem_limit_bytes=14 * MIB),
        cost_estimate=cost(2e8, 3e6),
        name="gate_stage",
    )(idx, y, read, *quarters, cum, gate)


def load_kernel(src_ref, dst_ref, sem):
    copy = pltpu.make_async_copy(src_ref, dst_ref, sem)
    copy.start()
    copy.wait()


def load(array):
    return pl.pallas_call(
        load_kernel,
        out_shape=sds(array.shape, array.dtype),
        in_specs=[pl.BlockSpec(memory_space=pltpu.HBM)],
        out_specs=VM,
        scratch_shapes=[pltpu.SemaphoreType.DMA],
        compiler_params=pltpu.CompilerParams(vmem_limit_bytes=8 * MIB),
        cost_estimate=cost(1, 8 * MIB),
        name="load",
    )(array)


def out_block(idx, slots, u, ss, gain, out_w):
    count = len(slots)
    rows = 64 * count

    def kernel(i, u_ref, ss_ref, gain_ref, w_ref, own_ref, oth_ref, lhs):
        for s in range(count):
            place = i[slots[s]]
            mean = ss_ref[pl.ds(place, 1), :] / (DINNER // GROUPS)
            scale = jnp.transpose(jnp.broadcast_to(lax.rsqrt(mean + 1e-05), (128, 128)))
            here = pl.ds(pl.multiple_of(place * 128, 128), 128)
            for p in range(4):
                ch = slice(128 * p, 128 * p + 128)
                normed = (u_ref[here, ch] * scale * gain_ref[:, ch]).astype(BF16)
                for t in range(8):
                    core, tile = t % 2, t // 2
                    at = lax.bitwise_xor(jnp.int32(core), i[13]) * rows + 64 * s + tile * 16
                    lhs[pl.ds(pl.multiple_of(at, 16), 16), ch] = normed[t * 16 : t * 16 + 16, :]

        def one(n, carry):
            here = pl.ds(pl.multiple_of(n * 512, 512), 512)
            part = dot(lhs[...], w_ref[:, here])
            own_ref[:, here] = part[0:rows, :]
            oth_ref[:, here] = part[rows : 2 * rows, :].astype(BF16)
            return carry

        lax.fori_loop(0, 8, one, 0)

    return pl.pallas_call(
        kernel,
        out_shape=[sds((rows, 4096), F32), sds((rows, 4096), BF16)],
        in_specs=[SM] + [VM] * 4,
        out_specs=[VM] * 2,
        scratch_shapes=[pltpu.VMEM((2 * rows, 512), BF16)],
        compiler_params=pltpu.CompilerParams(vmem_limit_bytes=20 * MIB),
        cost_estimate=cost(4 * rows * 512 * 4096, 6e6),
        name="out_block",
    )(idx, u, ss, gain, out_w)


def body(
    tokens,
    gate_weight,
    input_weight,
    state_weight,
    step_weight,
    input_conv,
    state_conv,
    log_rate,
    step_bias,
    skip_gain,
    norm_gain,
    out_weight,
):
    me = lax.axis_index("tp")
    x, zl, core = me // 8, (me // 2) % 4, me % 2
    y, later = lax.axis_index("ctx") % 4, lax.axis_index("ctx") // 4
    n = jnp.arange(16, dtype=jnp.int32)
    turn = jnp.where(n == 1, 3, jnp.where(n == 2, 1, jnp.where(n == 3, 2, 0)))
    tile = n - 4
    where = jnp.bitwise_xor(tile % 4, zl) * 2 + jnp.bitwise_xor(tile // 4, core)
    idx = jnp.where(n < 4, (x + turn) % 4, where)
    idx = jnp.where(n == 12, zl, jnp.where(n == 13, core, jnp.where(n == 14, y, jnp.where(n == 15, later, idx))))
    idx = idx.astype(jnp.int32)

    state_rows_w = state_weight.T
    state_pair = flip(state_rows_w, "tp", 1)
    taps_pair = flip(state_conv, "tp", 1)
    low = core == 0
    first = jnp.where(low, state_rows_w, state_pair)
    second = jnp.where(low, state_pair, state_rows_w)
    small_w = jnp.concatenate([first, second, step_weight.T, jnp.zeros((120, tokens.shape[1]), BF16)], axis=0)
    state_taps = jnp.concatenate(
        [jnp.where(low, state_conv, taps_pair), jnp.where(low, taps_pair, state_conv)], axis=1
    )
    par = jnp.concatenate([log_rate, step_bias, skip_gain])

    tiles = [tokens, flip(tokens, "tp", 2)]
    tiles.append(flip(tokens, "tp", 4))
    tiles.append(flip(tokens, "tp", 6))
    part1 = jnp.concatenate(tiles[:2], axis=0)
    right1 = along_x(part1, 1)
    left1 = along_x(part1, -1)
    other1 = flip(part1, "tp", 1)
    late, other1 = lax.optimization_barrier((tiles[2:], other1))
    part2 = jnp.concatenate(late, axis=0)
    right2 = along_x(part2, 1)
    left2 = along_x(part2, -1)
    other2 = flip(part2, "tp", 1)
    own_parts = [(part1, 0), (part2, 0), (other1, 0), (other2, 0)]
    last = tiles[0][8:]
    for s in (1, 2, 3):
        last = jnp.where(zl == 3 - s, tiles[s][8:], last)
    to = {
        "h0": lambda c, t: (c + 1, t) if c < 7 and t >= 24 and t % 2 else None,
        "hc": lambda c, t: (c, t - 1) if t >= 24 and t % 2 else None,
        "h1": lambda c, t: (c, t - 24) if t >= 24 else None,
        "h2": lambda c, t: (c, t - 8) if t >= 24 else ((c, t + 8) if t < 8 else None),
    }
    rim = hop(last, to["h0"])
    bufs = project_resident(own_parts, None, [0], idx, input_weight, small_w, None)
    far_a = along_x(right1, 1)
    side1 = flip(jnp.concatenate([right1, left1], axis=0), "tp", 1)
    rim = rim + hop(rim, to["hc"])
    rim = rim + hop(rim, to["h1"])
    left2, rim = lax.optimization_barrier((left2, rim))
    far_b = along_x(left2, -1)
    side2 = flip(jnp.concatenate([right2, left2], axis=0), "tp", 1)
    rim = rim + hop(rim, to["h2"])
    rights = [(right1, 0), (right2, 0), (side1, 0), (side2, 0)]
    lefts = [(left1, 0), (left2, 0), (side1, 1), (side2, 1)]
    bufs = project_resident(rights + lefts, None, [1, 2], idx, input_weight, small_w, bufs)
    rim = jnp.concatenate([jnp.zeros_like(rim), rim], axis=0)
    far_a_other = flip(far_a, "tp", 1)
    far_b_other = flip(far_b, "tp", 1)
    fars = [(far_a, 0), (far_b, 0), (far_a_other, 0), (far_b_other, 0)]
    input_rows, state_rows, step_raw, halo = project_resident(
        fars, rim, [3], idx, input_weight, small_w, bufs
    )

    piece = conv_states(idx, state_rows, halo, state_taps)
    pieces = jnp.stack([piece] + [flip(piece, "tp", 2 * s) for s in (1, 2, 3)])
    pieces_other = flip(pieces, "tp", 1)

    xs, x_hi, x_lo, dt, cum = inputs_stage(input_rows, halo, input_conv, step_raw, par)
    payload = state_stage(idx, pieces, pieces_other, x_hi, x_lo, cum)
    ends = [payload[0]] + [half_flip(payload[s], s) for s in (1, 2, 3)]
    y_local, read_vec = scan_stage(idx, pieces, pieces_other, xs, dt, cum, par)
    inc, pre, total = prefix_stage(idx, *ends)
    before = half_flip(total, 4)
    everything = own_parts + rights + lefts + fars
    (gate_rows,) = project(everything, [0, 1, 2, 3], idx, gate_weight, None, None, None)
    spread = spread_stage(idx, inc, pre, before)
    quarters = [spread[0]] + [half_flip(spread[s], s) for s in (1, 2, 3)]
    u, squares = gate_stage(idx, y_local, read_vec, quarters, cum, gate_rows)

    squares = squares + flip(squares, "tp", 1)
    squares = squares + flip(squares, "tp", 2)
    squares = squares + flip(squares, "tp", 4)

    gain = norm_gain.reshape(1, 512)
    out_w = load(out_weight)
    far_own, far_oth = out_block(idx, [3], u, squares, gain, out_w)
    far_sum = far_own + flip(far_oth, "tp", 1).astype(F32)
    got_a = along_x(narrow(far_sum[:32]), 1)
    got_b = along_x(narrow(far_sum[32:]), -1)
    rest_own, rest_oth = out_block(idx, [2, 1, 0], u, squares, gain, out_w)
    rest_got = flip(rest_oth, "tp", 1)
    half = out_w.shape[1] // 2
    outs = []
    moved = []
    for n in range(2):
        cols = slice(n * half, n * half + half)

        def rest_sum(rows):
            return rest_own[rows, cols] + rest_got[rows, cols].astype(F32)

        to_right = narrow(rest_sum(slice(0, 64)) + jnp.pad(widen(got_a[:, cols]), ((0, 32), (0, 0))))
        to_left = narrow(rest_sum(slice(64, 128)) + jnp.pad(widen(got_b[:, cols]), ((32, 0), (0, 0))))
        from_left = along_x(to_right, 1)
        from_right = along_x(to_left, -1)
        moved.append((rest_sum(slice(128, 192)), from_left, from_right))
    for n in range(2):
        own, from_left, from_right = moved[n]

        def tile_sum(place):
            at = place * 16
            return (
                lax.dynamic_slice_in_dim(own, at, 16, 0)
                + widen(lax.dynamic_slice_in_dim(from_left, at, 16, 0))
                + widen(lax.dynamic_slice_in_dim(from_right, at, 16, 0))
            )

        out = tile_sum(zl)
        for p in (1, 2, 3):
            part = narrow(tile_sum(jnp.bitwise_xor(zl, p)))
            part = flip(part, "tp", 2 * p)
            out = out + widen(part)
        outs.append(out.astype(BF16))
    return jnp.concatenate(outs, axis=1)


def half_flip(value, mask):
    return flip(value.astype(F16), "ctx", mask).astype(F32)


def narrow(value):
    return (value * 32.0).astype(F16)


def widen(value):
    return value.astype(F32) * 0.03125


def solution(mesh):
    placed = (
        P(("ctx", "tp"), None),
        P(None, "tp"),
        P(None, "tp"),
        P(None, "tp"),
        P(None, "tp"),
        P(None, "tp"),
        P(None, "tp"),
        P("tp"),
        P("tp"),
        P("tp"),
        P("tp"),
        P("tp", None),
    )

    return jax.shard_map(
        body, mesh=mesh, in_specs=placed, out_specs=P(("ctx", "tp"), None), check_vma=False
    )
```

```python
import jax
import jax.numpy as jnp
from jax import lax
from jax.experimental import pallas as pl
from jax.experimental.pallas import tpu as pltpu
from jax.sharding import PartitionSpec as P


GROUPS = 4
CONV = 4
DINNER = 16384
F32 = jnp.float32
BF16 = jnp.bfloat16
F16 = jnp.float16
MIB = 1024 * 1024


VM = pl.BlockSpec(memory_space=pltpu.VMEM)
SM = pl.BlockSpec(memory_space=pltpu.SMEM)


def sds(shape, dtype):
    return jax.ShapeDtypeStruct(shape, dtype)


def cost(flops, nbytes):
    return pl.CostEstimate(flops=int(flops), bytes_accessed=int(nbytes), transcendentals=0)


def send(array, axis, to):
    size = lax.axis_size(axis)
    pairs = [(i, to(i)) for i in range(size) if to(i) is not None]
    return lax.ppermute(array, axis, pairs)


def hop(array, to):
    pairs = [(c * 32 + t, to(c, t)) for c in range(8) for t in range(32)]
    pairs = [(i, d[0] * 32 + d[1]) for i, d in pairs if d is not None]
    return lax.ppermute(array, ("ctx", "tp"), pairs)


def flip(array, axis, mask):
    return send(array, axis, lambda i: i ^ mask)


def along_x(array, by):
    return send(array, "tp", lambda i: (i + 8 * by) % 32)


def dot(a, b):
    return lax.dot_general(a, b, (((1,), (0,)), ((), ())), preferred_element_type=F32)


def dot_nt(a, b):
    return lax.dot_general(a, b, (((1,), (1,)), ((), ())), preferred_element_type=F32)


def dot_tn(a, b):
    return lax.dot_general(a, b, (((0,), (0,)), ((), ())), preferred_element_type=F32)


def silu(v):
    return v * jax.nn.sigmoid(v)


def pair_scale(cols, pair):
    rows = cols.shape[0]
    lane = lax.broadcasted_iota(jnp.int32, (rows, 128), 1)
    low = jnp.broadcast_to(cols[:, 2 * pair : 2 * pair + 1], (rows, 128))
    high = jnp.broadcast_to(cols[:, 2 * pair + 1 : 2 * pair + 2], (rows, 128))
    return jnp.where(lane < 64, low, high)


def split(value):
    high = value.astype(BF16)
    return high, (value - high.astype(F32)).astype(BF16)


def project(parts, slots, idx, gate_w, input_w, small_w, bufs):
    depth = parts[0][0].shape[1]
    steps = 4
    kb = depth // steps
    count = len(slots)
    rows = 128 * count
    weights, wspecs, outs, accs = [], [], [], []
    if gate_w is not None:
        weights.append(gate_w)
        wspecs.append(pl.BlockSpec((kb, 512), lambda k, i: (k, 0)))
        outs.append(sds((512, 512), BF16))
        accs.append(pltpu.VMEM((rows, 512), F32))
    if input_w is not None:
        weights += [input_w, small_w]
        wspecs += [
            pl.BlockSpec((kb, 512), lambda k, i: (k, 0)),
            pl.BlockSpec((256, kb), lambda k, i: (0, k)),
        ]
        outs += [sds((512, 512), BF16), sds((512, 128), BF16), sds((8, 512), F32)]
        accs += [pltpu.VMEM((rows, 512), F32), pltpu.VMEM((rows, 256), F32)]
    nw, no, na = len(weights), len(outs), len(accs)
    aliased = [] if bufs is None else list(bufs)
    ready = [pltpu.VMEM((rows, 512), BF16)] if gate_w is not None else []
    if input_w is not None:
        ready += [pltpu.VMEM((rows, 512), BF16), pltpu.VMEM((rows, 128), BF16), pltpu.VMEM((8, rows), F32)]
        ready += [pltpu.VMEM((rows, 128), F32)]
    nl = len(parts)

    def kernel(i, *refs):
        lrefs, refs = refs[:nl], refs[nl:]
        wrefs, refs = refs[:nw], refs[nw + len(aliased) :]
        orefs, refs = refs[:no], refs[no:]
        arefs, refs = refs[:na], refs[na:]
        rrefs, sem = refs[:-1], refs[-1]
        k = pl.program_id(0)
        lhs = jnp.concatenate([r[...] for r in lrefs], axis=0)
        for n, w in enumerate(wrefs):
            nt = input_w is not None and n == nw - 1
            part = dot_nt(lhs, w[...]) if nt else dot(lhs, w[...])

            @pl.when(k == 0)
            def _():
                arefs[n][...] = part

            @pl.when(k > 0)
            def _():
                arefs[n][...] += part

        @pl.when(k == steps - 1)
        def _():
            copies = []
            for s in range(count):
                for t in range(8):
                    at = slice(s * 128 + t * 16, s * 128 + t * 16 + 16)
                    dst = pl.ds(pl.multiple_of(i[4 + t] * 16, 16) + s * 128, 16)
                    n = 0
                    if gate_w is not None:
                        rrefs[n][dst, :] = arefs[n][at, :].astype(BF16)
                        n += 1
                    if input_w is not None:
                        rrefs[n][dst, :] = arefs[n][at, :].astype(BF16)
                        rrefs[n + 1][dst, :] = arefs[n + 1][at, 0:128].astype(BF16)
                        rrefs[n + 3][dst, :] = arefs[n + 1][at, 128:256]
                here = slice(s * 128, s * 128 + 128)
                if input_w is not None:
                    rrefs[n + 2][:, here] = jnp.transpose(rrefs[n + 3][here, :])[0:8, :]
                there = pl.ds(pl.multiple_of(i[slots[s]] * 128, 128), 128)
                for n in range(no):
                    if n == no - 1 and input_w is not None:
                        source, target = rrefs[n].at[:, here], orefs[n].at[:, there]
                    else:
                        source, target = rrefs[n].at[here, :], orefs[n].at[there, :]
                    copies.append(pltpu.make_async_copy(source, target, sem.at[len(copies)]))
            for copy in copies:
                copy.start()
            for copy in copies:
                copy.wait()

    cols = (512 if gate_w is not None else 0) + (768 if input_w is not None else 0)
    first = 1 + nl + nw
    lspecs = [pl.BlockSpec((32, kb), lambda k, i, b=b: (b, k)) for _, b in parts]
    out = pl.pallas_call(
        kernel,
        out_shape=outs,
        grid_spec=pltpu.PrefetchScalarGridSpec(
            num_scalar_prefetch=1,
            grid=(steps,),
            in_specs=lspecs + wspecs + [pl.BlockSpec(memory_space=pl.ANY)] * len(aliased),
            out_specs=[pl.BlockSpec(memory_space=pl.ANY)] * no,
            scratch_shapes=accs + ready + [pltpu.SemaphoreType.DMA((no * count,))],
        ),
        input_output_aliases={first + n: n for n in range(len(aliased))},
        compiler_params=pltpu.CompilerParams(vmem_limit_bytes=14 * MIB),
        cost_estimate=cost(2 * rows * depth * cols, 2 * depth * cols),
    )(idx, *[p for p, _ in parts], *weights, *aliased)
    return list(out)


def project_resident(parts, halo, slots, idx, input_w, small_w, bufs):
    depth = parts[0][0].shape[1]
    kb = 1024 if halo is not None else 512
    count = len(slots)
    rows = 128 * count
    extra = 0 if halo is None else 16
    lefts, pieces = [], []
    for array, block in list(parts):
        known = [n for n, seen in enumerate(lefts) if seen is array]
        if not known:
            lefts.append(array)
        pieces.append((known[0] if known else len(lefts) - 1, slice(block * 32, block * 32 + 32)))
    if halo is not None:
        lefts.append(halo)
        pieces.append((len(lefts) - 1, slice(0, 16)))
    nl = len(lefts)
    outs = [sds((512, 512), BF16), sds((512, 128), BF16), sds((8, 512), F32)]
    ospecs = [pl.BlockSpec(memory_space=pl.ANY)] * 3
    if extra:
        outs.append(sds((16, 640), BF16))
        ospecs.append(VM)
    no = len(outs)
    aliased = [] if bufs is None else list(bufs)

    def kernel(i, *refs):
        lrefs, refs = refs[:nl], refs[nl:]
        w_ref, s_ref = refs[:2]
        refs = refs[2 + len(aliased) :]
        orefs, refs = refs[:no], refs[no:]
        acc, acc_s, main, small, turned, steps, sem = refs

        acc[...] = jnp.zeros_like(acc)
        acc_s[...] = jnp.zeros_like(acc_s)

        def one(k, carry):
            here = pl.ds(pl.multiple_of(k * kb, kb), kb)
            lhs = jnp.concatenate([lrefs[n][rows_of, here] for n, rows_of in pieces], axis=0)
            acc[...] += dot(lhs, w_ref[here, :])
            acc_s[...] += dot_nt(lhs, s_ref[:, here])
            return carry

        lax.fori_loop(0, depth // kb, one, 0)
        copies = []
        for s in range(count):
            for t in range(8):
                at = slice(s * 128 + t * 16, s * 128 + t * 16 + 16)
                dst = pl.ds(pl.multiple_of(i[4 + t] * 16, 16) + s * 128, 16)
                main[dst, :] = acc[at, :].astype(BF16)
                small[dst, :] = acc_s[at, 0:128].astype(BF16)
                turned[dst, :] = acc_s[at, 128:256]
            here = slice(s * 128, s * 128 + 128)
            steps[:, here] = jnp.transpose(turned[here, :])[0:8, :]
            there = pl.ds(pl.multiple_of(i[slots[s]] * 128, 128), 128)
            for source, target in (
                (main.at[here, :], orefs[0].at[there, :]),
                (small.at[here, :], orefs[1].at[there, :]),
                (steps.at[:, here], orefs[2].at[:, there]),
            ):
                copies.append(pltpu.make_async_copy(source, target, sem.at[len(copies)]))
        for copy in copies:
            copy.start()
        if extra:
            orefs[3][:, 0:512] = acc[rows : rows + 16, :].astype(BF16)
            orefs[3][:, 512:640] = acc_s[rows : rows + 16, 0:128].astype(BF16)
        for copy in copies:
            copy.wait()

    first = 1 + nl + 2
    out = pl.pallas_call(
        kernel,
        out_shape=outs,
        in_specs=[SM] + [VM] * (nl + 2) + [pl.BlockSpec(memory_space=pl.ANY)] * len(aliased),
        out_specs=ospecs,
        scratch_shapes=[
            pltpu.VMEM((rows + extra, 512), F32),
            pltpu.VMEM((rows + extra, 256), F32),
            pltpu.VMEM((rows, 512), BF16),
            pltpu.VMEM((rows, 128), BF16),
            pltpu.VMEM((rows, 128), F32),
            pltpu.VMEM((8, rows), F32),
            pltpu.SemaphoreType.DMA((3 * count,)),
        ],
        input_output_aliases={first + n: n for n in range(len(aliased))},
        compiler_params=pltpu.CompilerParams(vmem_limit_bytes=14 * MIB),
        cost_estimate=cost(2 * rows * depth * 768, 2 * depth * 768),
    )(idx, *lefts, input_w, small_w, *aliased)
    return list(out)


def conv_rows(window, taps, rows):
    running = taps[CONV : CONV + 1, :] + taps[0:1, :] * window[13 : 13 + rows, :]
    for k in range(1, CONV):
        running = running + taps[k : k + 1, :] * window[13 + k : 13 + k + rows, :]
    return silu(running)


def conv_states_kernel(idx, rows_ref, halo_ref, taps_ref, out_ref, full):
    taps = taps_ref[...]
    for k in range(4):
        if k == 0:
            window = jnp.concatenate([halo_ref[:, 512:640], rows_ref[0:128, :]], axis=0).astype(F32)
        else:
            window = rows_ref[128 * k - 16 : 128 * k + 128, :].astype(F32)
        full[128 * k : 128 * k + 128, :] = conv_rows(window, taps, 128).astype(BF16)
    half = idx[13]
    out_ref[...] = full[pl.ds(pl.multiple_of(half * 256, 256), 256), :]


def conv_states(idx, rows, halo, taps):
    return pl.pallas_call(
        conv_states_kernel,
        out_shape=sds((256, 128), BF16),
        in_specs=[SM, VM, VM, VM],
        out_specs=VM,
        scratch_shapes=[pltpu.VMEM((512, 128), BF16)],
        compiler_params=pltpu.CompilerParams(vmem_limit_bytes=14 * MIB),
        cost_estimate=cost(2e6, 4e5),
        name="conv_states",
    )(idx, rows, halo, taps)


def columns_of(rows8):
    return jnp.transpose(rows8)


def column(par, start):
    row = lax.broadcasted_iota(jnp.int32, (8, 128), 0)
    out = jnp.zeros((8, 128), F32)
    for h in range(8):
        out = jnp.where(row == h, par[start + h], out)
    return out


def inputs_kernel(par_ref, rows_ref, halo_ref, taps_ref, step_ref, x_ref, hi_ref, lo_ref, dt_ref, cum_ref, weight_ref, longer):
    taps = taps_ref[...]
    rate = jnp.exp(column(par_ref, 0))
    bias = column(par_ref, 8)
    lane = lax.bitwise_and(lax.broadcasted_iota(jnp.int32, (8, 512), 1), 127)
    raw = step_ref[...] + jnp.concatenate([bias] * 4, axis=1)
    dt = jnp.maximum(raw, 0.0) + jnp.log1p(jnp.exp(-jnp.abs(raw)))
    cum = -dt * jnp.concatenate([rate] * 4, axis=1)
    for b in range(7):
        cum = cum + jnp.where(lane >= (1 << b), pltpu.roll(cum, 1 << b, 1), 0.0)
    dt_ref[...] = dt
    cum_ref[...] = cum
    after = jnp.zeros((8, 1), F32)
    gaps = []
    for k in reversed(range(4)):
        total = cum[:, 128 * k + 127 : 128 * k + 128]
        gaps.insert(0, jnp.broadcast_to(total + after, (8, 128)))
        after = after + total
    weight_ref[...] = jnp.exp(jnp.concatenate(gaps, axis=1) - cum) * dt
    longer[0:16, :] = halo_ref[:, 0:512]
    longer[16:528, :] = rows_ref[...]

    def one(k, carry):
        start = pl.multiple_of(k * 128, 128)
        here = pl.ds(start, 128)
        cols = columns_of(weight_ref[:, here])
        window = longer[pl.ds(start, 144), :]
        for p in range(4):
            ch = slice(128 * p, 128 * p + 128)
            x = conv_rows(window[:, ch].astype(F32), taps[:, ch], 128).astype(BF16)
            x_ref[here, ch] = x
            hi, lo = split(x.astype(F32) * pair_scale(cols, p))
            hi_ref[here, ch] = hi
            lo_ref[here, ch] = lo
        return carry

    lax.fori_loop(0, 4, one, 0)


def inputs_stage(rows, halo, taps, step, par):
    return pl.pallas_call(
        inputs_kernel,
        out_shape=[sds((512, 512), BF16)] * 3 + [sds((8, 512), F32)] * 2,
        in_specs=[SM] + [VM] * 4,
        out_specs=[VM] * 5,
        scratch_shapes=[pltpu.VMEM((8, 512), F32), pltpu.VMEM((528, 512), BF16)],
        compiler_params=pltpu.CompilerParams(vmem_limit_bytes=14 * MIB),
        cost_estimate=cost(1e7, 2e6),
        name="inputs_stage",
    )(par, rows, halo, taps, step)


def gathered_block(idx, own_ref, oth_ref, block, rows):
    place = lax.bitwise_xor(jnp.int32(block), idx[12])
    return jnp.where(idx[13] == rows, own_ref[place], oth_ref[place])


LOG2 = 0.6931471805599453


def scaled(value):
    most = jnp.max(jnp.abs(value), axis=0, keepdims=True)
    power = jnp.ceil(jnp.log(most) * (1.0 / LOG2))
    power = jnp.minimum(jnp.maximum(power, -100.0), 120.0)
    return value * jnp.exp(power * -LOG2), power


def unscaled(ref_value):
    return ref_value[0:256, :] * jnp.exp(ref_value[256:257, :] * LOG2)


def state_kernel(idx, own_ref, oth_ref, hi_ref, lo_ref, cum_ref, out_ref):
    halves = []
    for n in range(2):
        write = jnp.concatenate(
            [gathered_block(idx, own_ref, oth_ref, n, 0), gathered_block(idx, own_ref, oth_ref, n, 1)], axis=0
        )
        halves.append(write)
    write = jnp.concatenate(halves, axis=1)
    state = dot_tn(write, hi_ref[...]) + dot_tn(write, lo_ref[...])
    total = (
        cum_ref[:, 127:128] + cum_ref[:, 255:256] + cum_ref[:, 383:384] + cum_ref[:, 511:512]
    )
    damp = jnp.maximum(total, -110.0) * 256.0
    lane = lax.broadcasted_iota(jnp.int32, (16, 128), 1)
    row = lax.broadcasted_iota(jnp.int32, (16, 128), 0)
    for q in range(4):
        place = lax.bitwise_xor(jnp.int32(q), idx[14])
        mant, power = scaled(state[:, 128 * q : 128 * q + 128])
        out_ref[place, 0:256, :] = mant
        low = jnp.broadcast_to(damp[2 * q : 2 * q + 1, :], (16, 128))
        high = jnp.broadcast_to(damp[2 * q + 1 : 2 * q + 2, :], (16, 128))
        value = jnp.where(lane < 64, low, high)
        one = value.astype(BF16).astype(F32)
        two = (value - one).astype(BF16).astype(F32)
        three = value - one - two
        packed = jnp.where(row == 1, one, jnp.where(row == 2, two, jnp.where(row == 3, three, 0.0)))
        out_ref[place, 256:272, :] = jnp.where(row == 0, power, packed)


def state_stage(idx, own, oth, hi, lo, cum):
    return pl.pallas_call(
        state_kernel,
        out_shape=sds((4, 272, 128), F32),
        in_specs=[SM] + [VM] * 5,
        out_specs=VM,
        compiler_params=pltpu.CompilerParams(vmem_limit_bytes=14 * MIB),
        cost_estimate=cost(2.7e8, 2e6),
        name="state_stage",
    )(idx, own, oth, hi, lo, cum)


def prefix_kernel(idx, s0, s1, s2, s3, inc_ref, pre_ref, tot_ref):
    place = idx[14]
    odd = lax.bitwise_and(place, 1) == 1
    far = lax.bitwise_and(place, 2) == 2
    slots = [s0[...], s1[...], s2[...], s3[...]]
    a, b = jnp.where(odd, slots[1], slots[0]), jnp.where(odd, slots[0], slots[1])
    c, d = jnp.where(odd, slots[3], slots[2]), jnp.where(odd, slots[2], slots[3])
    ordered = [jnp.where(far, c, a), jnp.where(far, d, b), jnp.where(far, a, c), jnp.where(far, b, d)]
    running = jnp.zeros((256, 128), F32)
    carried = jnp.ones((1, 128), F32)
    for k in range(4):
        inc_ref[k] = running
        pre_ref[k] = jnp.broadcast_to(carried, (8, 128))
        tail = ordered[k][256:272, :]
        damp = jnp.exp((tail[1:2, :] + tail[2:3, :] + tail[3:4, :]) * (1.0 / 256.0))
        running = damp * running + unscaled(ordered[k])
        carried = carried * damp
    mant, power = scaled(running)
    tot_ref[0:256, :] = mant
    tot_ref[256:272, :] = jnp.broadcast_to(power, (16, 128))


def prefix_stage(idx, s0, s1, s2, s3):
    return pl.pallas_call(
        prefix_kernel,
        out_shape=[sds((4, 256, 128), F32), sds((4, 8, 128), F32), sds((272, 128), F32)],
        in_specs=[SM] + [VM] * 4,
        out_specs=[VM] * 3,
        compiler_params=pltpu.CompilerParams(vmem_limit_bytes=14 * MIB),
        cost_estimate=cost(1e6, 1e6),
        name="prefix_stage",
    )(idx, s0, s1, s2, s3)


def spread_kernel(idx, inc_ref, pre_ref, far_ref, out_ref):
    far = jnp.where(idx[15] > 0, unscaled(far_ref[...]), 0.0)
    for k in range(4):
        place = lax.bitwise_xor(jnp.int32(k), idx[14])
        mant, power = scaled(inc_ref[k] + pre_ref[k][0:1, :] * far)
        out_ref[place, 0:256, :] = mant
        out_ref[place, 256:272, :] = jnp.broadcast_to(power, (16, 128))


def spread_stage(idx, inc, pre, far):
    return pl.pallas_call(
        spread_kernel,
        out_shape=sds((4, 272, 128), F32),
        in_specs=[SM] + [VM] * 3,
        out_specs=VM,
        compiler_params=pltpu.CompilerParams(vmem_limit_bytes=14 * MIB),
        cost_estimate=cost(1e6, 1e6),
        name="spread_stage",
    )(idx, inc, pre, far)


def scan_kernel(idx, par_ref, own_ref, oth_ref, x_ref, dt_ref, cum_ref, y_ref, read_ref, state):
    row = lax.broadcasted_iota(jnp.int32, (128, 128), 0)
    col = lax.broadcasted_iota(jnp.int32, (128, 128), 1)
    causal = row >= col
    left = col < 64
    zero = jnp.zeros((128, 128), BF16)
    state[...] = jnp.zeros_like(state)

    def one(k, carry):
        here = pl.ds(pl.multiple_of(k * 128, 128), 128)
        half = lax.div(k, 2)
        sub = pl.ds(pl.multiple_of(lax.rem(k, 2) * 128, 128), 128)

        def part(block):
            place = lax.bitwise_xor(jnp.int32(block), idx[12])
            return jnp.where(idx[13] == half, own_ref[place, sub, :], oth_ref[place, sub, :])

        write = jnp.concatenate([part(0), part(1)], axis=1)
        read = jnp.concatenate([part(2), part(3)], axis=1)
        read_ref[here, :] = read
        scores = dot_nt(read, write)
        cum = cum_ref[:, here]
        dt = dt_ref[:, here]
        cols = columns_of(cum)
        exp_cols = columns_of(jnp.exp(cum))
        total = cum[:, 127:128]
        end_cols = columns_of(jnp.exp(total - cum) * dt)
        damp = jnp.exp(total)
        for p in range(4):
            ch = slice(128 * p, 128 * p + 128)
            x = x_ref[here, ch]
            xf = x.astype(F32)
            mixes = []
            for h in (2 * p, 2 * p + 1):
                gap = jnp.broadcast_to(cols[:, h : h + 1], (128, 128)) - cum[h : h + 1, :]
                damping = jnp.exp(jnp.where(causal, gap, -jnp.inf))
                mixes.append(scores * damping * dt[h : h + 1, :])
            mix = jnp.concatenate(mixes, axis=1)
            both = jnp.concatenate([jnp.where(left, x, zero), jnp.where(left, zero, x)], axis=0)
            mix_hi, mix_lo = split(mix)
            y = dot(mix_hi, both) + dot(mix_lo, both)
            y = y + jnp.where(left[0:1, :], par_ref[16 + 2 * p], par_ref[17 + 2 * p]) * xf
            before = state[:, ch]
            s_hi, s_lo = split(before)
            y_ref[here, ch] = y + pair_scale(exp_cols, p) * (dot(read, s_hi) + dot(read, s_lo))
            in_hi, in_lo = split(xf * pair_scale(end_cols, p))
            keep = jnp.where(
                left[0:1, :],
                jnp.broadcast_to(damp[2 * p : 2 * p + 1, :], (1, 128)),
                jnp.broadcast_to(damp[2 * p + 1 : 2 * p + 2, :], (1, 128)),
            )
            state[:, ch] = keep * before + dot_tn(write, in_hi) + dot_tn(write, in_lo)
        return carry

    lax.fori_loop(0, 4, one, 0)


def scan_stage(idx, own, oth, x, dt, cum, par):
    return pl.pallas_call(
        scan_kernel,
        out_shape=[sds((512, 512), F32), sds((512, 256), BF16)],
        in_specs=[SM] * 2 + [VM] * 5,
        out_specs=[VM] * 2,
        scratch_shapes=[pltpu.VMEM((256, 512), F32)],
        compiler_params=pltpu.CompilerParams(vmem_limit_bytes=14 * MIB),
        cost_estimate=cost(6e9, 3e6),
        name="scan_stage",
    )(idx, par, own, oth, x, dt, cum)


def gate_kernel(idx, y_ref, read_ref, q0, q1, q2, q3, cum_ref, gate_ref, u_ref, ss_ref):
    place = idx[14]
    odd = lax.bitwise_and(place, 1) == 1
    far = lax.bitwise_and(place, 2) == 2
    slots = [q0[...], q1[...], q2[...], q3[...]]
    a, b = jnp.where(odd, slots[1], slots[0]), jnp.where(odd, slots[0], slots[1])
    c, d = jnp.where(odd, slots[3], slots[2]), jnp.where(odd, slots[2], slots[3])
    ordered = [jnp.where(far, c, a), jnp.where(far, d, b), jnp.where(far, a, c), jnp.where(far, b, d)]
    halves = [split(unscaled(v)) for v in ordered]

    def one(k, before):
        here = pl.ds(pl.multiple_of(k * 128, 128), 128)
        cum = cum_ref[:, here]
        cols = columns_of(jnp.exp(cum + before))
        read = read_ref[here, :]
        squares = jnp.zeros((128, 128), F32)
        for p in range(4):
            ch = slice(128 * p, 128 * p + 128)
            carried = dot(read, halves[p][0]) + dot(read, halves[p][1])
            y = y_ref[here, ch] + pair_scale(cols, p) * carried
            u = y * silu(gate_ref[here, ch].astype(F32))
            u_ref[here, ch] = u
            squares = squares + u * u
        ss_ref[pl.ds(k, 1), :] = jnp.sum(jnp.transpose(squares), axis=0, keepdims=True)
        return before + cum[:, 127:128]

    lax.fori_loop(0, 4, one, jnp.zeros((8, 1), F32), unroll=1)


def gate_stage(idx, y, read, quarters, cum, gate):
    return pl.pallas_call(
        gate_kernel,
        out_shape=[sds((512, 512), F32), sds((4, 128), F32)],
        in_specs=[SM] + [VM] * 8,
        out_specs=[VM] * 2,
        compiler_params=pltpu.CompilerParams(vmem_limit_bytes=14 * MIB),
        cost_estimate=cost(2e8, 3e6),
        name="gate_stage",
    )(idx, y, read, *quarters, cum, gate)


def load_kernel(src_ref, dst_ref, sem):
    copy = pltpu.make_async_copy(src_ref, dst_ref, sem)
    copy.start()
    copy.wait()


def load(array):
    return pl.pallas_call(
        load_kernel,
        out_shape=sds(array.shape, array.dtype),
        in_specs=[pl.BlockSpec(memory_space=pltpu.HBM)],
        out_specs=VM,
        scratch_shapes=[pltpu.SemaphoreType.DMA],
        compiler_params=pltpu.CompilerParams(vmem_limit_bytes=8 * MIB),
        cost_estimate=cost(1, 8 * MIB),
        name="load",
    )(array)


def out_block(idx, slots, u, ss, gain, out_w):
    count = len(slots)
    rows = 64 * count
    wide = 1024 if count == 1 else 512

    def kernel(i, u_ref, ss_ref, gain_ref, w_ref, own_ref, oth_ref, lhs):
        for s in range(count):
            place = i[slots[s]]
            mean = ss_ref[pl.ds(place, 1), :] / (DINNER // GROUPS)
            scale = jnp.transpose(jnp.broadcast_to(lax.rsqrt(mean + 1e-05), (128, 128)))
            here = pl.ds(pl.multiple_of(place * 128, 128), 128)
            for p in range(4):
                ch = slice(128 * p, 128 * p + 128)
                normed = (u_ref[here, ch] * scale * gain_ref[:, ch]).astype(BF16)
                for t in range(8):
                    core, tile = t % 2, t // 2
                    at = lax.bitwise_xor(jnp.int32(core), i[13]) * rows + 64 * s + tile * 16
                    lhs[pl.ds(pl.multiple_of(at, 16), 16), ch] = normed[t * 16 : t * 16 + 16, :]

        def one(n, carry):
            here = pl.ds(pl.multiple_of(n * wide, wide), wide)
            part = dot(lhs[...], w_ref[:, here])
            own_ref[:, here] = part[0:rows, :]
            oth_ref[:, here] = part[rows : 2 * rows, :].astype(BF16)
            return carry

        lax.fori_loop(0, 4096 // wide, one, 0)

    return pl.pallas_call(
        kernel,
        out_shape=[sds((rows, 4096), F32), sds((rows, 4096), BF16)],
        in_specs=[SM] + [VM] * 4,
        out_specs=[VM] * 2,
        scratch_shapes=[pltpu.VMEM((2 * rows, 512), BF16)],
        compiler_params=pltpu.CompilerParams(vmem_limit_bytes=20 * MIB),
        cost_estimate=cost(4 * rows * 512 * 4096, 6e6),
        name="out_block",
    )(idx, u, ss, gain, out_w)


def body(
    tokens,
    gate_weight,
    input_weight,
    state_weight,
    step_weight,
    input_conv,
    state_conv,
    log_rate,
    step_bias,
    skip_gain,
    norm_gain,
    out_weight,
):
    me = lax.axis_index("tp")
    x, zl, core = me // 8, (me // 2) % 4, me % 2
    y, later = lax.axis_index("ctx") % 4, lax.axis_index("ctx") // 4
    n = jnp.arange(16, dtype=jnp.int32)
    turn = jnp.where(n == 1, 3, jnp.where(n == 2, 1, jnp.where(n == 3, 2, 0)))
    tile = n - 4
    where = jnp.bitwise_xor(tile % 4, zl) * 2 + jnp.bitwise_xor(tile // 4, core)
    idx = jnp.where(n < 4, (x + turn) % 4, where)
    idx = jnp.where(n == 12, zl, jnp.where(n == 13, core, jnp.where(n == 14, y, jnp.where(n == 15, later, idx))))
    idx = idx.astype(jnp.int32)

    state_rows_w = state_weight.T
    state_pair = flip(state_rows_w, "tp", 1)
    taps_pair = flip(state_conv, "tp", 1)
    low = core == 0
    first = jnp.where(low, state_rows_w, state_pair)
    second = jnp.where(low, state_pair, state_rows_w)
    small_w = jnp.concatenate([first, second, step_weight.T, jnp.zeros((120, tokens.shape[1]), BF16)], axis=0)
    state_taps = jnp.concatenate(
        [jnp.where(low, state_conv, taps_pair), jnp.where(low, taps_pair, state_conv)], axis=1
    )
    par = jnp.concatenate([log_rate, step_bias, skip_gain])

    tiles = [tokens, flip(tokens, "tp", 2)]
    tiles.append(flip(tokens, "tp", 4))
    tiles.append(flip(tokens, "tp", 6))
    part1 = jnp.concatenate(tiles[:2], axis=0)
    right1 = along_x(part1, 1)
    left1 = along_x(part1, -1)
    other1 = flip(part1, "tp", 1)
    late, other1 = lax.optimization_barrier((tiles[2:], other1))
    part2 = jnp.concatenate(late, axis=0)
    right2 = along_x(part2, 1)
    left2 = along_x(part2, -1)
    other2 = flip(part2, "tp", 1)
    own_parts = [(part1, 0), (part2, 0), (other1, 0), (other2, 0)]
    last = tiles[0][8:]
    for s in (1, 2, 3):
        last = jnp.where(zl == 3 - s, tiles[s][8:], last)
    to = {
        "h0": lambda c, t: (c + 1, t) if c < 7 and t >= 24 and t % 2 else None,
        "hc": lambda c, t: (c, t - 1) if t >= 24 and t % 2 else None,
        "h1": lambda c, t: (c, t - 24) if t >= 24 else None,
        "h2": lambda c, t: (c, t - 8) if t >= 24 else ((c, t + 8) if t < 8 else None),
    }
    rim = hop(last, to["h0"])
    bufs = project_resident(own_parts, None, [0], idx, input_weight, small_w, None)
    far_a = along_x(right1, 1)
    side1 = flip(jnp.concatenate([right1, left1], axis=0), "tp", 1)
    rim = rim + hop(rim, to["hc"])
    rim = rim + hop(rim, to["h1"])
    far_b = along_x(left2, -1)
    side2 = flip(jnp.concatenate([right2, left2], axis=0), "tp", 1)
    rim = rim + hop(rim, to["h2"])
    rights = [(right1, 0), (right2, 0), (side1, 0), (side2, 0)]
    lefts = [(left1, 0), (left2, 0), (side1, 1), (side2, 1)]
    bufs = project_resident(rights + lefts, None, [1, 2], idx, input_weight, small_w, bufs)
    rim = jnp.concatenate([jnp.zeros_like(rim), rim], axis=0)
    far_a_other = flip(far_a, "tp", 1)
    far_b_other = flip(far_b, "tp", 1)
    fars = [(far_a, 0), (far_b, 0), (far_a_other, 0), (far_b_other, 0)]
    input_rows, state_rows, step_raw, halo = project_resident(
        fars, rim, [3], idx, input_weight, small_w, bufs
    )

    piece = conv_states(idx, state_rows, halo, state_taps)
    pieces = jnp.stack([piece] + [flip(piece, "tp", 2 * s) for s in (1, 2, 3)])
    pieces_other = flip(pieces, "tp", 1)

    xs, x_hi, x_lo, dt, cum = inputs_stage(input_rows, halo, input_conv, step_raw, par)
    payload = state_stage(idx, pieces, pieces_other, x_hi, x_lo, cum)
    ends = [payload[0]] + [half_flip(payload[s], s) for s in (1, 2, 3)]
    y_local, read_vec = scan_stage(idx, pieces, pieces_other, xs, dt, cum, par)
    inc, pre, total = prefix_stage(idx, *ends)
    before = half_flip(total, 4)
    everything = own_parts + rights + lefts + fars
    (gate_rows,) = project(everything, [0, 1, 2, 3], idx, gate_weight, None, None, None)
    spread = spread_stage(idx, inc, pre, before)
    quarters = [spread[0]] + [half_flip(spread[s], s) for s in (1, 2, 3)]
    u, squares = gate_stage(idx, y_local, read_vec, quarters, cum, gate_rows)

    squares = squares + flip(squares, "tp", 1)
    squares = squares + flip(squares, "tp", 2)
    squares = squares + flip(squares, "tp", 4)

    gain = norm_gain.reshape(1, 512)
    out_w = load(out_weight)
    far_own, far_oth = out_block(idx, [3], u, squares, gain, out_w)
    far_sum = far_own + flip(far_oth, "tp", 1).astype(F32)
    got_a = along_x(narrow(far_sum[:32]), 1)
    got_b = along_x(narrow(far_sum[32:]), -1)
    rest_own, rest_oth = out_block(idx, [2, 1, 0], u, squares, gain, out_w)
    rest_got = flip(rest_oth, "tp", 1)
    half = out_w.shape[1] // 2
    outs = []
    moved = []
    for n in range(2):
        cols = slice(n * half, n * half + half)

        def rest_sum(rows):
            return rest_own[rows, cols] + rest_got[rows, cols].astype(F32)

        to_right = narrow(rest_sum(slice(0, 64)) + jnp.pad(widen(got_a[:, cols]), ((0, 32), (0, 0))))
        to_left = narrow(rest_sum(slice(64, 128)) + jnp.pad(widen(got_b[:, cols]), ((32, 0), (0, 0))))
        from_left = along_x(to_right, 1)
        from_right = along_x(to_left, -1)
        moved.append((rest_sum(slice(128, 192)), from_left, from_right))
    for n in range(2):
        own, from_left, from_right = moved[n]

        def tile_sum(place):
            at = place * 16
            return (
                lax.dynamic_slice_in_dim(own, at, 16, 0)
                + widen(lax.dynamic_slice_in_dim(from_left, at, 16, 0))
                + widen(lax.dynamic_slice_in_dim(from_right, at, 16, 0))
            )

        out = tile_sum(zl)
        for p in (1, 2, 3):
            part = narrow(tile_sum(jnp.bitwise_xor(zl, p)))
            part = flip(part, "tp", 2 * p)
            out = out + widen(part)
        outs.append(out.astype(BF16))
    return jnp.concatenate(outs, axis=1)


def half_flip(value, mask):
    return flip(value.astype(F16), "ctx", mask).astype(F32)


def narrow(value):
    return (value * 32.0).astype(F16)


def widen(value):
    return value.astype(F32) * 0.03125


def solution(mesh):
    placed = (
        P(("ctx", "tp"), None),
        P(None, "tp"),
        P(None, "tp"),
        P(None, "tp"),
        P(None, "tp"),
        P(None, "tp"),
        P(None, "tp"),
        P("tp"),
        P("tp"),
        P("tp"),
        P("tp"),
        P("tp", None),
    )

    return jax.shard_map(
        body, mesh=mesh, in_specs=placed, out_specs=P(("ctx", "tp"), None), check_vma=False
    )
```

```python
import jax
import jax.numpy as jnp
from jax import lax
from jax.experimental import pallas as pl
from jax.experimental.pallas import tpu as pltpu
from jax.sharding import PartitionSpec as P


GROUPS = 4
CONV = 4
DINNER = 16384
F32 = jnp.float32
BF16 = jnp.bfloat16
F16 = jnp.float16
MIB = 1024 * 1024


VM = pl.BlockSpec(memory_space=pltpu.VMEM)
SM = pl.BlockSpec(memory_space=pltpu.SMEM)


def sds(shape, dtype):
    return jax.ShapeDtypeStruct(shape, dtype)


def cost(flops, nbytes):
    return pl.CostEstimate(flops=int(flops), bytes_accessed=int(nbytes), transcendentals=0)


def send(array, axis, to):
    size = lax.axis_size(axis)
    pairs = [(i, to(i)) for i in range(size) if to(i) is not None]
    return lax.ppermute(array, axis, pairs)


def hop(array, to):
    pairs = [(c * 32 + t, to(c, t)) for c in range(8) for t in range(32)]
    pairs = [(i, d[0] * 32 + d[1]) for i, d in pairs if d is not None]
    return lax.ppermute(array, ("ctx", "tp"), pairs)


def flip(array, axis, mask):
    return send(array, axis, lambda i: i ^ mask)


def along_x(array, by):
    return send(array, "tp", lambda i: (i + 8 * by) % 32)


def dot(a, b):
    return lax.dot_general(a, b, (((1,), (0,)), ((), ())), preferred_element_type=F32)


def dot_nt(a, b):
    return lax.dot_general(a, b, (((1,), (1,)), ((), ())), preferred_element_type=F32)


def dot_tn(a, b):
    return lax.dot_general(a, b, (((0,), (0,)), ((), ())), preferred_element_type=F32)


def silu(v):
    return v * jax.nn.sigmoid(v)


def pair_scale(cols, pair):
    rows = cols.shape[0]
    lane = lax.broadcasted_iota(jnp.int32, (rows, 128), 1)
    low = jnp.broadcast_to(cols[:, 2 * pair : 2 * pair + 1], (rows, 128))
    high = jnp.broadcast_to(cols[:, 2 * pair + 1 : 2 * pair + 2], (rows, 128))
    return jnp.where(lane < 64, low, high)


def split(value):
    high = value.astype(BF16)
    return high, (value - high.astype(F32)).astype(BF16)


def project(parts, slots, idx, gate_w, input_w, small_w, bufs):
    depth = parts[0][0].shape[1]
    steps = 4
    kb = depth // steps
    count = len(slots)
    rows = 128 * count
    weights, wspecs, outs, accs = [], [], [], []
    if gate_w is not None:
        weights.append(gate_w)
        wspecs.append(pl.BlockSpec((kb, 512), lambda k, i: (k, 0)))
        outs.append(sds((512, 512), BF16))
        accs.append(pltpu.VMEM((rows, 512), F32))
    if input_w is not None:
        weights += [input_w, small_w]
        wspecs += [
            pl.BlockSpec((kb, 512), lambda k, i: (k, 0)),
            pl.BlockSpec((256, kb), lambda k, i: (0, k)),
        ]
        outs += [sds((512, 512), BF16), sds((512, 128), BF16), sds((8, 512), F32)]
        accs += [pltpu.VMEM((rows, 512), F32), pltpu.VMEM((rows, 256), F32)]
    nw, no, na = len(weights), len(outs), len(accs)
    aliased = [] if bufs is None else list(bufs)
    ready = [pltpu.VMEM((rows, 512), BF16)] if gate_w is not None else []
    if input_w is not None:
        ready += [pltpu.VMEM((rows, 512), BF16), pltpu.VMEM((rows, 128), BF16), pltpu.VMEM((8, rows), F32)]
        ready += [pltpu.VMEM((rows, 128), F32)]
    nl = len(parts)

    def kernel(i, *refs):
        lrefs, refs = refs[:nl], refs[nl:]
        wrefs, refs = refs[:nw], refs[nw + len(aliased) :]
        orefs, refs = refs[:no], refs[no:]
        arefs, refs = refs[:na], refs[na:]
        rrefs, sem = refs[:-1], refs[-1]
        k = pl.program_id(0)
        lhs = jnp.concatenate([r[...] for r in lrefs], axis=0)
        for n, w in enumerate(wrefs):
            nt = input_w is not None and n == nw - 1
            part = dot_nt(lhs, w[...]) if nt else dot(lhs, w[...])

            @pl.when(k == 0)
            def _():
                arefs[n][...] = part

            @pl.when(k > 0)
            def _():
                arefs[n][...] += part

        @pl.when(k == steps - 1)
        def _():
            copies = []
            for s in range(count):
                for t in range(8):
                    at = slice(s * 128 + t * 16, s * 128 + t * 16 + 16)
                    dst = pl.ds(pl.multiple_of(i[4 + t] * 16, 16) + s * 128, 16)
                    n = 0
                    if gate_w is not None:
                        rrefs[n][dst, :] = arefs[n][at, :].astype(BF16)
                        n += 1
                    if input_w is not None:
                        rrefs[n][dst, :] = arefs[n][at, :].astype(BF16)
                        rrefs[n + 1][dst, :] = arefs[n + 1][at, 0:128].astype(BF16)
                        rrefs[n + 3][dst, :] = arefs[n + 1][at, 128:256]
                here = slice(s * 128, s * 128 + 128)
                if input_w is not None:
                    rrefs[n + 2][:, here] = jnp.transpose(rrefs[n + 3][here, :])[0:8, :]
                there = pl.ds(pl.multiple_of(i[slots[s]] * 128, 128), 128)
                for n in range(no):
                    if n == no - 1 and input_w is not None:
                        source, target = rrefs[n].at[:, here], orefs[n].at[:, there]
                    else:
                        source, target = rrefs[n].at[here, :], orefs[n].at[there, :]
                    copies.append(pltpu.make_async_copy(source, target, sem.at[len(copies)]))
            for copy in copies:
                copy.start()
            for copy in copies:
                copy.wait()

    cols = (512 if gate_w is not None else 0) + (768 if input_w is not None else 0)
    first = 1 + nl + nw
    lspecs = [pl.BlockSpec((32, kb), lambda k, i, b=b: (b, k)) for _, b in parts]
    out = pl.pallas_call(
        kernel,
        out_shape=outs,
        grid_spec=pltpu.PrefetchScalarGridSpec(
            num_scalar_prefetch=1,
            grid=(steps,),
            in_specs=lspecs + wspecs + [pl.BlockSpec(memory_space=pl.ANY)] * len(aliased),
            out_specs=[pl.BlockSpec(memory_space=pl.ANY)] * no,
            scratch_shapes=accs + ready + [pltpu.SemaphoreType.DMA((no * count,))],
        ),
        input_output_aliases={first + n: n for n in range(len(aliased))},
        compiler_params=pltpu.CompilerParams(vmem_limit_bytes=14 * MIB),
        cost_estimate=cost(2 * rows * depth * cols, 2 * depth * cols),
    )(idx, *[p for p, _ in parts], *weights, *aliased)
    return list(out)


def project_resident(parts, halo, slots, idx, input_w, small_w, bufs):
    depth = parts[0][0].shape[1]
    kb = 1024 if halo is not None else 512
    count = len(slots)
    rows = 128 * count
    extra = 0 if halo is None else 16
    lefts, pieces = [], []
    for array, block in list(parts):
        known = [n for n, seen in enumerate(lefts) if seen is array]
        if not known:
            lefts.append(array)
        pieces.append((known[0] if known else len(lefts) - 1, slice(block * 32, block * 32 + 32)))
    if halo is not None:
        lefts.append(halo)
        pieces.append((len(lefts) - 1, slice(0, 16)))
    nl = len(lefts)
    outs = [sds((512, 512), BF16), sds((512, 128), BF16), sds((8, 512), F32)]
    ospecs = [pl.BlockSpec(memory_space=pl.ANY)] * 3
    if extra:
        outs.append(sds((16, 640), BF16))
        ospecs.append(VM)
    no = len(outs)
    aliased = [] if bufs is None else list(bufs)

    def kernel(i, *refs):
        lrefs, refs = refs[:nl], refs[nl:]
        w_ref, s_ref = refs[:2]
        refs = refs[2 + len(aliased) :]
        orefs, refs = refs[:no], refs[no:]
        acc, acc_s, main, small, turned, steps, sem = refs

        acc[...] = jnp.zeros_like(acc)
        acc_s[...] = jnp.zeros_like(acc_s)

        def one(k, carry):
            here = pl.ds(pl.multiple_of(k * kb, kb), kb)
            lhs = jnp.concatenate([lrefs[n][rows_of, here] for n, rows_of in pieces], axis=0)
            acc[...] += dot(lhs, w_ref[here, :])
            acc_s[...] += dot_nt(lhs, s_ref[:, here])
            return carry

        lax.fori_loop(0, depth // kb, one, 0)
        copies = []
        for s in range(count):
            for t in range(8):
                at = slice(s * 128 + t * 16, s * 128 + t * 16 + 16)
                dst = pl.ds(pl.multiple_of(i[4 + t] * 16, 16) + s * 128, 16)
                main[dst, :] = acc[at, :].astype(BF16)
                small[dst, :] = acc_s[at, 0:128].astype(BF16)
                turned[dst, :] = acc_s[at, 128:256]
            here = slice(s * 128, s * 128 + 128)
            steps[:, here] = jnp.transpose(turned[here, :])[0:8, :]
            there = pl.ds(pl.multiple_of(i[slots[s]] * 128, 128), 128)
            for source, target in (
                (main.at[here, :], orefs[0].at[there, :]),
                (small.at[here, :], orefs[1].at[there, :]),
                (steps.at[:, here], orefs[2].at[:, there]),
            ):
                copies.append(pltpu.make_async_copy(source, target, sem.at[len(copies)]))
        for copy in copies:
            copy.start()
        if extra:
            orefs[3][:, 0:512] = acc[rows : rows + 16, :].astype(BF16)
            orefs[3][:, 512:640] = acc_s[rows : rows + 16, 0:128].astype(BF16)
        for copy in copies:
            copy.wait()

    first = 1 + nl + 2
    out = pl.pallas_call(
        kernel,
        out_shape=outs,
        in_specs=[SM] + [VM] * (nl + 2) + [pl.BlockSpec(memory_space=pl.ANY)] * len(aliased),
        out_specs=ospecs,
        scratch_shapes=[
            pltpu.VMEM((rows + extra, 512), F32),
            pltpu.VMEM((rows + extra, 256), F32),
            pltpu.VMEM((rows, 512), BF16),
            pltpu.VMEM((rows, 128), BF16),
            pltpu.VMEM((rows, 128), F32),
            pltpu.VMEM((8, rows), F32),
            pltpu.SemaphoreType.DMA((3 * count,)),
        ],
        input_output_aliases={first + n: n for n in range(len(aliased))},
        compiler_params=pltpu.CompilerParams(vmem_limit_bytes=14 * MIB),
        cost_estimate=cost(2 * rows * depth * 768, 2 * depth * 768),
    )(idx, *lefts, input_w, small_w, *aliased)
    return list(out)


def conv_rows(window, taps, rows):
    running = taps[CONV : CONV + 1, :] + taps[0:1, :] * window[13 : 13 + rows, :]
    for k in range(1, CONV):
        running = running + taps[k : k + 1, :] * window[13 + k : 13 + k + rows, :]
    return silu(running)


def conv_states_kernel(idx, rows_ref, halo_ref, taps_ref, out_ref, full):
    taps = taps_ref[...]
    for k in range(4):
        if k == 0:
            window = jnp.concatenate([halo_ref[:, 512:640], rows_ref[0:128, :]], axis=0).astype(F32)
        else:
            window = rows_ref[128 * k - 16 : 128 * k + 128, :].astype(F32)
        full[128 * k : 128 * k + 128, :] = conv_rows(window, taps, 128).astype(BF16)
    half = idx[13]
    out_ref[...] = full[pl.ds(pl.multiple_of(half * 256, 256), 256), :]


def conv_states(idx, rows, halo, taps):
    return pl.pallas_call(
        conv_states_kernel,
        out_shape=sds((256, 128), BF16),
        in_specs=[SM, VM, VM, VM],
        out_specs=VM,
        scratch_shapes=[pltpu.VMEM((512, 128), BF16)],
        compiler_params=pltpu.CompilerParams(vmem_limit_bytes=14 * MIB),
        cost_estimate=cost(2e6, 4e5),
        name="conv_states",
    )(idx, rows, halo, taps)


def columns_of(rows8):
    return jnp.transpose(rows8)


def column(par, start):
    row = lax.broadcasted_iota(jnp.int32, (8, 128), 0)
    out = jnp.zeros((8, 128), F32)
    for h in range(8):
        out = jnp.where(row == h, par[start + h], out)
    return out


def inputs_kernel(par_ref, rows_ref, halo_ref, taps_ref, step_ref, x_ref, hi_ref, lo_ref, dt_ref, cum_ref, weight_ref, longer):
    taps = taps_ref[...]
    rate = jnp.exp(column(par_ref, 0))
    bias = column(par_ref, 8)
    lane = lax.bitwise_and(lax.broadcasted_iota(jnp.int32, (8, 512), 1), 127)
    raw = step_ref[...] + jnp.concatenate([bias] * 4, axis=1)
    dt = jnp.maximum(raw, 0.0) + jnp.log1p(jnp.exp(-jnp.abs(raw)))
    cum = -dt * jnp.concatenate([rate] * 4, axis=1)
    for b in range(7):
        cum = cum + jnp.where(lane >= (1 << b), pltpu.roll(cum, 1 << b, 1), 0.0)
    dt_ref[...] = dt
    cum_ref[...] = cum
    after = jnp.zeros((8, 1), F32)
    gaps = []
    for k in reversed(range(4)):
        total = cum[:, 128 * k + 127 : 128 * k + 128]
        gaps.insert(0, jnp.broadcast_to(total + after, (8, 128)))
        after = after + total
    weight_ref[...] = jnp.exp(jnp.concatenate(gaps, axis=1) - cum) * dt
    longer[0:16, :] = halo_ref[:, 0:512]
    longer[16:528, :] = rows_ref[...]

    def one(k, carry):
        start = pl.multiple_of(k * 128, 128)
        here = pl.ds(start, 128)
        cols = columns_of(weight_ref[:, here])
        window = longer[pl.ds(start, 144), :]
        for p in range(4):
            ch = slice(128 * p, 128 * p + 128)
            x = conv_rows(window[:, ch].astype(F32), taps[:, ch], 128).astype(BF16)
            x_ref[here, ch] = x
            hi, lo = split(x.astype(F32) * pair_scale(cols, p))
            hi_ref[here, ch] = hi
            lo_ref[here, ch] = lo
        return carry

    lax.fori_loop(0, 4, one, 0)


def inputs_stage(rows, halo, taps, step, par):
    return pl.pallas_call(
        inputs_kernel,
        out_shape=[sds((512, 512), BF16)] * 3 + [sds((8, 512), F32)] * 2,
        in_specs=[SM] + [VM] * 4,
        out_specs=[VM] * 5,
        scratch_shapes=[pltpu.VMEM((8, 512), F32), pltpu.VMEM((528, 512), BF16)],
        compiler_params=pltpu.CompilerParams(vmem_limit_bytes=14 * MIB),
        cost_estimate=cost(1e7, 2e6),
        name="inputs_stage",
    )(par, rows, halo, taps, step)


def gathered_block(idx, own_ref, oth_ref, block, rows):
    place = lax.bitwise_xor(jnp.int32(block), idx[12])
    return jnp.where(idx[13] == rows, own_ref[place], oth_ref[place])


LOG2 = 0.6931471805599453


def scaled(value):
    most = jnp.max(jnp.abs(value), axis=0, keepdims=True)
    power = jnp.ceil(jnp.log(most) * (1.0 / LOG2))
    power = jnp.minimum(jnp.maximum(power, -100.0), 120.0)
    return value * jnp.exp(power * -LOG2), power


def unscaled(ref_value):
    return ref_value[0:256, :] * jnp.exp(ref_value[256:257, :] * LOG2)


def state_kernel(idx, own_ref, oth_ref, hi_ref, lo_ref, cum_ref, out_ref):
    halves = []
    for n in range(2):
        write = jnp.concatenate(
            [gathered_block(idx, own_ref, oth_ref, n, 0), gathered_block(idx, own_ref, oth_ref, n, 1)], axis=0
        )
        halves.append(write)
    write = jnp.concatenate(halves, axis=1)
    state = dot_tn(write, hi_ref[...]) + dot_tn(write, lo_ref[...])
    total = (
        cum_ref[:, 127:128] + cum_ref[:, 255:256] + cum_ref[:, 383:384] + cum_ref[:, 511:512]
    )
    damp = jnp.maximum(total, -110.0) * 256.0
    lane = lax.broadcasted_iota(jnp.int32, (16, 128), 1)
    row = lax.broadcasted_iota(jnp.int32, (16, 128), 0)
    for q in range(4):
        place = lax.bitwise_xor(jnp.int32(q), idx[14])
        mant, power = scaled(state[:, 128 * q : 128 * q + 128])
        out_ref[place, 0:256, :] = mant
        low = jnp.broadcast_to(damp[2 * q : 2 * q + 1, :], (16, 128))
        high = jnp.broadcast_to(damp[2 * q + 1 : 2 * q + 2, :], (16, 128))
        value = jnp.where(lane < 64, low, high)
        one = value.astype(BF16).astype(F32)
        two = (value - one).astype(BF16).astype(F32)
        three = value - one - two
        packed = jnp.where(row == 1, one, jnp.where(row == 2, two, jnp.where(row == 3, three, 0.0)))
        out_ref[place, 256:272, :] = jnp.where(row == 0, power, packed)


def state_stage(idx, own, oth, hi, lo, cum):
    return pl.pallas_call(
        state_kernel,
        out_shape=sds((4, 272, 128), F32),
        in_specs=[SM] + [VM] * 5,
        out_specs=VM,
        compiler_params=pltpu.CompilerParams(vmem_limit_bytes=14 * MIB),
        cost_estimate=cost(2.7e8, 2e6),
        name="state_stage",
    )(idx, own, oth, hi, lo, cum)


def prefix_kernel(idx, s0, s1, s2, s3, inc_ref, pre_ref, tot_ref):
    place = idx[14]
    odd = lax.bitwise_and(place, 1) == 1
    far = lax.bitwise_and(place, 2) == 2
    slots = [s0[...], s1[...], s2[...], s3[...]]
    a, b = jnp.where(odd, slots[1], slots[0]), jnp.where(odd, slots[0], slots[1])
    c, d = jnp.where(odd, slots[3], slots[2]), jnp.where(odd, slots[2], slots[3])
    ordered = [jnp.where(far, c, a), jnp.where(far, d, b), jnp.where(far, a, c), jnp.where(far, b, d)]
    running = jnp.zeros((256, 128), F32)
    carried = jnp.ones((1, 128), F32)
    for k in range(4):
        inc_ref[k] = running
        pre_ref[k] = jnp.broadcast_to(carried, (8, 128))
        tail = ordered[k][256:272, :]
        damp = jnp.exp((tail[1:2, :] + tail[2:3, :] + tail[3:4, :]) * (1.0 / 256.0))
        running = damp * running + unscaled(ordered[k])
        carried = carried * damp
    mant, power = scaled(running)
    tot_ref[0:256, :] = mant
    tot_ref[256:272, :] = jnp.broadcast_to(power, (16, 128))


def prefix_stage(idx, s0, s1, s2, s3):
    return pl.pallas_call(
        prefix_kernel,
        out_shape=[sds((4, 256, 128), F32), sds((4, 8, 128), F32), sds((272, 128), F32)],
        in_specs=[SM] + [VM] * 4,
        out_specs=[VM] * 3,
        compiler_params=pltpu.CompilerParams(vmem_limit_bytes=14 * MIB),
        cost_estimate=cost(1e6, 1e6),
        name="prefix_stage",
    )(idx, s0, s1, s2, s3)


def spread_kernel(idx, inc_ref, pre_ref, far_ref, out_ref):
    far = jnp.where(idx[15] > 0, unscaled(far_ref[...]), 0.0)
    for k in range(4):
        place = lax.bitwise_xor(jnp.int32(k), idx[14])
        mant, power = scaled(inc_ref[k] + pre_ref[k][0:1, :] * far)
        out_ref[place, 0:256, :] = mant
        out_ref[place, 256:272, :] = jnp.broadcast_to(power, (16, 128))


def spread_stage(idx, inc, pre, far):
    return pl.pallas_call(
        spread_kernel,
        out_shape=sds((4, 272, 128), F32),
        in_specs=[SM] + [VM] * 3,
        out_specs=VM,
        compiler_params=pltpu.CompilerParams(vmem_limit_bytes=14 * MIB),
        cost_estimate=cost(1e6, 1e6),
        name="spread_stage",
    )(idx, inc, pre, far)


def scan_kernel(idx, par_ref, own_ref, oth_ref, x_ref, dt_ref, cum_ref, y_ref, read_ref, state):
    row = lax.broadcasted_iota(jnp.int32, (128, 128), 0)
    col = lax.broadcasted_iota(jnp.int32, (128, 128), 1)
    causal = row >= col
    left = col < 64
    zero = jnp.zeros((128, 128), BF16)
    state[...] = jnp.zeros_like(state)

    def one(k, carry):
        here = pl.ds(pl.multiple_of(k * 128, 128), 128)
        half = lax.div(k, 2)
        sub = pl.ds(pl.multiple_of(lax.rem(k, 2) * 128, 128), 128)

        def part(block):
            place = lax.bitwise_xor(jnp.int32(block), idx[12])
            return jnp.where(idx[13] == half, own_ref[place, sub, :], oth_ref[place, sub, :])

        write = jnp.concatenate([part(0), part(1)], axis=1)
        read = jnp.concatenate([part(2), part(3)], axis=1)
        read_ref[here, :] = read
        scores = dot_nt(read, write)
        cum = cum_ref[:, here]
        dt = dt_ref[:, here]
        cols = columns_of(cum)
        exp_cols = columns_of(jnp.exp(cum))
        total = cum[:, 127:128]
        end_cols = columns_of(jnp.exp(total - cum) * dt)
        damp = jnp.exp(total)
        for p in range(4):
            ch = slice(128 * p, 128 * p + 128)
            x = x_ref[here, ch]
            xf = x.astype(F32)
            mixes = []
            for h in (2 * p, 2 * p + 1):
                gap = jnp.broadcast_to(cols[:, h : h + 1], (128, 128)) - cum[h : h + 1, :]
                damping = jnp.exp(jnp.where(causal, gap, -jnp.inf))
                mixes.append(scores * damping * dt[h : h + 1, :])
            mix = jnp.concatenate(mixes, axis=1)
            both = jnp.concatenate([jnp.where(left, x, zero), jnp.where(left, zero, x)], axis=0)
            mix_hi, mix_lo = split(mix)
            y = dot(mix_hi, both) + dot(mix_lo, both)
            y = y + jnp.where(left[0:1, :], par_ref[16 + 2 * p], par_ref[17 + 2 * p]) * xf
            before = state[:, ch]
            s_hi, s_lo = split(before)
            y_ref[here, ch] = y + pair_scale(exp_cols, p) * (dot(read, s_hi) + dot(read, s_lo))
            in_hi, in_lo = split(xf * pair_scale(end_cols, p))
            keep = jnp.where(
                left[0:1, :],
                jnp.broadcast_to(damp[2 * p : 2 * p + 1, :], (1, 128)),
                jnp.broadcast_to(damp[2 * p + 1 : 2 * p + 2, :], (1, 128)),
            )
            state[:, ch] = keep * before + dot_tn(write, in_hi) + dot_tn(write, in_lo)
        return carry

    lax.fori_loop(0, 4, one, 0)


def scan_stage(idx, own, oth, x, dt, cum, par):
    return pl.pallas_call(
        scan_kernel,
        out_shape=[sds((512, 512), F32), sds((512, 256), BF16)],
        in_specs=[SM] * 2 + [VM] * 5,
        out_specs=[VM] * 2,
        scratch_shapes=[pltpu.VMEM((256, 512), F32)],
        compiler_params=pltpu.CompilerParams(vmem_limit_bytes=14 * MIB),
        cost_estimate=cost(6e9, 3e6),
        name="scan_stage",
    )(idx, par, own, oth, x, dt, cum)


def gate_kernel(idx, y_ref, read_ref, q0, q1, q2, q3, cum_ref, gate_ref, u_ref, ss_ref):
    place = idx[14]
    odd = lax.bitwise_and(place, 1) == 1
    far = lax.bitwise_and(place, 2) == 2
    slots = [q0[...], q1[...], q2[...], q3[...]]
    a, b = jnp.where(odd, slots[1], slots[0]), jnp.where(odd, slots[0], slots[1])
    c, d = jnp.where(odd, slots[3], slots[2]), jnp.where(odd, slots[2], slots[3])
    ordered = [jnp.where(far, c, a), jnp.where(far, d, b), jnp.where(far, a, c), jnp.where(far, b, d)]
    halves = [split(unscaled(v)) for v in ordered]

    def one(k, before):
        here = pl.ds(pl.multiple_of(k * 128, 128), 128)
        cum = cum_ref[:, here]
        cols = columns_of(jnp.exp(cum + before))
        read = read_ref[here, :]
        squares = jnp.zeros((128, 128), F32)
        for p in range(4):
            ch = slice(128 * p, 128 * p + 128)
            carried = dot(read, halves[p][0]) + dot(read, halves[p][1])
            y = y_ref[here, ch] + pair_scale(cols, p) * carried
            u = y * silu(gate_ref[here, ch].astype(F32))
            u_ref[here, ch] = u
            squares = squares + u * u
        ss_ref[pl.ds(k, 1), :] = jnp.sum(jnp.transpose(squares), axis=0, keepdims=True)
        return before + cum[:, 127:128]

    lax.fori_loop(0, 4, one, jnp.zeros((8, 1), F32), unroll=1)


def gate_stage(idx, y, read, quarters, cum, gate):
    return pl.pallas_call(
        gate_kernel,
        out_shape=[sds((512, 512), F32), sds((4, 128), F32)],
        in_specs=[SM] + [VM] * 8,
        out_specs=[VM] * 2,
        compiler_params=pltpu.CompilerParams(vmem_limit_bytes=14 * MIB),
        cost_estimate=cost(2e8, 3e6),
        name="gate_stage",
    )(idx, y, read, *quarters, cum, gate)


def load_kernel(src_ref, dst_ref, sem):
    copy = pltpu.make_async_copy(src_ref, dst_ref, sem)
    copy.start()
    copy.wait()


def load(array):
    return pl.pallas_call(
        load_kernel,
        out_shape=sds(array.shape, array.dtype),
        in_specs=[pl.BlockSpec(memory_space=pltpu.HBM)],
        out_specs=VM,
        scratch_shapes=[pltpu.SemaphoreType.DMA],
        compiler_params=pltpu.CompilerParams(vmem_limit_bytes=8 * MIB),
        cost_estimate=cost(1, 8 * MIB),
        name="load",
    )(array)


def out_block(idx, slots, u, ss, gain, out_w):
    count = len(slots)
    rows = 64 * count
    wide = 1024 if count == 1 else 512

    def kernel(i, u_ref, ss_ref, gain_ref, w_ref, own_ref, oth_ref, lhs):
        for s in range(count):
            place = i[slots[s]]
            mean = ss_ref[pl.ds(place, 1), :] / (DINNER // GROUPS)
            scale = jnp.transpose(jnp.broadcast_to(lax.rsqrt(mean + 1e-05), (128, 128)))
            here = pl.ds(pl.multiple_of(place * 128, 128), 128)
            for p in range(4):
                ch = slice(128 * p, 128 * p + 128)
                normed = (u_ref[here, ch] * scale * gain_ref[:, ch]).astype(BF16)
                for t in range(8):
                    core, tile = t % 2, t // 2
                    at = lax.bitwise_xor(jnp.int32(core), i[13]) * rows + 64 * s + tile * 16
                    lhs[pl.ds(pl.multiple_of(at, 16), 16), ch] = normed[t * 16 : t * 16 + 16, :]

        def one(n, carry):
            here = pl.ds(pl.multiple_of(n * wide, wide), wide)
            part = dot(lhs[...], w_ref[:, here])
            own_ref[:, here] = part[0:rows, :]
            oth_ref[:, here] = part[rows : 2 * rows, :].astype(BF16)
            return carry

        lax.fori_loop(0, 4096 // wide, one, 0)

    return pl.pallas_call(
        kernel,
        out_shape=[sds((rows, 4096), F32), sds((rows, 4096), BF16)],
        in_specs=[SM] + [VM] * 4,
        out_specs=[VM] * 2,
        scratch_shapes=[pltpu.VMEM((2 * rows, 512), BF16)],
        compiler_params=pltpu.CompilerParams(vmem_limit_bytes=20 * MIB),
        cost_estimate=cost(4 * rows * 512 * 4096, 6e6),
        name="out_block",
    )(idx, u, ss, gain, out_w)


def body(
    tokens,
    gate_weight,
    input_weight,
    state_weight,
    step_weight,
    input_conv,
    state_conv,
    log_rate,
    step_bias,
    skip_gain,
    norm_gain,
    out_weight,
):
    me = lax.axis_index("tp")
    x, zl, core = me // 8, (me // 2) % 4, me % 2
    y, later = lax.axis_index("ctx") % 4, lax.axis_index("ctx") // 4
    n = jnp.arange(16, dtype=jnp.int32)
    turn = jnp.where(n == 1, 3, jnp.where(n == 2, 1, jnp.where(n == 3, 2, 0)))
    tile = n - 4
    where = jnp.bitwise_xor(tile % 4, zl) * 2 + jnp.bitwise_xor(tile // 4, core)
    idx = jnp.where(n < 4, (x + turn) % 4, where)
    idx = jnp.where(n == 12, zl, jnp.where(n == 13, core, jnp.where(n == 14, y, jnp.where(n == 15, later, idx))))
    idx = idx.astype(jnp.int32)

    state_rows_w = state_weight.T
    state_pair = flip(state_rows_w, "tp", 1)
    taps_pair = flip(state_conv, "tp", 1)
    low = core == 0
    first = jnp.where(low, state_rows_w, state_pair)
    second = jnp.where(low, state_pair, state_rows_w)
    small_w = jnp.concatenate(
        [first, second, step_weight.T, jnp.zeros((120, tokens.shape[1]), BF16)], axis=0
    )
    state_taps = jnp.concatenate(
        [jnp.where(low, state_conv, taps_pair), jnp.where(low, taps_pair, state_conv)], axis=1
    )
    par = jnp.concatenate([log_rate, step_bias, skip_gain])

    tiles = [tokens, flip(tokens, "tp", 2)]
    tiles.append(flip(tokens, "tp", 4))
    tiles.append(flip(tokens, "tp", 6))
    part1 = jnp.concatenate(tiles[:2], axis=0)
    right1 = along_x(part1, 1)
    left1 = along_x(part1, -1)
    other1 = flip(part1, "tp", 1)
    late, other1 = lax.optimization_barrier((tiles[2:], other1))
    part2 = jnp.concatenate(late, axis=0)
    right2 = along_x(part2, 1)
    left2 = along_x(part2, -1)
    other2 = flip(part2, "tp", 1)
    own_parts = [(part1, 0), (part2, 0), (other1, 0), (other2, 0)]
    last = tiles[0][8:]
    for s in (1, 2, 3):
        last = jnp.where(zl == 3 - s, tiles[s][8:], last)
    to = {
        "h0": lambda c, t: (c + 1, t) if c < 7 and t >= 24 and t % 2 else None,
        "hc": lambda c, t: (c, t - 1) if t >= 24 and t % 2 else None,
        "h1": lambda c, t: (c, t - 24) if t >= 24 else None,
        "h2": lambda c, t: (c, t - 8) if t >= 24 else ((c, t + 8) if t < 8 else None),
    }
    rim = hop(last, to["h0"])
    far_a = along_x(right1, 1)
    side1 = flip(jnp.concatenate([right1, left1], axis=0), "tp", 1)
    rim = rim + hop(rim, to["hc"])
    rim = rim + hop(rim, to["h1"])
    far_b = along_x(left2, -1)
    side2 = flip(jnp.concatenate([right2, left2], axis=0), "tp", 1)
    rim = rim + hop(rim, to["h2"])
    rights = [(right1, 0), (right2, 0), (side1, 0), (side2, 0)]
    lefts = [(left1, 0), (left2, 0), (side1, 1), (side2, 1)]
    bufs = project_resident(
        own_parts + rights + lefts, None, [0, 1, 2], idx, input_weight, small_w, None
    )
    rim = jnp.concatenate([jnp.zeros_like(rim), rim], axis=0)
    far_a_other = flip(far_a, "tp", 1)
    far_b_other = flip(far_b, "tp", 1)
    fars = [(far_a, 0), (far_b, 0), (far_a_other, 0), (far_b_other, 0)]
    input_rows, state_rows, step_raw, halo = project_resident(
        fars, rim, [3], idx, input_weight, small_w, bufs
    )

    piece = conv_states(idx, state_rows, halo, state_taps)
    pieces = jnp.stack([piece] + [flip(piece, "tp", 2 * s) for s in (1, 2, 3)])
    pieces_other = flip(pieces, "tp", 1)

    xs, x_hi, x_lo, dt, cum = inputs_stage(input_rows, halo, input_conv, step_raw, par)
    payload = state_stage(idx, pieces, pieces_other, x_hi, x_lo, cum)
    ends = [payload[0]] + [half_flip(payload[s], s) for s in (1, 2, 3)]
    y_local, read_vec = scan_stage(idx, pieces, pieces_other, xs, dt, cum, par)
    inc, pre, total = prefix_stage(idx, *ends)
    before = half_flip(total, 4)
    everything = own_parts + rights + lefts + fars
    (gate_rows,) = project(everything, [0, 1, 2, 3], idx, gate_weight, None, None, None)
    spread = spread_stage(idx, inc, pre, before)
    quarters = [spread[0]] + [half_flip(spread[s], s) for s in (1, 2, 3)]
    u, squares = gate_stage(idx, y_local, read_vec, quarters, cum, gate_rows)

    squares = squares + flip(squares, "tp", 1)
    squares = squares + flip(squares, "tp", 2)
    squares = squares + flip(squares, "tp", 4)

    gain = norm_gain.reshape(1, 512)
    out_w = load(out_weight)
    far_own, far_oth = out_block(idx, [3], u, squares, gain, out_w)
    far_sum = far_own + flip(far_oth, "tp", 1).astype(F32)
    got_a = along_x(narrow(far_sum[:32]), 1)
    got_b = along_x(narrow(far_sum[32:]), -1)
    rest_own, rest_oth = out_block(idx, [2, 1, 0], u, squares, gain, out_w)
    rest_got = flip(rest_oth, "tp", 1)
    half = out_w.shape[1] // 2
    outs = []
    moved = []
    for n in range(2):
        cols = slice(n * half, n * half + half)

        def rest_sum(rows):
            return rest_own[rows, cols] + rest_got[rows, cols].astype(F32)

        to_right = narrow(rest_sum(slice(0, 64)) + jnp.pad(widen(got_a[:, cols]), ((0, 32), (0, 0))))
        to_left = narrow(rest_sum(slice(64, 128)) + jnp.pad(widen(got_b[:, cols]), ((32, 0), (0, 0))))
        from_left = along_x(to_right, 1)
        from_right = along_x(to_left, -1)
        moved.append((rest_sum(slice(128, 192)), from_left, from_right))
    for n in range(2):
        own, from_left, from_right = moved[n]

        def tile_sum(place):
            at = place * 16
            return (
                lax.dynamic_slice_in_dim(own, at, 16, 0)
                + widen(lax.dynamic_slice_in_dim(from_left, at, 16, 0))
                + widen(lax.dynamic_slice_in_dim(from_right, at, 16, 0))
            )

        out = tile_sum(zl)
        for p in (1, 2, 3):
            part = narrow(tile_sum(jnp.bitwise_xor(zl, p)))
            part = flip(part, "tp", 2 * p)
            out = out + widen(part)
        outs.append(out.astype(BF16))
    return jnp.concatenate(outs, axis=1)


def half_flip(value, mask):
    return flip(value.astype(F16), "ctx", mask).astype(F32)


def narrow(value):
    return (value * 32.0).astype(F16)


def widen(value):
    return value.astype(F32) * 0.03125


def solution(mesh):
    placed = (
        P(("ctx", "tp"), None),
        P(None, "tp"),
        P(None, "tp"),
        P(None, "tp"),
        P(None, "tp"),
        P(None, "tp"),
        P(None, "tp"),
        P("tp"),
        P("tp"),
        P("tp"),
        P("tp"),
        P("tp", None),
    )

    return jax.shard_map(
        body, mesh=mesh, in_specs=placed, out_specs=P(("ctx", "tp"), None), check_vma=False
    )
```

```python
import jax
import jax.numpy as jnp
from jax import lax
from jax.experimental import pallas as pl
from jax.experimental.pallas import tpu as pltpu
from jax.sharding import PartitionSpec as P


GROUPS = 4
CONV = 4
DINNER = 16384
F32 = jnp.float32
BF16 = jnp.bfloat16
F16 = jnp.float16
MIB = 1024 * 1024


VM = pl.BlockSpec(memory_space=pltpu.VMEM)
SM = pl.BlockSpec(memory_space=pltpu.SMEM)


def sds(shape, dtype):
    return jax.ShapeDtypeStruct(shape, dtype)


def cost(flops, nbytes):
    return pl.CostEstimate(flops=int(flops), bytes_accessed=int(nbytes), transcendentals=0)


def send(array, axis, to):
    size = lax.axis_size(axis)
    pairs = [(i, to(i)) for i in range(size) if to(i) is not None]
    return lax.ppermute(array, axis, pairs)


def hop(array, to):
    pairs = [(c * 32 + t, to(c, t)) for c in range(8) for t in range(32)]
    pairs = [(i, d[0] * 32 + d[1]) for i, d in pairs if d is not None]
    return lax.ppermute(array, ("ctx", "tp"), pairs)


def flip(array, axis, mask):
    return send(array, axis, lambda i: i ^ mask)


def along_x(array, by):
    return send(array, "tp", lambda i: (i + 8 * by) % 32)


def dot(a, b):
    return lax.dot_general(a, b, (((1,), (0,)), ((), ())), preferred_element_type=F32)


def dot_nt(a, b):
    return lax.dot_general(a, b, (((1,), (1,)), ((), ())), preferred_element_type=F32)


def dot_tn(a, b):
    return lax.dot_general(a, b, (((0,), (0,)), ((), ())), preferred_element_type=F32)


def silu(v):
    return v * jax.nn.sigmoid(v)


def pair_scale(cols, pair):
    rows = cols.shape[0]
    lane = lax.broadcasted_iota(jnp.int32, (rows, 128), 1)
    low = jnp.broadcast_to(cols[:, 2 * pair : 2 * pair + 1], (rows, 128))
    high = jnp.broadcast_to(cols[:, 2 * pair + 1 : 2 * pair + 2], (rows, 128))
    return jnp.where(lane < 64, low, high)


def split(value):
    high = value.astype(BF16)
    return high, (value - high.astype(F32)).astype(BF16)


def gate_of(parts, slots, idx, gate_w):
    depth = parts[0][0].shape[1]
    steps = 4
    kb = depth // steps
    count = len(slots)
    rows = 128 * count
    nl = len(parts)

    def kernel(i, *refs):
        lrefs, w_ref, out_ref, acc, ready, sem = refs[:nl], *refs[nl:]
        k = pl.program_id(0)
        part = dot(jnp.concatenate([r[...] for r in lrefs], axis=0), w_ref[...])

        @pl.when(k == 0)
        def _():
            acc[...] = part

        @pl.when(k > 0)
        def _():
            acc[...] += part

        @pl.when(k == steps - 1)
        def _():
            def tile(n, carry):
                at = pl.ds(pl.multiple_of(n * 16, 16), 16)
                to = i[4 + lax.rem(n, 8)] * 16 + lax.div(n, 8) * 128
                rounded = acc[at, :].astype(BF16).astype(F32)
                ready[pl.ds(pl.multiple_of(to, 16), 16), :] = silu(rounded)
                return carry

            lax.fori_loop(0, 8 * count, tile, 0, unroll=2)
            copies = []
            for s in range(count):
                there = pl.ds(pl.multiple_of(i[slots[s]] * 128, 128), 128)
                copies.append(
                    pltpu.make_async_copy(ready.at[s * 128 : s * 128 + 128, :], out_ref.at[there, :], sem.at[s])
                )
            for copy in copies:
                copy.start()
            for copy in copies:
                copy.wait()

    return pl.pallas_call(
        kernel,
        out_shape=sds((512, 512), F32),
        grid_spec=pltpu.PrefetchScalarGridSpec(
            num_scalar_prefetch=1,
            grid=(steps,),
            in_specs=[pl.BlockSpec((32, kb), lambda k, i, b=b: (b, k)) for _, b in parts]
            + [pl.BlockSpec((kb, 512), lambda k, i: (k, 0))],
            out_specs=pl.BlockSpec(memory_space=pl.ANY),
            scratch_shapes=[
                pltpu.VMEM((rows, 512), F32),
                pltpu.VMEM((rows, 512), F32),
                pltpu.SemaphoreType.DMA((count,)),
            ],
        ),
        compiler_params=pltpu.CompilerParams(vmem_limit_bytes=14 * MIB),
        cost_estimate=cost(2 * rows * depth * 512, 2 * depth * 512),
    )(idx, *[p for p, _ in parts], gate_w)


def project_resident(parts, halo, slots, idx, input_w, small_w, bufs):
    depth = parts[0][0].shape[1]
    kb = 1024 if halo is not None else 512
    count = len(slots)
    rows = 128 * count
    extra = 0 if halo is None else 16
    lefts, pieces = [], []
    for array, block in list(parts):
        known = [n for n, seen in enumerate(lefts) if seen is array]
        if not known:
            lefts.append(array)
        pieces.append((known[0] if known else len(lefts) - 1, slice(block * 32, block * 32 + 32)))
    if halo is not None:
        lefts.append(halo)
        pieces.append((len(lefts) - 1, slice(0, 16)))
    nl = len(lefts)
    outs = [sds((512, 512), BF16), sds((512, 128), BF16), sds((8, 512), F32)]
    ospecs = [pl.BlockSpec(memory_space=pl.ANY)] * 3
    if extra:
        outs.append(sds((16, 640), BF16))
        ospecs.append(VM)
    no = len(outs)
    aliased = [] if bufs is None else list(bufs)

    def kernel(i, *refs):
        lrefs, refs = refs[:nl], refs[nl:]
        w_ref, s_ref = refs[:2]
        refs = refs[2 + len(aliased) :]
        orefs, refs = refs[:no], refs[no:]
        acc, acc_s, main, small, turned, steps, sem = refs

        acc[...] = jnp.zeros_like(acc)
        acc_s[...] = jnp.zeros_like(acc_s)

        def one(k, carry):
            here = pl.ds(pl.multiple_of(k * kb, kb), kb)
            lhs = jnp.concatenate([lrefs[n][rows_of, here] for n, rows_of in pieces], axis=0)
            acc[...] += dot(lhs, w_ref[here, :])
            acc_s[...] += dot_nt(lhs, s_ref[:, here])
            return carry

        lax.fori_loop(0, depth // kb, one, 0)
        copies = []
        for s in range(count):
            for t in range(8):
                at = slice(s * 128 + t * 16, s * 128 + t * 16 + 16)
                dst = pl.ds(pl.multiple_of(i[4 + t] * 16, 16) + s * 128, 16)
                main[dst, :] = acc[at, :].astype(BF16)
                small[dst, :] = acc_s[at, 0:128].astype(BF16)
                turned[dst, :] = acc_s[at, 128:256]
            here = slice(s * 128, s * 128 + 128)
            steps[:, here] = jnp.transpose(turned[here, :])[0:8, :]
            there = pl.ds(pl.multiple_of(i[slots[s]] * 128, 128), 128)
            for source, target in (
                (main.at[here, :], orefs[0].at[there, :]),
                (small.at[here, :], orefs[1].at[there, :]),
                (steps.at[:, here], orefs[2].at[:, there]),
            ):
                copies.append(pltpu.make_async_copy(source, target, sem.at[len(copies)]))
        for copy in copies:
            copy.start()
        if extra:
            orefs[3][:, 0:512] = acc[rows : rows + 16, :].astype(BF16)
            orefs[3][:, 512:640] = acc_s[rows : rows + 16, 0:128].astype(BF16)
        for copy in copies:
            copy.wait()

    first = 1 + nl + 2
    out = pl.pallas_call(
        kernel,
        out_shape=outs,
        in_specs=[SM] + [VM] * (nl + 2) + [pl.BlockSpec(memory_space=pl.ANY)] * len(aliased),
        out_specs=ospecs,
        scratch_shapes=[
            pltpu.VMEM((rows + extra, 512), F32),
            pltpu.VMEM((rows + extra, 256), F32),
            pltpu.VMEM((rows, 512), BF16),
            pltpu.VMEM((rows, 128), BF16),
            pltpu.VMEM((rows, 128), F32),
            pltpu.VMEM((8, rows), F32),
            pltpu.SemaphoreType.DMA((3 * count,)),
        ],
        input_output_aliases={first + n: n for n in range(len(aliased))},
        compiler_params=pltpu.CompilerParams(vmem_limit_bytes=14 * MIB),
        cost_estimate=cost(2 * rows * depth * 768, 2 * depth * 768),
    )(idx, *lefts, input_w, small_w, *aliased)
    return list(out)


def conv_rows(window, taps, rows):
    running = taps[CONV : CONV + 1, :] + taps[0:1, :] * window[13 : 13 + rows, :]
    for k in range(1, CONV):
        running = running + taps[k : k + 1, :] * window[13 + k : 13 + k + rows, :]
    return silu(running)


def conv_states_kernel(idx, rows_ref, halo_ref, taps_ref, out_ref, full):
    taps = taps_ref[...]
    for k in range(4):
        if k == 0:
            window = jnp.concatenate([halo_ref[:, 512:640], rows_ref[0:128, :]], axis=0).astype(F32)
        else:
            window = rows_ref[128 * k - 16 : 128 * k + 128, :].astype(F32)
        full[128 * k : 128 * k + 128, :] = conv_rows(window, taps, 128).astype(BF16)
    half = idx[13]
    out_ref[...] = full[pl.ds(pl.multiple_of(half * 256, 256), 256), :]


def conv_states(idx, rows, halo, taps):
    return pl.pallas_call(
        conv_states_kernel,
        out_shape=sds((256, 128), BF16),
        in_specs=[SM, VM, VM, VM],
        out_specs=VM,
        scratch_shapes=[pltpu.VMEM((512, 128), BF16)],
        compiler_params=pltpu.CompilerParams(vmem_limit_bytes=14 * MIB),
        cost_estimate=cost(2e6, 4e5),
        name="conv_states",
    )(idx, rows, halo, taps)


def columns_of(rows8):
    return jnp.transpose(rows8)


def column(par, start):
    row = lax.broadcasted_iota(jnp.int32, (8, 128), 0)
    out = jnp.zeros((8, 128), F32)
    for h in range(8):
        out = jnp.where(row == h, par[start + h], out)
    return out


def inputs_kernel(par_ref, rows_ref, halo_ref, taps_ref, step_ref, x_ref, hi_ref, lo_ref, dt_ref, cum_ref, weight_ref, longer):
    taps = taps_ref[...]
    rate = jnp.exp(column(par_ref, 0))
    bias = column(par_ref, 8)
    lane = lax.bitwise_and(lax.broadcasted_iota(jnp.int32, (8, 512), 1), 127)
    raw = step_ref[...] + jnp.concatenate([bias] * 4, axis=1)
    dt = jnp.maximum(raw, 0.0) + jnp.log1p(jnp.exp(-jnp.abs(raw)))
    cum = -dt * jnp.concatenate([rate] * 4, axis=1)
    for b in range(7):
        cum = cum + jnp.where(lane >= (1 << b), pltpu.roll(cum, 1 << b, 1), 0.0)
    dt_ref[...] = dt
    cum_ref[...] = cum
    after = jnp.zeros((8, 1), F32)
    gaps = []
    for k in reversed(range(4)):
        total = cum[:, 128 * k + 127 : 128 * k + 128]
        gaps.insert(0, jnp.broadcast_to(total + after, (8, 128)))
        after = after + total
    weight_ref[...] = jnp.exp(jnp.concatenate(gaps, axis=1) - cum) * dt
    longer[0:16, :] = halo_ref[:, 0:512]
    longer[16:528, :] = rows_ref[...]

    def one(k, carry):
        start = pl.multiple_of(k * 128, 128)
        here = pl.ds(start, 128)
        cols = columns_of(weight_ref[:, here])
        window = longer[pl.ds(start, 144), :]
        for p in range(4):
            ch = slice(128 * p, 128 * p + 128)
            x = conv_rows(window[:, ch].astype(F32), taps[:, ch], 128).astype(BF16)
            x_ref[here, ch] = x
            hi, lo = split(x.astype(F32) * pair_scale(cols, p))
            hi_ref[here, ch] = hi
            lo_ref[here, ch] = lo
        return carry

    lax.fori_loop(0, 4, one, 0)


def inputs_stage(rows, halo, taps, step, par):
    return pl.pallas_call(
        inputs_kernel,
        out_shape=[sds((512, 512), BF16)] * 3 + [sds((8, 512), F32)] * 2,
        in_specs=[SM] + [VM] * 4,
        out_specs=[VM] * 5,
        scratch_shapes=[pltpu.VMEM((8, 512), F32), pltpu.VMEM((528, 512), BF16)],
        compiler_params=pltpu.CompilerParams(vmem_limit_bytes=14 * MIB),
        cost_estimate=cost(1e7, 2e6),
        name="inputs_stage",
    )(par, rows, halo, taps, step)


def gathered_block(idx, own_ref, oth_ref, block, rows):
    place = lax.bitwise_xor(jnp.int32(block), idx[12])
    return jnp.where(idx[13] == rows, own_ref[place], oth_ref[place])


LOG2 = 0.6931471805599453


def scaled(value):
    most = jnp.max(jnp.abs(value), axis=0, keepdims=True)
    power = jnp.ceil(jnp.log(most) * (1.0 / LOG2))
    power = jnp.minimum(jnp.maximum(power, -100.0), 120.0)
    return value * jnp.exp(power * -LOG2), power


def unscaled(ref_value):
    return ref_value[0:256, :] * jnp.exp(ref_value[256:257, :] * LOG2)


def state_kernel(idx, own_ref, oth_ref, hi_ref, lo_ref, cum_ref, out_ref):
    halves = []
    for n in range(2):
        write = jnp.concatenate(
            [gathered_block(idx, own_ref, oth_ref, n, 0), gathered_block(idx, own_ref, oth_ref, n, 1)], axis=0
        )
        halves.append(write)
    write = jnp.concatenate(halves, axis=1)
    state = dot_tn(write, hi_ref[...]) + dot_tn(write, lo_ref[...])
    total = (
        cum_ref[:, 127:128] + cum_ref[:, 255:256] + cum_ref[:, 383:384] + cum_ref[:, 511:512]
    )
    damp = jnp.maximum(total, -110.0) * 256.0
    lane = lax.broadcasted_iota(jnp.int32, (16, 128), 1)
    row = lax.broadcasted_iota(jnp.int32, (16, 128), 0)
    for q in range(4):
        place = lax.bitwise_xor(jnp.int32(q), idx[14])
        mant, power = scaled(state[:, 128 * q : 128 * q + 128])
        out_ref[place, 0:256, :] = mant
        low = jnp.broadcast_to(damp[2 * q : 2 * q + 1, :], (16, 128))
        high = jnp.broadcast_to(damp[2 * q + 1 : 2 * q + 2, :], (16, 128))
        value = jnp.where(lane < 64, low, high)
        one = value.astype(BF16).astype(F32)
        two = (value - one).astype(BF16).astype(F32)
        three = value - one - two
        packed = jnp.where(row == 1, one, jnp.where(row == 2, two, jnp.where(row == 3, three, 0.0)))
        out_ref[place, 256:272, :] = jnp.where(row == 0, power, packed)


def state_stage(idx, own, oth, hi, lo, cum):
    return pl.pallas_call(
        state_kernel,
        out_shape=sds((4, 272, 128), F32),
        in_specs=[SM] + [VM] * 5,
        out_specs=VM,
        compiler_params=pltpu.CompilerParams(vmem_limit_bytes=14 * MIB),
        cost_estimate=cost(2.7e8, 2e6),
        name="state_stage",
    )(idx, own, oth, hi, lo, cum)


def prefix_kernel(idx, s0, s1, s2, s3, inc_ref, pre_ref, tot_ref):
    place = idx[14]
    odd = lax.bitwise_and(place, 1) == 1
    far = lax.bitwise_and(place, 2) == 2
    slots = [s0[...], s1[...], s2[...], s3[...]]
    a, b = jnp.where(odd, slots[1], slots[0]), jnp.where(odd, slots[0], slots[1])
    c, d = jnp.where(odd, slots[3], slots[2]), jnp.where(odd, slots[2], slots[3])
    ordered = [jnp.where(far, c, a), jnp.where(far, d, b), jnp.where(far, a, c), jnp.where(far, b, d)]
    running = jnp.zeros((256, 128), F32)
    carried = jnp.ones((1, 128), F32)
    for k in range(4):
        inc_ref[k] = running
        pre_ref[k] = jnp.broadcast_to(carried, (8, 128))
        tail = ordered[k][256:272, :]
        damp = jnp.exp((tail[1:2, :] + tail[2:3, :] + tail[3:4, :]) * (1.0 / 256.0))
        running = damp * running + unscaled(ordered[k])
        carried = carried * damp
    mant, power = scaled(running)
    tot_ref[0:256, :] = mant
    tot_ref[256:272, :] = jnp.broadcast_to(power, (16, 128))


def prefix_stage(idx, s0, s1, s2, s3):
    return pl.pallas_call(
        prefix_kernel,
        out_shape=[sds((4, 256, 128), F32), sds((4, 8, 128), F32), sds((272, 128), F32)],
        in_specs=[SM] + [VM] * 4,
        out_specs=[VM] * 3,
        compiler_params=pltpu.CompilerParams(vmem_limit_bytes=14 * MIB),
        cost_estimate=cost(1e6, 1e6),
        name="prefix_stage",
    )(idx, s0, s1, s2, s3)


def spread_kernel(idx, inc_ref, pre_ref, far_ref, out_ref):
    far = jnp.where(idx[15] > 0, unscaled(far_ref[...]), 0.0)
    for k in range(4):
        place = lax.bitwise_xor(jnp.int32(k), idx[14])
        mant, power = scaled(inc_ref[k] + pre_ref[k][0:1, :] * far)
        out_ref[place, 0:256, :] = mant
        out_ref[place, 256:272, :] = jnp.broadcast_to(power, (16, 128))


def spread_stage(idx, inc, pre, far):
    return pl.pallas_call(
        spread_kernel,
        out_shape=sds((4, 272, 128), F32),
        in_specs=[SM] + [VM] * 3,
        out_specs=VM,
        compiler_params=pltpu.CompilerParams(vmem_limit_bytes=14 * MIB),
        cost_estimate=cost(1e6, 1e6),
        name="spread_stage",
    )(idx, inc, pre, far)


def scan_kernel(idx, par_ref, own_ref, oth_ref, x_ref, dt_ref, cum_ref, y_ref, read_ref, state):
    row = lax.broadcasted_iota(jnp.int32, (128, 128), 0)
    col = lax.broadcasted_iota(jnp.int32, (128, 128), 1)
    causal = row >= col
    left = col < 64
    zero = jnp.zeros((128, 128), BF16)
    state[...] = jnp.zeros_like(state)

    def one(k, carry):
        here = pl.ds(pl.multiple_of(k * 128, 128), 128)
        half = lax.div(k, 2)
        sub = pl.ds(pl.multiple_of(lax.rem(k, 2) * 128, 128), 128)

        def part(block):
            place = lax.bitwise_xor(jnp.int32(block), idx[12])
            return jnp.where(idx[13] == half, own_ref[place, sub, :], oth_ref[place, sub, :])

        write = jnp.concatenate([part(0), part(1)], axis=1)
        read = jnp.concatenate([part(2), part(3)], axis=1)
        read_ref[here, :] = read
        scores = dot_nt(read, write)
        cum = cum_ref[:, here]
        dt = dt_ref[:, here]
        cols = columns_of(cum)
        exp_cols = columns_of(jnp.exp(cum))
        total = cum[:, 127:128]
        end_cols = columns_of(jnp.exp(total - cum) * dt)
        damp = jnp.exp(total)
        for p in range(4):
            ch = slice(128 * p, 128 * p + 128)
            x = x_ref[here, ch]
            xf = x.astype(F32)
            mixes = []
            for h in (2 * p, 2 * p + 1):
                gap = jnp.broadcast_to(cols[:, h : h + 1], (128, 128)) - cum[h : h + 1, :]
                damping = jnp.exp(jnp.where(causal, gap, -jnp.inf))
                mixes.append(scores * damping * dt[h : h + 1, :])
            mix = jnp.concatenate(mixes, axis=1)
            both = jnp.concatenate([jnp.where(left, x, zero), jnp.where(left, zero, x)], axis=0)
            mix_hi, mix_lo = split(mix)
            y = dot(mix_hi, both) + dot(mix_lo, both)
            y = y + jnp.where(left[0:1, :], par_ref[16 + 2 * p], par_ref[17 + 2 * p]) * xf
            before = state[:, ch]
            s_hi, s_lo = split(before)
            y_ref[here, ch] = y + pair_scale(exp_cols, p) * (dot(read, s_hi) + dot(read, s_lo))
            in_hi, in_lo = split(xf * pair_scale(end_cols, p))
            keep = jnp.where(
                left[0:1, :],
                jnp.broadcast_to(damp[2 * p : 2 * p + 1, :], (1, 128)),
                jnp.broadcast_to(damp[2 * p + 1 : 2 * p + 2, :], (1, 128)),
            )
            state[:, ch] = keep * before + dot_tn(write, in_hi) + dot_tn(write, in_lo)
        return carry

    lax.fori_loop(0, 4, one, 0)


def scan_stage(idx, own, oth, x, dt, cum, par):
    return pl.pallas_call(
        scan_kernel,
        out_shape=[sds((512, 512), F32), sds((512, 256), BF16)],
        in_specs=[SM] * 2 + [VM] * 5,
        out_specs=[VM] * 2,
        scratch_shapes=[pltpu.VMEM((256, 512), F32)],
        compiler_params=pltpu.CompilerParams(vmem_limit_bytes=14 * MIB),
        cost_estimate=cost(6e9, 3e6),
        name="scan_stage",
    )(idx, par, own, oth, x, dt, cum)


def gate_kernel(idx, y_ref, read_ref, q0, q1, q2, q3, cum_ref, gate_ref, u_ref, ss_ref):
    place = idx[14]
    odd = lax.bitwise_and(place, 1) == 1
    far = lax.bitwise_and(place, 2) == 2
    slots = [q0[...], q1[...], q2[...], q3[...]]
    a, b = jnp.where(odd, slots[1], slots[0]), jnp.where(odd, slots[0], slots[1])
    c, d = jnp.where(odd, slots[3], slots[2]), jnp.where(odd, slots[2], slots[3])
    ordered = [jnp.where(far, c, a), jnp.where(far, d, b), jnp.where(far, a, c), jnp.where(far, b, d)]
    halves = [split(unscaled(v)) for v in ordered]

    def one(k, before):
        here = pl.ds(pl.multiple_of(k * 128, 128), 128)
        cum = cum_ref[:, here]
        cols = columns_of(jnp.exp(cum + before))
        read = read_ref[here, :]
        squares = jnp.zeros((128, 128), F32)
        for p in range(4):
            ch = slice(128 * p, 128 * p + 128)
            carried = dot(read, halves[p][0]) + dot(read, halves[p][1])
            y = y_ref[here, ch] + pair_scale(cols, p) * carried
            u = y * gate_ref[here, ch]
            u_ref[here, ch] = u
            squares = squares + u * u
        ss_ref[pl.ds(k, 1), :] = jnp.sum(jnp.transpose(squares), axis=0, keepdims=True)
        return before + cum[:, 127:128]

    lax.fori_loop(0, 4, one, jnp.zeros((8, 1), F32), unroll=1)


def gate_stage(idx, y, read, quarters, cum, gate):
    return pl.pallas_call(
        gate_kernel,
        out_shape=[sds((512, 512), F32), sds((4, 128), F32)],
        in_specs=[SM] + [VM] * 8,
        out_specs=[VM] * 2,
        compiler_params=pltpu.CompilerParams(vmem_limit_bytes=14 * MIB),
        cost_estimate=cost(2e8, 3e6),
        name="gate_stage",
    )(idx, y, read, *quarters, cum, gate)


def load_kernel(src_ref, dst_ref, sem):
    copy = pltpu.make_async_copy(src_ref, dst_ref, sem)
    copy.start()
    copy.wait()


def load(array):
    return pl.pallas_call(
        load_kernel,
        out_shape=sds(array.shape, array.dtype),
        in_specs=[pl.BlockSpec(memory_space=pltpu.HBM)],
        out_specs=VM,
        scratch_shapes=[pltpu.SemaphoreType.DMA],
        compiler_params=pltpu.CompilerParams(vmem_limit_bytes=8 * MIB),
        cost_estimate=cost(1, 8 * MIB),
        name="load",
    )(array)


def out_block(idx, slots, u, ss, gain, out_w):
    count = len(slots)
    rows = 64 * count
    wide = 1024 if count == 1 else 512

    def kernel(i, u_ref, ss_ref, gain_ref, w_ref, own_ref, oth_ref, lhs):
        for s in range(count):
            place = i[slots[s]]
            mean = ss_ref[pl.ds(place, 1), :] / (DINNER // GROUPS)
            scale = jnp.transpose(jnp.broadcast_to(lax.rsqrt(mean + 1e-05), (128, 128)))
            here = pl.ds(pl.multiple_of(place * 128, 128), 128)
            for p in range(4):
                ch = slice(128 * p, 128 * p + 128)
                normed = (u_ref[here, ch] * scale * gain_ref[:, ch]).astype(BF16)
                for t in range(8):
                    core, tile = t % 2, t // 2
                    at = lax.bitwise_xor(jnp.int32(core), i[13]) * rows + 64 * s + tile * 16
                    lhs[pl.ds(pl.multiple_of(at, 16), 16), ch] = normed[t * 16 : t * 16 + 16, :]

        def one(n, carry):
            here = pl.ds(pl.multiple_of(n * wide, wide), wide)
            part = dot(lhs[...], w_ref[:, here])
            own_ref[:, here] = part[0:rows, :]
            oth_ref[:, here] = part[rows : 2 * rows, :].astype(BF16)
            return carry

        lax.fori_loop(0, 4096 // wide, one, 0)

    return pl.pallas_call(
        kernel,
        out_shape=[sds((rows, 4096), F32), sds((rows, 4096), BF16)],
        in_specs=[SM] + [VM] * 4,
        out_specs=[VM] * 2,
        scratch_shapes=[pltpu.VMEM((2 * rows, 512), BF16)],
        compiler_params=pltpu.CompilerParams(vmem_limit_bytes=20 * MIB),
        cost_estimate=cost(4 * rows * 512 * 4096, 6e6),
        name="out_block",
    )(idx, u, ss, gain, out_w)


def body(
    tokens,
    gate_weight,
    input_weight,
    state_weight,
    step_weight,
    input_conv,
    state_conv,
    log_rate,
    step_bias,
    skip_gain,
    norm_gain,
    out_weight,
):
    me = lax.axis_index("tp")
    x, zl, core = me // 8, (me // 2) % 4, me % 2
    y, later = lax.axis_index("ctx") % 4, lax.axis_index("ctx") // 4
    n = jnp.arange(16, dtype=jnp.int32)
    turn = jnp.where(n == 1, 3, jnp.where(n == 2, 1, jnp.where(n == 3, 2, 0)))
    tile = n - 4
    where = jnp.bitwise_xor(tile % 4, zl) * 2 + jnp.bitwise_xor(tile // 4, core)
    idx = jnp.where(n < 4, (x + turn) % 4, where)
    idx = jnp.where(n == 12, zl, jnp.where(n == 13, core, jnp.where(n == 14, y, jnp.where(n == 15, later, idx))))
    idx = idx.astype(jnp.int32)

    state_rows_w = state_weight.T
    state_pair = flip(state_rows_w, "tp", 1)
    taps_pair = flip(state_conv, "tp", 1)
    low = core == 0
    first = jnp.where(low, state_rows_w, state_pair)
    second = jnp.where(low, state_pair, state_rows_w)
    small_w = jnp.concatenate(
        [first, second, step_weight.T, jnp.zeros((120, tokens.shape[1]), BF16)], axis=0
    )
    state_taps = jnp.concatenate(
        [jnp.where(low, state_conv, taps_pair), jnp.where(low, taps_pair, state_conv)], axis=1
    )
    par = jnp.concatenate([log_rate, step_bias, skip_gain])

    tiles = [tokens, flip(tokens, "tp", 2)]
    tiles.append(flip(tokens, "tp", 4))
    tiles.append(flip(tokens, "tp", 6))
    part1 = jnp.concatenate(tiles[:2], axis=0)
    right1 = along_x(part1, 1)
    left1 = along_x(part1, -1)
    other1 = flip(part1, "tp", 1)
    late, other1 = lax.optimization_barrier((tiles[2:], other1))
    part2 = jnp.concatenate(late, axis=0)
    right2 = along_x(part2, 1)
    left2 = along_x(part2, -1)
    other2 = flip(part2, "tp", 1)
    own_parts = [(part1, 0), (part2, 0), (other1, 0), (other2, 0)]
    last = tiles[0][8:]
    for s in (1, 2, 3):
        last = jnp.where(zl == 3 - s, tiles[s][8:], last)
    to = {
        "h0": lambda c, t: (c + 1, t) if c < 7 and t >= 24 and t % 2 else None,
        "hc": lambda c, t: (c, t - 1) if t >= 24 and t % 2 else None,
        "h1": lambda c, t: (c, t - 24) if t >= 24 else None,
        "h2": lambda c, t: (c, t - 8) if t >= 24 else ((c, t + 8) if t < 8 else None),
    }
    rim = hop(last, to["h0"])
    far_a = along_x(right1, 1)
    side1 = flip(jnp.concatenate([right1, left1], axis=0), "tp", 1)
    rim = rim + hop(rim, to["hc"])
    rim = rim + hop(rim, to["h1"])
    far_b = along_x(left2, -1)
    side2 = flip(jnp.concatenate([right2, left2], axis=0), "tp", 1)
    rim = rim + hop(rim, to["h2"])
    rights = [(right1, 0), (right2, 0), (side1, 0), (side2, 0)]
    lefts = [(left1, 0), (left2, 0), (side1, 1), (side2, 1)]
    bufs = project_resident(
        own_parts + rights + lefts, None, [0, 1, 2], idx, input_weight, small_w, None
    )
    rim = jnp.concatenate([jnp.zeros_like(rim), rim], axis=0)
    far_a_other = flip(far_a, "tp", 1)
    far_b_other = flip(far_b, "tp", 1)
    fars = [(far_a, 0), (far_b, 0), (far_a_other, 0), (far_b_other, 0)]
    input_rows, state_rows, step_raw, halo = project_resident(
        fars, rim, [3], idx, input_weight, small_w, bufs
    )

    piece = conv_states(idx, state_rows, halo, state_taps)
    pieces = jnp.stack([piece] + [flip(piece, "tp", 2 * s) for s in (1, 2, 3)])
    pieces_other = flip(pieces, "tp", 1)

    xs, x_hi, x_lo, dt, cum = inputs_stage(input_rows, halo, input_conv, step_raw, par)
    payload = state_stage(idx, pieces, pieces_other, x_hi, x_lo, cum)
    ends = [payload[0]] + [half_flip(payload[s], s) for s in (1, 2, 3)]
    y_local, read_vec = scan_stage(idx, pieces, pieces_other, xs, dt, cum, par)
    inc, pre, total = prefix_stage(idx, *ends)
    before = half_flip(total, 4)
    everything = own_parts + rights + lefts + fars
    gate = gate_of(everything, [0, 1, 2, 3], idx, gate_weight)
    spread = spread_stage(idx, inc, pre, before)
    quarters = [spread[0]] + [half_flip(spread[s], s) for s in (1, 2, 3)]
    u, squares = gate_stage(idx, y_local, read_vec, quarters, cum, gate)

    squares = squares + flip(squares, "tp", 1)
    squares = squares + flip(squares, "tp", 2)
    squares = squares + flip(squares, "tp", 4)

    gain = norm_gain.reshape(1, 512)
    out_w = load(out_weight)
    far_own, far_oth = out_block(idx, [3], u, squares, gain, out_w)
    far_sum = far_own + flip(far_oth, "tp", 1).astype(F32)
    got_a = along_x(narrow(far_sum[:32]), 1)
    got_b = along_x(narrow(far_sum[32:]), -1)
    rest_own, rest_oth = out_block(idx, [2, 1, 0], u, squares, gain, out_w)
    rest_got = flip(rest_oth, "tp", 1)
    half = out_w.shape[1] // 2
    outs = []
    moved = []
    for n in range(2):
        cols = slice(n * half, n * half + half)

        def rest_sum(rows):
            return rest_own[rows, cols] + rest_got[rows, cols].astype(F32)

        to_right = narrow(rest_sum(slice(0, 64)) + jnp.pad(widen(got_a[:, cols]), ((0, 32), (0, 0))))
        to_left = narrow(rest_sum(slice(64, 128)) + jnp.pad(widen(got_b[:, cols]), ((32, 0), (0, 0))))
        from_left = along_x(to_right, 1)
        from_right = along_x(to_left, -1)
        moved.append((rest_sum(slice(128, 192)), from_left, from_right))
    for n in range(2):
        own, from_left, from_right = moved[n]

        def tile_sum(place):
            at = place * 16
            return (
                lax.dynamic_slice_in_dim(own, at, 16, 0)
                + widen(lax.dynamic_slice_in_dim(from_left, at, 16, 0))
                + widen(lax.dynamic_slice_in_dim(from_right, at, 16, 0))
            )

        out = tile_sum(zl)
        for p in (1, 2, 3):
            part = narrow(tile_sum(jnp.bitwise_xor(zl, p)))
            part = flip(part, "tp", 2 * p)
            out = out + widen(part)
        outs.append(out.astype(BF16))
    return jnp.concatenate(outs, axis=1)


def half_flip(value, mask):
    return flip(value.astype(F16), "ctx", mask).astype(F32)


def narrow(value):
    return (value * 32.0).astype(F16)


def widen(value):
    return value.astype(F32) * 0.03125


def solution(mesh):
    placed = (
        P(("ctx", "tp"), None),
        P(None, "tp"),
        P(None, "tp"),
        P(None, "tp"),
        P(None, "tp"),
        P(None, "tp"),
        P(None, "tp"),
        P("tp"),
        P("tp"),
        P("tp"),
        P("tp"),
        P("tp", None),
    )

    return jax.shard_map(
        body, mesh=mesh, in_specs=placed, out_specs=P(("ctx", "tp"), None), check_vma=False
    )
```
